32 devices in a mesh: rep: 4 (over z), fsdp: 8 (over y, x, core).
Axes of the slice: x: 2, y: 2, z: 4, core: 2. Of those that a mesh axis runs over, the one named last changes fastest.
Arguments:
- tokens: bfloat16 [4, 2048, 1024], P('rep', 'fsdp'), may hold values from -6 to 6
- segment_ids: int32 [4, 2048], P('rep'), may hold values from 0 to 7, never falling along the last dimension, each value on 1 to 1280 neighbouring positions
- qkv_weight: bfloat16 [1024, 3072], P('fsdp'), may hold values from -0.1875 to 0.1875
- out_weight: bfloat16 [1024, 1024], P('fsdp'), may hold values from -1.5 to 1.5
- up_weight: bfloat16 [1024, 4096], P('fsdp'), may hold values from -0.1875 to 0.1875
- down_weight: bfloat16 [4096, 1024], P('fsdp'), may hold values from -0.09375 to 0.09375
- proj_bias: float32 [4, 1024], replicated, may hold values from -1.2 to 1.2
- hidden_bias: float32 [4096], replicated, may hold values from -1.2 to 1.2
- norm_gain: float32 [2, 1024], replicated, may hold values from 0.5 to 1.5
- norm_shift: float32 [2, 1024], replicated, may hold values from -1.2 to 1.2
- cotangent: bfloat16 [4, 2048, 1024], P('rep', 'fsdp'), may hold values from -6 to 6
Outputs:
- output: bfloat16 [4, 2048, 1024], P('rep', 'fsdp')
- input_grad: bfloat16 [4, 2048, 1024], P('rep', 'fsdp')
- qkv_grad: float32 [1024, 3072], P('fsdp')
- out_grad: float32 [1024, 1024], P('fsdp')
- up_grad: float32 [1024, 4096], P('fsdp')
- down_grad: float32 [4096, 1024], P('fsdp')
- proj_bias_grad: float32 [4, 1024], replicated
- hidden_bias_grad: float32 [4096], replicated
- gain_grad: float32 [2, 1024], replicated
- shift_grad: float32 [2, 1024], replicated
The draws below stay inside these ranges and needn't reach their ends.
Inputs may be any that keep to these rules, and one draw needn't show every extreme that they name: `segment_ids`: in each sequence documents are numbered 0 to 7 in order, each 1 to 1280 tokens long, one exactly 1280.
All inputs are finite; a program needn't handle non-finite values.
Results may differ from the reference program's by a relative error of at most 0.018.
Values may be sent and summed in bfloat16 or wider, within the bound.
A program may use at most 192 MiB of HBM per device.

```python
import math
import jax
import jax.numpy as jnp
import numpy as np
from jax import lax

D = 1024
HEADS = 16
FF = 4096
SEQ = 2048
SEQS = 4
DOCS = 8
LONGEST = 1280


def levels(rng, shape, shards, smallest, largest):
    def one(dim, parts):
        draws = jax.random.uniform(jax.random.fold_in(jax.random.fold_in(rng, 6), dim), (parts,), jnp.float32, smallest / len(shards), largest / len(shards))
        return jnp.repeat(jnp.exp(draws), shape[dim] // parts).reshape((-1,) + (1,) * (len(shape) - dim - 1))

    loudness = one(*shards[0])
    for cut in shards[1:]:
        loudness = loudness * one(*cut)
    return loudness


def split_up(amount, total, reach, slope):
    weights = [(1 << 20) // math.isqrt(rank ** slope) + 1 for rank in range(2, amount + 1)]
    rest, counts = total - reach - (amount - 1), [1] * (amount - 1)
    while rest > 0:
        candidates = [i for i in range(amount - 1) if counts[i] < reach]
        whole, budget = sum([weights[i] for i in candidates]), rest
        for i in candidates:
            addition = min(reach - counts[i], max(1, budget * weights[i] // whole), rest)
            counts[i] = counts[i] + addition
            rest = rest - addition
    return np.array([reach] + counts)


def ragged_sizes(key, count, total, most, lean):
    if count == 2:
        one = jax.random.randint(key, (), max(1, total - most), min(most, total - 1) + 1)
        return jnp.stack([one, total - one])
    lengths = jnp.asarray(split_up(count, total, most, lean), jnp.int32)
    pairs = (count - 1) // 2
    source_of, sink = lengths[1:1 + 2 * pairs:2], lengths[2:2 + 2 * pairs:2]
    room = jnp.minimum(source_of - 1, most - sink)
    passed = jax.random.randint(jax.random.fold_in(key, 1), (pairs,), 0, 1 << 20) % (room + 1)
    lengths = lengths.at[1:1 + 2 * pairs:2].set(source_of - passed).at[2:2 + 2 * pairs:2].set(sink + passed)
    return lengths[jax.random.permutation(jax.random.fold_in(key, 2), count)]


def noise(stream_key, extent, width, limit, split=(), kind=jnp.bfloat16):
    entries = jax.random.normal(stream_key, extent, jnp.float32) * width
    if len(split) > 0:
        entries = levels(stream_key, extent, split, -0.22, 0.18) * entries
    return jnp.clip(entries, min=-limit, max=limit).astype(kind)


def setup_inputs(seed: int = 0) -> dict:
    seeds = jax.random.split(jax.random.key(seed), 12)
    tokens = noise(seeds[0], (SEQS, SEQ, D), 1.0, 6.0, ((0, 4), (1, 8)))
    segment_ids = jax.vmap(lambda own: jnp.searchsorted(jnp.cumsum(ragged_sizes(own, DOCS, SEQ, LONGEST, 2)), jnp.arange(SEQ), side="right"))(jax.random.split(seeds[1], SEQS)).reshape((SEQS, SEQ)).astype(jnp.int32)
    qkv_weight = noise(seeds[2], (D, 3 * D), D ** -0.5, 0.1875, ((0, 8),))
    out_weight = noise(seeds[3], (D, D), (D // 64) ** -0.5, 1.5, ((0, 8),))
    up_weight = noise(seeds[4], (D, FF), D ** -0.5, 0.1875, ((0, 8),))
    down_weight = noise(seeds[5], (FF, D), FF ** -0.5, 0.09375, ((0, 8),))
    proj_bias = noise(seeds[6], (4, D), 0.2, 1.2, (), jnp.float32)
    hidden_bias = noise(seeds[7], (FF,), 0.2, 1.2, (), jnp.float32)
    norm_gain = jnp.clip(1.0 + 0.1 * jax.random.normal(seeds[8], (2, D), jnp.float32), 0.5, 1.5)
    norm_shift = noise(seeds[9], (2, D), 0.2, 1.2, (), jnp.float32)
    cotangent = noise(seeds[10], (SEQS, SEQ, D), 1.0, 6.0, ((0, 4), (1, 8)))
    return dict(tokens=tokens, segment_ids=segment_ids, qkv_weight=qkv_weight, out_weight=out_weight, up_weight=up_weight, down_weight=down_weight, proj_bias=proj_bias, hidden_bias=hidden_bias, norm_gain=norm_gain, norm_shift=norm_shift, cotangent=cotangent)


@jax.custom_vjp
def low(v):
    return lax.optimization_barrier(v.astype(jnp.bfloat16)).astype(jnp.float32)

@jax.custom_vjp
def low_back(v):
    return v

def low_keep(v):
    return (low(v), None)

def low_pass(kept, grad):
    return (grad,)

def back_keep(v):
    return (v, None)

def back_low(kept, grad):
    return (low(grad),)
low.defvjp(low_keep, low_pass)
low_back.defvjp(back_keep, back_low)

def layer_norm(hidden, gain, shift):
    center = hidden - lax.optimization_barrier(jnp.mean(hidden, axis=-1, keepdims=True))
    spread = lax.optimization_barrier(jnp.mean(center * center, axis=-1, keepdims=True))
    return center * lax.rsqrt(spread + 1e-05) * gain + shift

def matmul(left, right):
    return jnp.dot(left, right, precision=lax.Precision.HIGHEST, preferred_element_type=jnp.float32)

def encoder_layer(parameters, inputs, segments):
    qkv_weight, out_weight, up_weight, down_weight, proj_bias, hidden_bias, norm_gain, norm_shift = parameters
    length, model_width = inputs.shape
    head_dim = model_width // HEADS
    score_scale = head_dim ** (-0.5)
    projected = matmul(inputs, qkv_weight)
    queries = low(low_back(projected[:, :model_width] + proj_bias[0]))
    key_rows = low(low_back(projected[:, model_width:2 * model_width]))
    value_rows = low(low_back(projected[:, 2 * model_width:] + proj_bias[1]))
    query_heads = queries.reshape(length, HEADS, head_dim)
    key_heads = key_rows.reshape(length, HEADS, head_dim)
    value_heads = value_rows.reshape(length, HEADS, head_dim)
    block_rows = math.gcd(length, 512)

    def attend(pair):
        query_block, doc_block = pair
        scores = jnp.einsum('qhd,khd->hqk', query_block, key_heads, precision=lax.Precision.HIGHEST) * score_scale
        scores = low_back(scores)
        same_doc = (doc_block[:, None] == segments[None, :])[None]
        row_top = lax.optimization_barrier(jnp.max(jnp.where(same_doc, scores, -1e+30), axis=2, keepdims=True))
        weights = jnp.where(same_doc, jnp.exp(scores - row_top), 0.0)
        probabilities = low(weights / lax.optimization_barrier(jnp.sum(weights, axis=2, keepdims=True)))
        return jnp.einsum('hqk,khd->qhd', probabilities, value_heads, precision=lax.Precision.HIGHEST)
    mapped = lax.map(jax.checkpoint(attend), (query_heads.reshape(length // block_rows, block_rows, HEADS, head_dim), segments.reshape(length // block_rows, block_rows)))
    attended = low(low_back(mapped.reshape(length, model_width)))
    branch = low_back(matmul(attended, out_weight) + proj_bias[2])
    first_norm = layer_norm(inputs + branch, norm_gain[0], norm_shift[0])
    hidden_pre = low_back(matmul(low(first_norm), up_weight) + hidden_bias)
    activated = low(jax.nn.gelu(hidden_pre, approximate=False))
    second = low_back(matmul(activated, down_weight) + proj_bias[3])
    return layer_norm(first_norm + second, norm_gain[1], norm_shift[1])

def reference(tokens, segment_ids, qkv_weight, out_weight, up_weight, down_weight, proj_bias, hidden_bias, norm_gain, norm_shift, cotangent):
    parameters = (qkv_weight.astype(jnp.float32), out_weight.astype(jnp.float32), up_weight.astype(jnp.float32), down_weight.astype(jnp.float32), proj_bias.astype(jnp.float32), hidden_bias.astype(jnp.float32), norm_gain.astype(jnp.float32), norm_shift.astype(jnp.float32))
    inputs = tokens.astype(jnp.float32)
    outgrad = cotangent.astype(jnp.float32)

    def forward(params_in, inputs_in):

        def one_sequence(pair):
            return encoder_layer(params_in, pair[0], pair[1])
        return lax.map(one_sequence, (inputs_in, segment_ids))
    output, pullback = jax.vjp(forward, parameters, inputs)
    gradients, input_grad = pullback(outgrad)
    grad_scale = (SEQS * SEQ) ** (-0.5)
    return (output.astype(jnp.bfloat16), input_grad.astype(jnp.bfloat16), gradients[0] * grad_scale, gradients[1] * grad_scale, gradients[2] * grad_scale, gradients[3] * grad_scale, gradients[4] * grad_scale, gradients[5] * grad_scale, gradients[6] * grad_scale, gradients[7] * grad_scale)
```

```python
import functools
import math

import jax
import jax.numpy as jnp
from jax import lax
from jax.experimental import pallas as pl
from jax.experimental.pallas import tpu as pltpu
from jax.sharding import PartitionSpec as P

HEADS = 16

NEGATIVE = -1e30
BQ = 256
VM = pl.BlockSpec(memory_space=pltpu.VMEM)
SM = pl.BlockSpec(memory_space=pltpu.SMEM)


def nt(a, b):
    return lax.dot_general(a, b, (((1,), (1,)), ((), ())), preferred_element_type=jnp.float32)


def nn(a, b):
    return jnp.dot(a, b, preferred_element_type=jnp.float32)


def block_range(seg_s, blk, i, n):
    first = seg_s[0, i * blk]
    last = seg_s[0, i * blk + blk - 1]
    lo = jnp.int32(0)
    hi = jnp.int32(0)
    for j in range(n):
        lo = lo + (seg_s[0, j * blk + blk - 1] < first).astype(jnp.int32)
        hi = hi + (seg_s[0, j * blk] <= last).astype(jnp.int32)
    return lo, hi


def head_lanes(shape, half):
    return lax.broadcasted_iota(jnp.int32, shape, 1) < half


def attn_fwd_body(scale, seg_s, seg_v, q_ref, k_ref, v_ref, o_ref, a_ref, lse_ref):
    length, width = q_ref.shape
    half = width // 2
    n = length // BQ
    first = head_lanes((BQ, width), half)

    @pl.loop(0, n)
    def _(i):
        lo, hi = block_range(seg_s, BQ, i, n)
        rows = pl.ds(pl.multiple_of(i * BQ, BQ), BQ)
        q = q_ref[rows, :] * jnp.bfloat16(scale)
        zero = jnp.zeros_like(q)
        qs = (jnp.where(first, q, zero), jnp.where(first, zero, q))
        seg_row = seg_v[:, rows].astype(jnp.float32)
        seg_col = jnp.transpose(jnp.broadcast_to(seg_row, (128, BQ)))
        seg_col = jnp.concatenate([seg_col] * (BQ // 128), axis=1)

        def step(j, state):
            cols = pl.ds(pl.multiple_of(j * BQ, BQ), BQ)
            kb = k_ref[cols, :]
            vb = v_ref[cols, :]
            same = seg_col == seg_v[:, cols].astype(jnp.float32)
            out = []
            for h in range(2):
                m, l, acc = state[h]
                s = jnp.where(same, nt(qs[h], kb), NEGATIVE)
                top = jnp.maximum(m, jnp.max(s, axis=1, keepdims=True))
                p = jnp.exp(s - top)
                factor = jnp.exp(m - top)
                l = l * factor + jnp.sum(p, axis=1, keepdims=True)
                acc = acc * factor + nn(p.astype(jnp.bfloat16), vb)
                out.append((top, l, acc))
            return tuple(out)

        one = (jnp.full((BQ, 1), NEGATIVE, jnp.float32), jnp.zeros((BQ, 1), jnp.float32), jnp.zeros((BQ, width), jnp.float32))
        (m0, l0, acc0), (m1, l1, acc1) = lax.fori_loop(lo, hi, step, (one, one))
        o = jnp.where(first, acc0 / l0, acc1 / l1)
        o_ref[rows, :] = o
        a_ref[rows, :] = o.astype(jnp.bfloat16)
        lse_ref[0:1, rows] = jnp.transpose(jnp.broadcast_to(m0 + jnp.log(l0), (BQ, 128)))[0:1, :]
        lse_ref[1:2, rows] = jnp.transpose(jnp.broadcast_to(m1 + jnp.log(l1), (BQ, 128)))[0:1, :]


def attn_fwd(scale, seg, q, k, v):
    length, width = q.shape
    return pl.pallas_call(
        functools.partial(attn_fwd_body, scale),
        name="attn_fwd",
        out_shape=(
            jax.ShapeDtypeStruct((length, width), jnp.float32),
            jax.ShapeDtypeStruct((length, width), jnp.bfloat16),
            jax.ShapeDtypeStruct((8, length), jnp.float32),
        ),
        in_specs=[SM, VM, VM, VM, VM],
        out_specs=(VM, VM, VM),
        compiler_params=pltpu.CompilerParams(vmem_limit_bytes=32 << 20),
        cost_estimate=pl.CostEstimate(flops=4 * length * length * width, bytes_accessed=6 * length * width, transcendentals=2 * length * length),
    )(seg, seg, q, k, v)


def attn_bwd_body(scale, seg_s, seg_v, q_ref, k_ref, v_ref, g_ref, o_ref, lse_ref, dq_ref, dk_ref, dv_ref, corr, dqt, dk_acc, dv_acc):
    length, width = q_ref.shape
    half = width // 2
    n = length // BQ
    first = head_lanes((BQ, width), half)

    @pl.loop(0, n)
    def _(i):
        rows = pl.ds(pl.multiple_of(i * BQ, BQ), BQ)
        prod = jnp.transpose(g_ref[rows, :].astype(jnp.float32) * o_ref[rows, :])
        corr[0:1, rows] = jnp.sum(prod[:half], axis=0, keepdims=True)
        corr[1:2, rows] = jnp.sum(prod[half:], axis=0, keepdims=True)
        dqt[:, rows] = jnp.zeros((width, BQ), jnp.float32)

    @pl.loop(0, n)
    def _(j):
        lo, hi = block_range(seg_s, BQ, j, n)
        rows = pl.ds(pl.multiple_of(j * BQ, BQ), BQ)
        kb = k_ref[rows, :]
        vb = v_ref[rows, :]
        zero = jnp.zeros_like(kb)
        ks = (jnp.where(first, kb, zero), jnp.where(first, zero, kb))
        vs = (jnp.where(first, vb, zero), jnp.where(first, zero, vb))
        kt = jnp.transpose(kb)
        seg_row = seg_v[:, rows].astype(jnp.float32)
        seg_col = jnp.transpose(jnp.broadcast_to(seg_row, (128, BQ)))
        seg_col = jnp.concatenate([seg_col] * (BQ // 128), axis=1)
        dk_acc[...] = jnp.zeros_like(dk_acc)
        dv_acc[...] = jnp.zeros_like(dv_acc)

        def step(i, _):
            cols = pl.ds(pl.multiple_of(i * BQ, BQ), BQ)
            qb = q_ref[cols, :] * jnp.bfloat16(scale)
            gb = g_ref[cols, :]
            same = seg_col == seg_v[:, cols].astype(jnp.float32)
            ps, ds = [], []
            for h in range(2):
                s = jnp.where(same, nt(ks[h], qb), NEGATIVE)
                p = jnp.exp(s - lse_ref[h : h + 1, cols])
                dp = nt(vs[h], gb)
                d = (p * (dp - corr[h : h + 1, cols])).astype(jnp.bfloat16)
                ps.append(p.astype(jnp.bfloat16))
                ds.append(d)
                dqt[h * half : (h + 1) * half, cols] += nn(kt[h * half : (h + 1) * half, :], d)
            gz = jnp.concatenate([jnp.where(first, gb, zero), jnp.where(first, zero, gb)], axis=0)
            qz = jnp.concatenate([jnp.where(first, qb, zero), jnp.where(first, zero, qb)], axis=0)
            dv_acc[...] += nn(jnp.concatenate(ps, axis=1), gz)
            dk_acc[...] += nn(jnp.concatenate(ds, axis=1), qz)
            return 0

        lax.fori_loop(lo, hi, step, 0)
        dk_ref[rows, :] = dk_acc[...].astype(jnp.bfloat16)
        dv_ref[rows, :] = dv_acc[...].astype(jnp.bfloat16)

    @pl.loop(0, n)
    def _(i):
        rows = pl.ds(pl.multiple_of(i * BQ, BQ), BQ)
        dq_ref[rows, :] = (jnp.transpose(dqt[:, rows]) * scale).astype(jnp.bfloat16)


def attn_bwd(scale, seg, q, k, v, g, o, lse):
    length, width = q.shape
    return pl.pallas_call(
        functools.partial(attn_bwd_body, scale),
        name="attn_bwd",
        out_shape=tuple(jax.ShapeDtypeStruct((length, width), jnp.bfloat16) for _ in range(3)),
        in_specs=[SM, VM, VM, VM, VM, VM, VM, VM],
        out_specs=(VM, VM, VM),
        scratch_shapes=[
            pltpu.VMEM((8, length), jnp.float32),
            pltpu.VMEM((width, length), jnp.float32),
            pltpu.VMEM((BQ, width), jnp.float32),
            pltpu.VMEM((BQ, width), jnp.float32),
        ],
        compiler_params=pltpu.CompilerParams(vmem_limit_bytes=32 << 20),
        cost_estimate=pl.CostEstimate(flops=10 * length * length * width, bytes_accessed=14 * length * width, transcendentals=2 * length * length),
    )(seg, seg, q, k, v, g, o, lse)


def normalize(hidden, gain, shift):
    center = hidden - jnp.mean(hidden, axis=-1, keepdims=True)
    spread = jnp.mean(center * center, axis=-1, keepdims=True)
    return center * lax.rsqrt(spread + 1e-05) * gain + shift


def exact_gelu(value):
    return jax.nn.gelu(value, approximate=False)


def gather_attention(qkv_weight, out_weight):
    return (
        lax.all_gather(qkv_weight, "fsdp", axis=0, tiled=True),
        lax.all_gather(out_weight, "fsdp", axis=0, tiled=True),
    )


def gather_feedforward(up_weight, down_weight):
    return (
        lax.all_gather(up_weight, "fsdp", axis=0, tiled=True),
        lax.all_gather(down_weight, "fsdp", axis=0, tiled=True),
    )


def block_plan(row_count):
    block_rows = math.gcd(row_count, 1024)
    return (block_rows, row_count // block_rows)


def split_heads(matrix):
    return matrix.reshape(matrix.shape[0], HEADS, matrix.shape[1] // HEADS)


def join_heads(stacked):
    return jnp.transpose(stacked, (1, 0, 2)).reshape(
        stacked.shape[1], stacked.shape[0] * stacked.shape[2]
    )


def local_gather(
    tokens,
    segment_ids,
    qkv_weight,
    out_weight,
    up_weight,
    down_weight,
    proj_bias,
    hidden_bias,
    norm_gain,
    norm_shift,
    cotangent,
):
    inputs = tokens[0]
    tok_count, model_width = inputs.shape
    head_dim = model_width // HEADS
    score_scale = head_dim ** (-0.5)
    doc_ids = segment_ids[0]
    own_index = lax.axis_index("fsdp")
    own_docs = lax.dynamic_slice_in_dim(doc_ids, own_index * tok_count, tok_count)
    qkv_full, out_full = gather_attention(qkv_weight, out_weight)
    projected = jnp.dot(inputs, qkv_full, preferred_element_type=jnp.float32)
    queries = (projected[:, :model_width] + proj_bias[0]).astype(jnp.bfloat16)
    key_rows = projected[:, model_width : 2 * model_width].astype(jnp.bfloat16)
    value_rows = (projected[:, 2 * model_width :] + proj_bias[1]).astype(jnp.bfloat16)
    query_heads = split_heads(queries)
    key_own = split_heads(key_rows)
    value_own = split_heads(value_rows)
    initial = (
        jnp.zeros((HEADS, tok_count, head_dim), jnp.float32),
        jnp.full((HEADS, tok_count), NEGATIVE, jnp.float32),
        jnp.zeros((HEADS, tok_count), jnp.float32),
    )
    key_piece = lax.all_gather(key_rows, "fsdp", axis=0, tiled=True)
    value_piece = lax.all_gather(value_rows, "fsdp", axis=0, tiled=True)
    block_rows, blocks = block_plan(key_piece.shape[0])

    def forward_advance(block_index, running_state):
        weighted, running, denominator = running_state
        offset = block_index * block_rows
        key_block = split_heads(lax.dynamic_slice_in_dim(key_piece, offset, block_rows))
        value_block = split_heads(lax.dynamic_slice_in_dim(value_piece, offset, block_rows))
        block_docs = lax.dynamic_slice_in_dim(doc_ids, offset, block_rows)
        scores = (
            jnp.einsum("qhd,khd->hqk", query_heads, key_block, preferred_element_type=jnp.float32)
            * score_scale
        )
        same_doc = (own_docs[:, None] == block_docs[None, :])[None]
        highest = jnp.maximum(running, jnp.max(jnp.where(same_doc, scores, NEGATIVE), axis=2))
        factor = jnp.exp(running - highest)
        weights = jnp.where(same_doc, jnp.exp(scores - highest[:, :, None]), 0.0)
        denominator = denominator * factor + jnp.sum(weights, axis=2)
        weighted = weighted * factor[:, :, None] + jnp.einsum(
            "hqk,khd->hqd",
            weights.astype(jnp.bfloat16),
            value_block,
            preferred_element_type=jnp.float32,
        )
        return (weighted, highest, denominator)

    weighted, running, denominator = lax.fori_loop(0, blocks, forward_advance, initial)
    attended_heads = weighted / denominator[:, :, None]
    log_total = running + jnp.log(denominator)
    attended_low = join_heads(attended_heads).astype(jnp.bfloat16)
    branch = jnp.dot(attended_low, out_full, preferred_element_type=jnp.float32) + proj_bias[2]
    first_norm, norm_one_back = jax.vjp(
        normalize, inputs.astype(jnp.float32) + branch, norm_gain[0], norm_shift[0]
    )
    first_low = first_norm.astype(jnp.bfloat16)
    up_full, down_full = gather_feedforward(up_weight, down_weight)
    hidden_pre = jnp.dot(first_low, up_full, preferred_element_type=jnp.float32) + hidden_bias
    activated, gelu_back = jax.vjp(exact_gelu, hidden_pre)
    activated_low = activated.astype(jnp.bfloat16)
    second = jnp.dot(activated_low, down_full, preferred_element_type=jnp.float32) + proj_bias[3]
    output, norm_two_back = jax.vjp(normalize, first_norm + second, norm_gain[1], norm_shift[1])
    up_back, down_back = gather_feedforward(up_weight, down_weight)
    qkv_back, out_back = gather_attention(qkv_weight, out_weight)
    grad_second, gain_two, shift_two = norm_two_back(cotangent[0].astype(jnp.float32))
    second_low = grad_second.astype(jnp.bfloat16)
    down_term = jnp.einsum(
        "tf,td->fd", activated_low, second_low, preferred_element_type=jnp.float32
    )
    activated_grad = jnp.einsum(
        "td,fd->tf", second_low, down_back, preferred_element_type=jnp.float32
    )
    (pre_grad,) = gelu_back(activated_grad)
    pre_low = pre_grad.astype(jnp.bfloat16)
    up_term = jnp.einsum("td,tf->df", first_low, pre_low, preferred_element_type=jnp.float32)
    first_grad = grad_second + jnp.einsum(
        "tf,df->td", pre_low, up_back, preferred_element_type=jnp.float32
    )
    branch_grad, gain_one, shift_one = norm_one_back(first_grad)
    branch_low = branch_grad.astype(jnp.bfloat16)
    out_term = jnp.einsum("te,td->ed", attended_low, branch_low, preferred_element_type=jnp.float32)
    attended_grad = jnp.einsum(
        "td,ed->te", branch_low, out_back, preferred_element_type=jnp.float32
    ).astype(jnp.bfloat16)
    grad_heads = split_heads(attended_grad)
    correction = jnp.einsum("qhd,hqd->hq", grad_heads.astype(jnp.float32), attended_heads)
    lse_all, correction_all = (
        lax.all_gather(log_total, "fsdp", axis=1, tiled=True),
        lax.all_gather(correction, "fsdp", axis=1, tiled=True),
    )
    query_key_piece = lax.all_gather(key_rows, "fsdp", axis=0, tiled=True)
    query_value_piece = lax.all_gather(value_rows, "fsdp", axis=0, tiled=True)
    query_block_rows, blocks = block_plan(query_key_piece.shape[0])

    def query_advance(block_index, query_state):
        offset = block_index * query_block_rows
        key_block = split_heads(lax.dynamic_slice_in_dim(query_key_piece, offset, query_block_rows))
        value_block = split_heads(
            lax.dynamic_slice_in_dim(query_value_piece, offset, query_block_rows)
        )
        block_docs = lax.dynamic_slice_in_dim(doc_ids, offset, query_block_rows)
        scores = (
            jnp.einsum("qhd,khd->hqk", query_heads, key_block, preferred_element_type=jnp.float32)
            * score_scale
        )
        same_doc = (own_docs[:, None] == block_docs[None, :])[None]
        probabilities = jnp.where(same_doc, jnp.exp(scores - log_total[:, :, None]), 0.0)
        prob_grad = jnp.einsum(
            "qhd,khd->hqk", grad_heads, value_block, preferred_element_type=jnp.float32
        )
        score_grad = (probabilities * (prob_grad - correction[:, :, None])).astype(jnp.bfloat16)
        return query_state + jnp.einsum(
            "hqk,khd->hqd", score_grad, key_block, preferred_element_type=jnp.float32
        )

    query_acc = lax.fori_loop(
        0, blocks, query_advance, jnp.zeros((HEADS, tok_count, head_dim), jnp.float32)
    )
    query_grad = (join_heads(query_acc) * score_scale).astype(jnp.bfloat16)
    empty_heads = jnp.zeros((HEADS, tok_count, head_dim), jnp.float32)
    query_piece = lax.all_gather(queries, "fsdp", axis=0, tiled=True)
    grad_piece = lax.all_gather(attended_grad, "fsdp", axis=0, tiled=True)
    key_block_rows, blocks = block_plan(query_piece.shape[0])

    def key_advance(block_index, key_state):
        key_acc, value_acc = key_state
        offset = block_index * key_block_rows
        query_block = split_heads(lax.dynamic_slice_in_dim(query_piece, offset, key_block_rows))
        grad_block = split_heads(lax.dynamic_slice_in_dim(grad_piece, offset, key_block_rows))
        block_docs = lax.dynamic_slice_in_dim(doc_ids, offset, key_block_rows)
        lse_block = lax.dynamic_slice_in_dim(lse_all, offset, key_block_rows, axis=1)
        corr_block = lax.dynamic_slice_in_dim(correction_all, offset, key_block_rows, axis=1)
        scores = (
            jnp.einsum("qhd,khd->hqk", query_block, key_own, preferred_element_type=jnp.float32)
            * score_scale
        )
        same_doc = (block_docs[:, None] == own_docs[None, :])[None]
        probabilities = jnp.where(same_doc, jnp.exp(scores - lse_block[:, :, None]), 0.0)
        value_acc = value_acc + jnp.einsum(
            "hqk,qhd->hkd",
            probabilities.astype(jnp.bfloat16),
            grad_block,
            preferred_element_type=jnp.float32,
        )
        prob_grad = jnp.einsum(
            "qhd,khd->hqk", grad_block, value_own, preferred_element_type=jnp.float32
        )
        score_grad = (probabilities * (prob_grad - corr_block[:, :, None])).astype(jnp.bfloat16)
        key_acc = key_acc + jnp.einsum(
            "hqk,qhd->hkd", score_grad, query_block, preferred_element_type=jnp.float32
        )
        return (key_acc, value_acc)

    key_acc, value_acc = lax.fori_loop(0, blocks, key_advance, (empty_heads, empty_heads))
    key_grad = (join_heads(key_acc) * score_scale).astype(jnp.bfloat16)
    value_grad = join_heads(value_acc).astype(jnp.bfloat16)
    qkv_grad_low = jnp.concatenate([query_grad, key_grad, value_grad], axis=1)
    qkv_term = jnp.einsum("td,te->de", inputs, qkv_grad_low, preferred_element_type=jnp.float32)
    input_grad = branch_grad + jnp.einsum(
        "te,de->td", qkv_grad_low, qkv_back, preferred_element_type=jnp.float32
    )
    bias_term = jnp.stack(
        [
            jnp.sum(query_grad.astype(jnp.float32), axis=0),
            jnp.sum(value_grad.astype(jnp.float32), axis=0),
            jnp.sum(branch_low.astype(jnp.float32), axis=0),
            jnp.sum(second_low.astype(jnp.float32), axis=0),
        ]
    )
    hidden_term = jnp.sum(pre_low.astype(jnp.float32), axis=0)
    gain_term = jnp.stack([gain_one, gain_two])
    shift_term = jnp.stack([shift_one, shift_two])
    bias_total, hidden_total, gain_total, shift_total = lax.psum(
        (bias_term, hidden_term, gain_term, shift_term), ("rep", "fsdp")
    )
    up_sum, down_sum = (
        lax.psum_scatter(up_term, "fsdp", scatter_dimension=0, tiled=True),
        lax.psum_scatter(down_term, "fsdp", scatter_dimension=0, tiled=True),
    )
    qkv_sum, out_sum = (
        lax.psum_scatter(qkv_term, "fsdp", scatter_dimension=0, tiled=True),
        lax.psum_scatter(out_term, "fsdp", scatter_dimension=0, tiled=True),
    )
    qkv_total, out_total, up_total, down_total = lax.psum(
        (qkv_sum, out_sum, up_sum, down_sum), "rep"
    )
    grad_scale = (tok_count * lax.axis_size("fsdp") * lax.axis_size("rep")) ** (-0.5)
    return (
        output.astype(jnp.bfloat16)[None],
        input_grad.astype(jnp.bfloat16)[None],
        qkv_total * grad_scale,
        out_total * grad_scale,
        up_total * grad_scale,
        down_total * grad_scale,
        bias_total * grad_scale,
        hidden_total * grad_scale,
        gain_total * grad_scale,
        shift_total * grad_scale,
    )


def exchange(rows, parts):
    count, width = rows.shape
    split = jnp.transpose(rows.reshape(count, parts, width // parts), (1, 0, 2))
    return lax.all_to_all(split, "fsdp", 0, 0).reshape(parts * count, width // parts)


def exchange_back(rows, parts):
    count, width = rows.shape
    got = lax.all_to_all(rows.reshape(parts, count // parts, width), "fsdp", 0, 0)
    return jnp.transpose(got, (1, 0, 2)).reshape(count // parts, parts * width)


def local_tensor(tokens, segment_ids, qkv_weight, out_weight, up_weight, down_weight, proj_bias, hidden_bias, norm_gain, norm_shift, cotangent):
    f32, bf16 = jnp.float32, jnp.bfloat16
    inputs = tokens[0]
    tok_count, model_width = inputs.shape
    parts = lax.axis_size("fsdp")
    own = lax.axis_index("fsdp")
    head_dim = model_width // HEADS
    scale = head_dim ** (-0.5)
    width = model_width // parts
    ff = hidden_bias.shape[0] // parts

    def dot(spec, a, b):
        return jnp.einsum(spec, a, b, preferred_element_type=f32)

    def mine(vector, size):
        return lax.dynamic_slice_in_dim(vector, own * size, size)

    tokens_all = lax.all_gather(inputs, "fsdp", axis=0, tiled=True)
    weight_pieces = [exchange(qkv_weight[:, i * model_width : (i + 1) * model_width], parts) for i in range(3)]
    queries = (dot("td,de->te", tokens_all, weight_pieces[0]) + mine(proj_bias[0], width)).astype(bf16)
    key_rows = dot("td,de->te", tokens_all, weight_pieces[1]).astype(bf16)
    value_rows = (dot("td,de->te", tokens_all, weight_pieces[2]) + mine(proj_bias[1], width)).astype(bf16)
    attended, attended_low_heads, lse = attn_fwd(scale, segment_ids, queries, key_rows, value_rows)
    attended_low = exchange_back(attended_low_heads, parts)
    out_full = lax.all_gather(out_weight, "fsdp", axis=0, tiled=True)
    branch = dot("te,ed->td", attended_low, out_full) + proj_bias[2]
    first_norm, norm_one_back = jax.vjp(normalize, inputs.astype(f32) + branch, norm_gain[0], norm_shift[0])
    first_low = first_norm.astype(bf16)
    up_mine = exchange(up_weight, parts)
    first_all = lax.all_gather(first_low, "fsdp", axis=0, tiled=True)
    hidden_pre = dot("td,df->tf", first_all, up_mine) + mine(hidden_bias, ff)
    activated, gelu_back = jax.vjp(exact_gelu, hidden_pre)
    activated_low = activated.astype(bf16)
    second = lax.psum_scatter(dot("tf,fd->td", activated_low, down_weight).astype(bf16), "fsdp", scatter_dimension=0, tiled=True).astype(f32) + proj_bias[3]
    output, norm_two_back = jax.vjp(normalize, first_norm + second, norm_gain[1], norm_shift[1])
    grad_second, gain_two, shift_two = norm_two_back(cotangent[0].astype(f32))
    second_low = grad_second.astype(bf16)
    second_all = lax.all_gather(second_low, "fsdp", axis=0, tiled=True)
    (pre_grad,) = gelu_back(dot("td,fd->tf", second_all, down_weight))
    pre_low = pre_grad.astype(bf16)
    down_sum = dot("tf,td->fd", activated_low, second_all)
    first_grad = grad_second + lax.psum_scatter(dot("tf,df->td", pre_low, up_mine).astype(bf16), "fsdp", scatter_dimension=0, tiled=True).astype(f32)
    up_cols = dot("td,tf->df", first_all, pre_low)
    up_sum = exchange_back(up_cols.astype(bf16), parts)
    branch_grad, gain_one, shift_one = norm_one_back(first_grad)
    branch_low = branch_grad.astype(bf16)
    attended_grad = dot("td,ed->te", branch_low, out_full).astype(bf16)
    grad_heads = exchange(attended_grad, parts)
    out_term = dot("te,td->ed", attended_low, branch_low)
    out_sum = lax.psum_scatter(out_term.astype(bf16), "fsdp", scatter_dimension=0, tiled=True)
    up_total, down_total, out_total = lax.psum((up_sum, down_sum.astype(bf16), out_sum), "rep")
    query_grad, key_grad, value_grad = attn_bwd(scale, segment_ids, queries, key_rows, value_rows, grad_heads, attended, lse)
    partial_input = dot("te,de->td", query_grad, weight_pieces[0]) + dot("te,de->td", key_grad, weight_pieces[1]) + dot("te,de->td", value_grad, weight_pieces[2])
    input_grad = branch_grad + lax.psum_scatter(partial_input.astype(bf16), "fsdp", scatter_dimension=0, tiled=True).astype(f32)
    qkv_sum = jnp.concatenate([exchange_back(dot("td,te->de", tokens_all, g).astype(bf16), parts) for g in (query_grad, key_grad, value_grad)], axis=1)
    qkv_total = lax.psum(qkv_sum, "rep")

    def placed(vector):
        return lax.dynamic_update_slice_in_dim(jnp.zeros((vector.shape[0] * parts,), f32), vector, own * vector.shape[0], 0)

    bias_term = jnp.stack([
        placed(jnp.sum(query_grad.astype(f32), axis=0)),
        placed(jnp.sum(value_grad.astype(f32), axis=0)),
        jnp.sum(branch_low.astype(f32), axis=0),
        jnp.sum(second_low.astype(f32), axis=0),
    ])
    hidden_term = placed(jnp.sum(pre_low.astype(f32), axis=0))
    bias_total, hidden_total, gain_total, shift_total = lax.psum(
        (bias_term, hidden_term, jnp.stack([gain_one, gain_two]), jnp.stack([shift_one, shift_two])), ("rep", "fsdp")
    )
    grad_scale = (tok_count * parts * lax.axis_size("rep")) ** (-0.5)
    return (
        output.astype(bf16)[None],
        input_grad.astype(bf16)[None],
        qkv_total.astype(f32) * grad_scale,
        out_total.astype(f32) * grad_scale,
        up_total.astype(f32) * grad_scale,
        down_total.astype(f32) * grad_scale,
        bias_total * grad_scale,
        hidden_total * grad_scale,
        gain_total * grad_scale,
        shift_total * grad_scale,
    )


def solution(mesh):
    local = local_tensor if HEADS == 2 * mesh.shape["fsdp"] else local_gather
    return jax.shard_map(
        local,
        mesh=mesh,
        in_specs=(
            P("rep", "fsdp", None),
            P("rep", None),
            P("fsdp", None),
            P("fsdp", None),
            P("fsdp", None),
            P("fsdp", None),
            P(),
            P(),
            P(),
            P(),
            P("rep", "fsdp", None),
        ),
        out_specs=(
            P("rep", "fsdp", None),
            P("rep", "fsdp", None),
            P("fsdp", None),
            P("fsdp", None),
            P("fsdp", None),
            P("fsdp", None),
            P(),
            P(),
            P(),
            P(),
        ),
        check_vma=False,
    )
```

```python
import functools
import math

import jax
import jax.numpy as jnp
from jax import lax
from jax.experimental import pallas as pl
from jax.experimental.pallas import tpu as pltpu
from jax.sharding import PartitionSpec as P

HEADS = 16

NEGATIVE = -1e30
BQ = 256
VM = pl.BlockSpec(memory_space=pltpu.VMEM)
SM = pl.BlockSpec(memory_space=pltpu.SMEM)


def nt(a, b):
    return lax.dot_general(a, b, (((1,), (1,)), ((), ())), preferred_element_type=jnp.float32)


def nn(a, b):
    return jnp.dot(a, b, preferred_element_type=jnp.float32)


def block_range(seg_s, blk, i, n):
    first = seg_s[0, i * blk]
    last = seg_s[0, i * blk + blk - 1]
    lo = jnp.int32(0)
    hi = jnp.int32(0)
    for j in range(n):
        lo = lo + (seg_s[0, j * blk + blk - 1] < first).astype(jnp.int32)
        hi = hi + (seg_s[0, j * blk] <= last).astype(jnp.int32)
    return lo, hi


def head_lanes(shape, half):
    return lax.broadcasted_iota(jnp.int32, shape, 1) < half


def attn_fwd_body(scale, seg_s, seg_v, q_ref, k_ref, v_ref, o_ref, a_ref, lse_ref):
    length, width = q_ref.shape
    half = width // 2
    n = length // BQ
    first = head_lanes((BQ, width), half)

    @pl.loop(0, n)
    def _(i):
        lo, hi = block_range(seg_s, BQ, i, n)
        rows = pl.ds(pl.multiple_of(i * BQ, BQ), BQ)
        q = q_ref[rows, :] * jnp.bfloat16(scale)
        zero = jnp.zeros_like(q)
        qs = (jnp.where(first, q, zero), jnp.where(first, zero, q))
        seg_row = seg_v[:, rows].astype(jnp.float32)
        seg_col = jnp.transpose(jnp.broadcast_to(seg_row, (128, BQ)))
        seg_col = jnp.concatenate([seg_col] * (BQ // 128), axis=1)

        def step(j, state):
            cols = pl.ds(pl.multiple_of(j * BQ, BQ), BQ)
            kb = k_ref[cols, :]
            vb = v_ref[cols, :]
            same = seg_col == seg_v[:, cols].astype(jnp.float32)
            out = []
            for h in range(2):
                m, l, acc = state[h]
                s = jnp.where(same, nt(qs[h], kb), NEGATIVE)
                top = jnp.maximum(m, jnp.max(s, axis=1, keepdims=True))
                p = jnp.exp(s - top)
                factor = jnp.exp(m - top)
                l = l * factor + jnp.sum(p, axis=1, keepdims=True)
                acc = acc * factor + nn(p.astype(jnp.bfloat16), vb)
                out.append((top, l, acc))
            return tuple(out)

        one = (jnp.full((BQ, 1), NEGATIVE, jnp.float32), jnp.zeros((BQ, 1), jnp.float32), jnp.zeros((BQ, width), jnp.float32))
        (m0, l0, acc0), (m1, l1, acc1) = lax.fori_loop(lo, hi, step, (one, one))
        o = jnp.where(first, acc0 / l0, acc1 / l1)
        o_ref[rows, :] = o
        a_ref[rows, :] = o.astype(jnp.bfloat16)
        lse_ref[0:1, rows] = jnp.transpose(jnp.broadcast_to(m0 + jnp.log(l0), (BQ, 128)))[0:1, :]
        lse_ref[1:2, rows] = jnp.transpose(jnp.broadcast_to(m1 + jnp.log(l1), (BQ, 128)))[0:1, :]


def attn_fwd(scale, seg, q, k, v):
    length, width = q.shape
    return pl.pallas_call(
        functools.partial(attn_fwd_body, scale),
        name="attn_fwd",
        out_shape=(
            jax.ShapeDtypeStruct((length, width), jnp.float32),
            jax.ShapeDtypeStruct((length, width), jnp.bfloat16),
            jax.ShapeDtypeStruct((8, length), jnp.float32),
        ),
        in_specs=[SM, VM, VM, VM, VM],
        out_specs=(VM, VM, VM),
        compiler_params=pltpu.CompilerParams(vmem_limit_bytes=32 << 20),
        cost_estimate=pl.CostEstimate(flops=4 * length * length * width, bytes_accessed=6 * length * width, transcendentals=2 * length * length),
    )(seg, seg, q, k, v)


def attn_bwd_body(scale, seg_s, seg_v, q_ref, k_ref, v_ref, g_ref, o_ref, lse_ref, dq_ref, dk_ref, dv_ref, corr, dqt, dk_acc, dv_acc):
    length, width = q_ref.shape
    half = width // 2
    n = length // BQ
    first = head_lanes((BQ, width), half)

    @pl.loop(0, n)
    def _(i):
        rows = pl.ds(pl.multiple_of(i * BQ, BQ), BQ)
        prod = jnp.transpose(g_ref[rows, :].astype(jnp.float32) * o_ref[rows, :])
        corr[0:1, rows] = jnp.sum(prod[:half], axis=0, keepdims=True)
        corr[1:2, rows] = jnp.sum(prod[half:], axis=0, keepdims=True)
        dqt[:, rows] = jnp.zeros((width, BQ), jnp.float32)

    @pl.loop(0, n)
    def _(j):
        lo, hi = block_range(seg_s, BQ, j, n)
        rows = pl.ds(pl.multiple_of(j * BQ, BQ), BQ)
        kb = k_ref[rows, :]
        vb = v_ref[rows, :]
        zero = jnp.zeros_like(kb)
        ks = (jnp.where(first, kb, zero), jnp.where(first, zero, kb))
        vs = (jnp.where(first, vb, zero), jnp.where(first, zero, vb))
        kt = jnp.transpose(kb)
        seg_row = seg_v[:, rows].astype(jnp.float32)
        seg_col = jnp.transpose(jnp.broadcast_to(seg_row, (128, BQ)))
        seg_col = jnp.concatenate([seg_col] * (BQ // 128), axis=1)
        dk_acc[...] = jnp.zeros_like(dk_acc)
        dv_acc[...] = jnp.zeros_like(dv_acc)

        def step(i, _):
            cols = pl.ds(pl.multiple_of(i * BQ, BQ), BQ)
            qb = q_ref[cols, :] * jnp.bfloat16(scale)
            gb = g_ref[cols, :]
            same = seg_col == seg_v[:, cols].astype(jnp.float32)
            ps, ds = [], []
            for h in range(2):
                s = jnp.where(same, nt(ks[h], qb), NEGATIVE)
                p = jnp.exp(s - lse_ref[h : h + 1, cols])
                dp = nt(vs[h], gb)
                d = (p * (dp - corr[h : h + 1, cols])).astype(jnp.bfloat16)
                ps.append(p.astype(jnp.bfloat16))
                ds.append(d)
                dqt[h * half : (h + 1) * half, cols] += nn(kt[h * half : (h + 1) * half, :], d)
            gz = jnp.concatenate([jnp.where(first, gb, zero), jnp.where(first, zero, gb)], axis=0)
            qz = jnp.concatenate([jnp.where(first, qb, zero), jnp.where(first, zero, qb)], axis=0)
            dv_acc[...] += nn(jnp.concatenate(ps, axis=1), gz)
            dk_acc[...] += nn(jnp.concatenate(ds, axis=1), qz)
            return 0

        lax.fori_loop(lo, hi, step, 0)
        dk_ref[lax.rem(j, 2), j // 2] = dk_acc[...].astype(jnp.bfloat16)
        dv_ref[lax.rem(j, 2), j // 2] = dv_acc[...].astype(jnp.bfloat16)

    @pl.loop(0, n)
    def _(i):
        rows = pl.ds(pl.multiple_of(i * BQ, BQ), BQ)
        dq_ref[lax.rem(i, 2), i // 2] = (jnp.transpose(dqt[:, rows]) * scale).astype(jnp.bfloat16)


def attn_bwd(scale, seg, q, k, v, g, o, lse):
    length, width = q.shape
    return pl.pallas_call(
        functools.partial(attn_bwd_body, scale),
        name="attn_bwd",
        out_shape=tuple(jax.ShapeDtypeStruct((2, length // BQ // 2, BQ, width), jnp.bfloat16) for _ in range(3)),
        in_specs=[SM, VM, VM, VM, VM, VM, VM, VM],
        out_specs=(VM, VM, VM),
        scratch_shapes=[
            pltpu.VMEM((8, length), jnp.float32),
            pltpu.VMEM((width, length), jnp.float32),
            pltpu.VMEM((BQ, width), jnp.float32),
            pltpu.VMEM((BQ, width), jnp.float32),
        ],
        compiler_params=pltpu.CompilerParams(vmem_limit_bytes=32 << 20),
        cost_estimate=pl.CostEstimate(flops=10 * length * length * width, bytes_accessed=14 * length * width, transcendentals=2 * length * length),
    )(seg, seg, q, k, v, g, o, lse)


MESH = pl.DeviceIdType.MESH
ANY = pl.BlockSpec(memory_space=pl.ANY)
F32 = jnp.float32
BF16 = jnp.bfloat16


def tn(a, b):
    return lax.dot_general(a, b, (((0,), (0,)), ((), ())), preferred_element_type=F32)


def fold_rows(v):
    return jnp.sum(v.reshape(v.shape[0] // 8, 8, v.shape[1]), axis=0)


class Wires:
    def __init__(self, send_sems, recv_sems, local_sems):
        self.send_sems, self.recv_sems, self.local_sems = send_sems, recv_sems, local_sems
        self.count = 0
        self.local_count = 0
        self.sent = []
        self.rep = lax.axis_index("rep")
        self.own = lax.axis_index("fsdp")

    def remote(self, src, dst, peer, rep=None):
        i = self.count
        self.count = i + 1
        return pltpu.make_async_remote_copy(
            src_ref=src, dst_ref=dst, send_sem=self.send_sems.at[i], recv_sem=self.recv_sems.at[i],
            device_id=(self.rep if rep is None else rep, peer), device_id_type=MESH,
        )

    def send(self, src, dst, peer):
        copy = self.remote(src, dst, peer)
        copy.start()
        self.sent.append(copy)
        return copy

    def local(self, src, dst):
        copy = pltpu.make_async_copy(src, dst, self.local_sems.at[self.local_count])
        self.local_count += 1
        copy.start()
        return copy

    def greet(self, peers):
        barrier = pltpu.get_barrier_semaphore()
        for rep, peer in peers:
            pl.semaphore_signal(barrier, inc=1, device_id=(rep, peer), device_id_type=MESH)
        pl.semaphore_wait(barrier, len(peers))

    def finish(self):
        for copy in self.sent:
            copy.wait_send()


def rows_of(index, size):
    return pl.ds(pl.multiple_of(index * size, size), size)


class Spread:
    def __init__(self, wires, slots, half):
        self.wires, self.slots, self.half = wires, slots, half
        self.chip = wires.own // 2
        self.x, self.y = lax.bitwise_xor(wires.own, 2), lax.bitwise_xor(wires.own, 4)
        self.cx, self.cy, self.cd = (lax.bitwise_xor(self.chip, m) for m in (1, 2, 3))
        self.a, self.b = pl.ds(0, half), pl.ds(half, half)

    def piece(self, chip, part):
        return self.slots.at[chip, part]

    def put(self, chip, part, peer):
        return self.wires.send(self.piece(chip, part), self.piece(chip, part), peer)

    def first_half(self):
        self.xa = self.put(self.chip, self.a, self.x)
        self.ya = self.put(self.chip, self.a, self.y)

    def second_half(self):
        self.yb = self.put(self.chip, self.b, self.y)
        self.xb = self.put(self.chip, self.b, self.x)

    def relay(self):
        self.xa.wait_recv()
        self.da = self.put(self.cx, self.a, self.y)
        self.yb.wait_recv()
        self.db = self.put(self.cy, self.b, self.x)

    def wait_sides(self):
        self.xb.wait_recv()
        self.ya.wait_recv()

    def wait_diagonal(self):
        self.da.wait_recv()
        self.db.wait_recv()


class Gather:
    def __init__(self, wires, part, side, last, half):
        self.wires, self.part, self.side, self.last, self.half = wires, part, side, last, half
        self.chip = wires.own // 2
        self.x, self.y = lax.bitwise_xor(wires.own, 2), lax.bitwise_xor(wires.own, 4)
        self.cx, self.cy, self.cd = (lax.bitwise_xor(self.chip, m) for m in (1, 2, 3))
        self.a, self.b = pl.ds(0, half), pl.ds(half, half)

    def send_x(self):
        self.x_own = self.wires.send(self.part.at[self.cx, self.a], self.side.at[0], self.x)

    def send_y(self):
        self.y_own = self.wires.send(self.part.at[self.cy, self.b], self.side.at[1], self.y)

    def send_diagonal(self):
        self.x_far = self.wires.send(self.part.at[self.cd, self.a], self.side.at[2], self.x)
        self.y_far = self.wires.send(self.part.at[self.cd, self.b], self.side.at[3], self.y)

    def relay(self):
        step = 32

        def add(chip, start, slot):
            @pl.loop(0, self.half // step)
            def _(t):
                rows = pl.ds(pl.multiple_of(start + t * step, step), step)
                near = self.part[chip, rows, :].astype(F32) + self.side[slot, rows_of(t, step), :].astype(F32)
                self.part[chip, rows, :] = near.astype(BF16)

        self.x_far.wait_recv()
        add(self.cy, 0, 2)
        self.y_last = self.wires.send(self.part.at[self.cy, self.a], self.last.at[0], self.y)
        self.y_far.wait_recv()
        add(self.cx, self.half, 3)
        self.x_last = self.wires.send(self.part.at[self.cx, self.b], self.last.at[1], self.x)

    def wait_first(self):
        self.x_own.wait_recv()
        self.y_last.wait_recv()

    def wait_second(self):
        self.y_own.wait_recv()
        self.x_last.wait_recv()

    def total(self, which, offset, size):
        rows = pl.ds(pl.multiple_of(which * self.half + offset, size), size)
        here = pl.ds(pl.multiple_of(offset, size), size)
        return self.part[self.chip, rows, :].astype(F32) + self.side[which, here, :].astype(F32) + self.last[which, here, :].astype(F32)


def middle_body(
    heads, x, cot, up_w, out_w, down_w, got_x, got_y, got_d, proj_bias, hidden_bias, gain, shift,
    output, branch_grad, grad_heads, vec, down_grad, upout_grad,
    att, out_full, up_full, down_full, h1, z1, r1, gs, fl, act, slope, part, side, last, sl, pre, part2, side2, last2,
    branch_low, agl, acc, d_send, d_recv, d_keep, u_send, u_recv, u_keep, o_send, o_recv, o_keep,
    send_sems, recv_sems, local_sems,
):
    w = Wires(send_sems, recv_sems, local_sems)
    own = w.own
    core, chip = lax.rem(own, 2), own // 2
    mate = lax.bitwise_xor(own, 1)
    cx, cy, cd = (lax.bitwise_xor(chip, m) for m in (1, 2, 3))
    toks, width = x.shape
    ff = up_full.shape[1]
    head_width = heads.shape[1]
    half = toks // 2
    piece = up_w.shape[0]
    tile = 256
    w.greet([(w.rep, lax.bitwise_xor(own, m)) for m in range(1, 8)])

    swaps = []
    for m in (6, 2, 4, 1, 3, 5, 7):
        peer = lax.bitwise_xor(own, m)
        swaps.append(w.send(heads.at[rows_of(peer, toks)], att.at[:, rows_of(own, head_width)], peer))
    weights = []
    for m, src in ((0, None), (2, got_x), (4, got_y), (6, got_d)):
        dst = rows_of(lax.bitwise_xor(own, m), piece)
        src_out = out_w if src is None else src.at[pl.ds(piece, piece)]
        src_up = up_w.at[:, rows_of(chip, ff)] if src is None else src.at[pl.ds(0, piece)]
        for s, full in ((src_out, out_full), (src_up, up_full)):
            weights.append((w.local(s, full.at[dst]), w.send(s, full.at[dst], mate)))
    dst = rows_of(core, ff // 2)
    weights.append((w.local(down_w, down_full.at[dst]), w.send(down_w, down_full.at[dst], mate)))
    att[:, rows_of(own, head_width)] = heads[rows_of(own, toks), :]
    for copy in swaps:
        copy.wait_recv()
    for here, there in weights:
        here.wait()
        there.wait_recv()

    @pl.loop(0, width // tile)
    def _(n):
        cols = rows_of(n, tile)
        h1[:, cols] = nn(att[...], out_full[:, cols]) + proj_bias[2:3, cols] + x[:, cols].astype(F32)

    step = 32
    acc[...] = jnp.zeros_like(acc)

    def first_rows(t):
        rows = rows_of(t, step)
        v = h1[rows, :]
        center = v - jnp.mean(v, axis=1, keepdims=True)
        inv = lax.rsqrt(jnp.mean(center * center, axis=1, keepdims=True) + 1e-05)
        z = center * inv
        z1[rows, :] = z
        r1[rows, :] = jnp.broadcast_to(inv, (step, 128))
        fl[chip, rows, :] = (z * gain[0:1, :] + shift[0:1, :]).astype(BF16)

    spread = Spread(w, fl, half)
    pl.loop(0, half // step)(first_rows)
    spread.first_half()
    pl.loop(half // step, toks // step)(first_rows)
    spread.second_half()

    def forward(k):
        @pl.loop(0, ff // tile)
        def _(n):
            cols = rows_of(n, tile)
            hidden = nn(fl[k], up_full[:, cols]) + hidden_bias[:, pl.ds(pl.multiple_of(chip * ff + n * tile, tile), tile)]
            cdf = 0.5 * (1.0 + lax.erf(hidden * (2.0**-0.5)))
            act[k, :, cols] = (hidden * cdf).astype(BF16)
            slope[k, :, cols] = cdf + hidden * (jnp.exp(-0.5 * hidden * hidden) * ((2.0 * math.pi) ** -0.5))

        @pl.loop(0, width // tile)
        def _(n):
            cols = rows_of(n, tile)
            part[k, :, cols] = nn(act[k], down_full[:, cols]).astype(BF16)

    forward(chip)
    gather = Gather(w, part, side, last, half)
    spread.relay()
    spread.wait_sides()
    forward(cx)
    gather.send_x()
    forward(cy)
    gather.send_y()
    spread.wait_diagonal()
    forward(cd)
    gather.send_diagonal()
    gather.relay()

    def second_rows(which, t):
        rows = pl.ds(pl.multiple_of(which * half + t * step, step), step)
        v = z1[rows, :] * gain[0:1, :] + shift[0:1, :] + gather.total(which, t * step, step) + proj_bias[3:4, :]
        center = v - jnp.mean(v, axis=1, keepdims=True)
        inv = lax.rsqrt(jnp.mean(center * center, axis=1, keepdims=True) + 1e-05)
        z = center * inv
        output[rows, :] = (z * gain[1:2, :] + shift[1:2, :]).astype(BF16)
        c = cot[rows, :].astype(F32)
        e = c * gain[1:2, :]
        grad = inv * (e - jnp.mean(e, axis=1, keepdims=True) - z * jnp.mean(e * z, axis=1, keepdims=True))
        gs[rows, :] = grad
        low = grad.astype(BF16)
        sl[chip, rows, :] = low
        acc[0] += fold_rows(c * z)
        acc[1] += fold_rows(c)
        acc[2] += fold_rows(low.astype(F32))

    spread2 = Spread(w, sl, half)
    gather.wait_first()
    pl.loop(0, half // step)(functools.partial(second_rows, 0))
    spread2.first_half()
    gather.wait_second()
    pl.loop(0, half // step)(functools.partial(second_rows, 1))
    spread2.second_half()

    def backward(k):
        @pl.loop(0, ff // tile)
        def _(n):
            cols = rows_of(n, tile)
            grad = nt(sl[k], down_full[cols, :]) * slope[k, :, cols]
            low = grad.astype(BF16)
            pre[k, :, cols] = low
            acc[3, :, cols] += fold_rows(low.astype(F32))

        @pl.loop(0, width // tile)
        def _(n):
            cols = rows_of(n, tile)
            part2[k, :, cols] = nt(pre[k], up_full[cols, :]).astype(BF16)

    backward(chip)
    gather2 = Gather(w, part2, side2, last2, half)
    spread2.relay()
    spread2.wait_sides()
    backward(cx)
    gather2.send_x()
    backward(cy)
    gather2.send_y()
    spread2.wait_diagonal()
    backward(cd)
    gather2.send_diagonal()

    def down_rows(which, n):
        cols = pl.ds(pl.multiple_of(which * (ff // 2) + n * tile, tile), tile)
        lhs = act[:, :, cols].reshape(4 * toks, tile)
        return tn(lhs, sl[...].reshape(4 * toks, width))

    @pl.loop(0, ff // 2 // tile)
    def _(n):
        d_send[rows_of(n, tile), :] = down_rows(1 - core, n).astype(BF16)

    d_copy = w.send(d_send, d_recv, mate)
    gather2.relay()

    @pl.loop(0, ff // 2 // tile)
    def _(n):
        d_keep[rows_of(n, tile), :] = down_rows(core, n)

    def up_rows(which, k):
        cols = pl.ds(pl.multiple_of((2 * k + which) * piece, piece), piece)
        lhs = fl[:, :, cols].reshape(4 * toks, piece)
        return tn(lhs, pre[...].reshape(4 * toks, ff))

    @pl.loop(0, 4)
    def _(k):
        u_send[k] = up_rows(1 - core, k).astype(BF16)

    u_copy = w.send(u_send, u_recv, mate)

    def branch_rows(which, t):
        rows = pl.ds(pl.multiple_of(which * half + t * step, step), step)
        grad = gs[rows, :] + gather2.total(which, t * step, step)
        z = z1[rows, :]
        e = grad * gain[0:1, :]
        out = r1[rows, 0:1] * (e - jnp.mean(e, axis=1, keepdims=True) - z * jnp.mean(e * z, axis=1, keepdims=True))
        branch_grad[rows, :] = out
        low = out.astype(BF16)
        branch_low[rows, :] = low
        acc[4] += fold_rows(grad * z)
        acc[5] += fold_rows(grad)
        acc[6] += fold_rows(low.astype(F32))

    gather2.wait_first()
    pl.loop(0, half // step)(functools.partial(branch_rows, 0))
    gather2.wait_second()
    pl.loop(0, half // step)(functools.partial(branch_rows, 1))

    @pl.loop(0, width // tile)
    def _(n):
        cols = rows_of(n, tile)
        agl[:, cols] = nt(branch_low[...], out_full[cols, :]).astype(BF16)

    backs = []
    for m in (6, 2, 4, 1, 3, 5, 7):
        peer = lax.bitwise_xor(own, m)
        backs.append(w.send(agl.at[:, rows_of(peer, head_width)], grad_heads.at[rows_of(own, toks)], peer))
    grad_heads[rows_of(own, toks), :] = agl[:, rows_of(own, head_width)]

    def out_rows(which, k):
        cols = pl.ds(pl.multiple_of((2 * k + which) * piece, piece), piece)
        return tn(att[:, cols], branch_low[...])

    @pl.loop(0, 4)
    def _(k):
        o_send[k] = out_rows(1 - core, k).astype(BF16)

    o_copy = w.send(o_send, o_recv, mate)

    @pl.loop(0, 4)
    def _(k):
        u_keep[k] = up_rows(core, k)
        o_keep[k] = out_rows(core, k)

    d_copy.wait_recv()

    @pl.loop(0, ff // 2 // 64)
    def _(t):
        rows = rows_of(t, 64)
        down_grad[rows, :] = (d_keep[rows, :] + d_recv[rows, :].astype(F32)).astype(BF16)

    u_copy.wait_recv()
    o_copy.wait_recv()

    @pl.loop(0, 4)
    def _(k):
        upout_grad[k, 0] = (u_keep[k] + u_recv[k].astype(F32)).astype(BF16)
        upout_grad[k, 1] = (o_keep[k] + o_recv[k].astype(F32)).astype(BF16)

    vec[...] = jnp.zeros_like(vec)
    for row, slot in ((2, 6), (3, 2), (4, 4), (5, 0), (6, 5), (7, 1)):
        vec[row : row + 1, :] = jnp.sum(acc[slot], axis=0, keepdims=True)
    hidden_sum = jnp.sum(acc[3], axis=0, keepdims=True)
    for k in range(4):
        vec[8 + k : 9 + k, :] = jnp.where(chip == k, hidden_sum, jnp.zeros_like(hidden_sum))
    for copy in backs:
        copy.wait_recv()
    w.finish()


def middle(heads, x, cot, up_w, out_w, down_w, got_x, got_y, got_d, proj_bias, hidden_bias, gain, shift):
    toks, width = x.shape
    ff = up_w.shape[1] // 4
    piece = up_w.shape[0]
    half = toks // 2
    shape = jax.ShapeDtypeStruct
    vm = pltpu.VMEM
    return pl.pallas_call(
        middle_body,
        name="middle",
        out_shape=(
            shape((toks, width), BF16),
            shape((toks, width), F32),
            shape(heads.shape, BF16),
            shape((16, width), F32),
            shape((ff // 2, width), BF16),
            shape((4, 2, piece, width), BF16),
        ),
        in_specs=[VM, VM, VM] + [ANY] * 6 + [VM] * 4,
        out_specs=(VM,) * 6,
        scratch_shapes=[
            vm((toks, width), BF16), vm((width, width), BF16), vm((width, ff), BF16), vm((ff, width), BF16),
            vm((toks, width), F32), vm((toks, width), F32), vm((toks, 128), F32), vm((toks, width), F32),
            vm((4, toks, width), BF16), vm((4, toks, ff), BF16), vm((4, toks, ff), F32),
            vm((4, toks, width), BF16), vm((4, half, width), BF16), vm((2, half, width), BF16),
            vm((4, toks, width), BF16), vm((4, toks, ff), BF16),
            vm((4, toks, width), BF16), vm((4, half, width), BF16), vm((2, half, width), BF16),
            vm((toks, width), BF16), vm((toks, width), BF16), vm((8, 8, width), F32),
            vm((ff // 2, width), BF16), vm((ff // 2, width), BF16), vm((ff // 2, width), F32),
            vm((4, piece, ff), BF16), vm((4, piece, ff), BF16), vm((4, piece, ff), F32),
            vm((4, piece, width), BF16), vm((4, piece, width), BF16), vm((4, piece, width), F32),
            pltpu.SemaphoreType.DMA((64,)), pltpu.SemaphoreType.DMA((64,)), pltpu.SemaphoreType.DMA((16,)),
        ],
        compiler_params=pltpu.CompilerParams(collective_id=1, has_side_effects=True, vmem_limit_bytes=60 << 20),
    )(heads, x, cot, up_w, out_w, down_w, got_x, got_y, got_d, proj_bias, hidden_bias, gain, shift)


def project_body(x, qkv_w, proj_bias, q_out, k_out, v_out, xs, w_full, stage, send_sems, recv_sems, local_sems):
    w = Wires(send_sems, recv_sems, local_sems)
    own = w.own
    core, chip = lax.rem(own, 2), own // 2
    mate = lax.bitwise_xor(own, 1)
    toks, width = x.shape
    piece = qkv_w.shape[0]
    share = width // 4
    head_width = share // 2
    w.greet([(w.rep, lax.bitwise_xor(own, m)) for m in (1, 2, 4, 6)])
    mine = rows_of(own, piece)

    def source(part, to_chip):
        return qkv_w.at[:, pl.ds(pl.multiple_of(part * width + to_chip * share, share), share)]

    arrivals = []
    for m in (6, 2, 4):
        peer = lax.bitwise_xor(own, m)
        copies = [w.send(source(p, lax.bitwise_xor(chip, m // 2)), w_full.at[mine, pl.ds(p * share, share)], peer) for p in range(3)]
        arrivals.append((peer, copies))
    xs[chip] = x[...]
    spread = Spread(w, xs, toks // 2)
    spread.first_half()
    spread.second_half()
    here = [w.local(source(p, chip), w_full.at[mine, pl.ds(p * share, share)]) for p in range(3)]
    theirs = [w.send(source(p, chip), w_full.at[mine, pl.ds(p * share, share)], mate) for p in range(3)]
    for peer, copies in arrivals:
        for copy in copies:
            copy.wait_recv()
        rows = rows_of(peer, piece)
        theirs.append(w.send(w_full.at[rows], w_full.at[rows], mate))
    for copy in here:
        copy.wait()
    for copy in theirs:
        copy.wait_recv()
    outs = (q_out, k_out, v_out)
    swaps = []

    def block(k):
        rows = rows_of(2 * k + core, toks)
        for p in range(3):
            r = nn(xs[k], w_full[:, pl.ds(p * share, share)])
            if p != 1:
                r = r + proj_bias[p // 2 : p // 2 + 1, rows_of(chip, share)]
            stage[k, :, pl.ds(p * share, share)] = r.astype(BF16)
            swaps.append(w.send(stage.at[k, :, pl.ds(pl.multiple_of(p * share + (1 - core) * head_width, head_width), head_width)], outs[p].at[rows], mate))
            outs[p][rows, :] = stage[k, :, pl.ds(pl.multiple_of(p * share + core * head_width, head_width), head_width)]

    block(chip)
    spread.relay()
    spread.wait_sides()
    block(spread.cx)
    block(spread.cy)
    spread.wait_diagonal()
    block(spread.cd)
    for copy in swaps:
        copy.wait_recv()
    w.finish()


def project(x, qkv_w, proj_bias):
    toks, width = x.shape
    piece = qkv_w.shape[0]
    shape = jax.ShapeDtypeStruct
    vm = pltpu.VMEM
    heads = shape((8 * toks, width // 8), BF16)
    return pl.pallas_call(
        project_body,
        name="project",
        out_shape=(heads, heads, heads, shape((4, toks, width), BF16), shape((8 * piece, 3 * width // 4), BF16)),
        in_specs=[VM] * 3,
        out_specs=(VM,) * 5,
        scratch_shapes=[
            vm((4, toks, 3 * width // 4), BF16),
            pltpu.SemaphoreType.DMA((48,)), pltpu.SemaphoreType.DMA((48,)), pltpu.SemaphoreType.DMA((8,)),
        ],
        compiler_params=pltpu.CompilerParams(collective_id=0, has_side_effects=True, vmem_limit_bytes=40 << 20),
    )(x, qkv_w, proj_bias)


CHUNKS = 8


def finish_body(
    dq, dk, dv, xs, w_full, branch_grad, vec, input_grad, qkv_total, vec_total,
    grads, part, side, last, q_send, q_recv, q_keep, q_piece, z_own, z_in, z_mid, z_far, z_out, v_sum, v_recv,
    send_sems, recv_sems, local_sems,
):
    w = Wires(send_sems, recv_sems, local_sems)
    own, rep = w.own, w.rep
    core, chip = lax.rem(own, 2), own // 2
    mate = lax.bitwise_xor(own, 1)
    toks, width = branch_grad.shape
    share = width // 4
    head_width = share // 2
    piece = q_keep.shape[1]
    half = toks // 2
    tile = 256
    z1, z2, z3 = (lax.bitwise_xor(rep, m) for m in (1, 2, 3))
    w.greet([(rep, lax.bitwise_xor(own, m)) for m in (1, 2, 4, 6)] + [(z1, own), (z2, own), (z3, own)])

    swaps = []
    for p, g in enumerate((dq, dk, dv)):
        cols = pl.ds(pl.multiple_of(p * share + core * head_width, head_width), head_width)
        swaps.append(w.send(g.at[1 - core], grads.at[:, :, cols], mate))
        grads[:, :, cols] = g[core]
    v_sum[...] = vec[...]
    for row, g in ((0, dq), (1, dv)):
        total = jnp.sum(g[...].reshape(8 * toks, head_width).astype(F32), axis=0, keepdims=True)
        v_sum[row : row + 1, rows_of(own, head_width)] = total
    rounds = [(None, mate), (None, lax.bitwise_xor(own, 2)), (None, lax.bitwise_xor(own, 4)), (z1, own), (z2, own)]
    flying = []

    def vec_start(i):
        copy = w.remote(v_sum.at[...] if i == 0 else v_recv.at[4 + i], v_recv.at[i], rounds[i][1], rounds[i][0])
        copy.start()
        w.sent.append(copy)
        flying.append(copy)

    def vec_step(i):
        flying[i].wait_recv()
        base = v_sum[...] if i == 0 else v_recv[4 + i]
        if i < 4:
            v_recv[5 + i] = base + v_recv[i]
            vec_start(i + 1)
        else:
            vec_total[...] = base + v_recv[i]

    vec_start(0)
    for copy in swaps:
        copy.wait_recv()

    def qkv_rows(which, k):
        cols = pl.ds(pl.multiple_of((2 * k + which) * piece, piece), piece)
        return tn(xs[:, :, cols].reshape(4 * toks, piece), grads[...].reshape(4 * toks, 3 * share))

    @pl.loop(0, 4)
    def _(k):
        q_send[k] = qkv_rows(1 - core, k).astype(BF16)

    q_copy = w.send(q_send, q_recv, mate)

    @pl.loop(0, 4)
    def _(k):
        q_keep[k] = qkv_rows(core, k)

    q_copy.wait_recv()

    @pl.loop(0, 4)
    def _(k):
        q_piece[k] = (q_keep[k] + q_recv[k].astype(F32)).astype(BF16)

    moved = []
    for m in (6, 2, 4):
        peer = lax.bitwise_xor(own, m)
        for p in range(3):
            dst = z_own.at[:, pl.ds(pl.multiple_of(p * width + chip * share, share), share)]
            moved.append(w.send(q_piece.at[lax.bitwise_xor(chip, m // 2), :, pl.ds(p * share, share)], dst, peer))
    for p in range(3):
        z_own[:, pl.ds(pl.multiple_of(p * width + chip * share, share), share)] = q_piece[chip, :, pl.ds(p * share, share)]
    vec_step(0)

    def partial(k):
        @pl.loop(0, width // tile)
        def _(n):
            cols = rows_of(n, tile)
            part[k, :, cols] = nt(grads[k], w_full[cols, :]).astype(BF16)

    gather = Gather(w, part, side, last, half)
    partial(gather.cd)
    gather.send_diagonal()
    partial(gather.cx)
    gather.send_x()
    partial(gather.cy)
    gather.send_y()
    partial(chip)
    vec_step(1)
    for copy in moved:
        copy.wait_recv()

    size = piece // CHUNKS
    inner = jnp.logical_or(rep == 1, rep == 2)
    first, middle_hop, back = [], [], []
    for i in range(CHUNKS):
        rows = pl.ds(i * size, size)
        first.append(w.remote(z_own.at[rows], z_in.at[rows], own, z1))
    for i in range(CHUNKS):
        rows = pl.ds(i * size, size)
        middle_hop.append(w.remote(z_mid.at[rows], z_far.at[rows], own, z3))
    for i in range(CHUNKS):
        rows = pl.ds(i * size, size)
        back.append(w.remote(z_out.at[rows], z_out.at[rows], own, z1))

    @pl.when(jnp.logical_not(inner))
    def _():
        for i in range(CHUNKS):
            first[i].start()

    @pl.when(inner)
    def _():
        for i in range(CHUNKS):
            rows = pl.ds(i * size, size)
            first[i].wait_recv()
            z_mid[rows, :] = (z_own[rows, :].astype(F32) + z_in[rows, :].astype(F32)).astype(BF16)
            middle_hop[i].start()

    gather.relay()
    vec_step(2)

    @pl.when(inner)
    def _():
        for i in range(CHUNKS):
            rows = pl.ds(i * size, size)
            middle_hop[i].wait_recv()
            z_out[rows, :] = (z_mid[rows, :].astype(F32) + z_far[rows, :].astype(F32)).astype(BF16)
            back[i].start()

    vec_step(3)
    step = 32

    def final_rows(which, t):
        rows = pl.ds(pl.multiple_of(which * half + t * step, step), step)
        input_grad[rows, :] = (branch_grad[rows, :] + gather.total(which, t * step, step)).astype(BF16)

    gather.wait_first()
    pl.loop(0, half // step)(functools.partial(final_rows, 0))
    gather.wait_second()
    pl.loop(0, half // step)(functools.partial(final_rows, 1))
    vec_step(4)

    @pl.when(jnp.logical_not(inner))
    def _():
        for i in range(CHUNKS):
            first[i].wait_send()
            back[i].wait_recv()

    @pl.when(inner)
    def _():
        for i in range(CHUNKS):
            middle_hop[i].wait_send()
            back[i].wait_send()

    qkv_total[...] = z_out[...]
    w.finish()


def finish(dq, dk, dv, xs, w_full, branch_grad, vec):
    toks, width = branch_grad.shape
    piece = w_full.shape[0] // 8
    half = toks // 2
    shape = jax.ShapeDtypeStruct
    vm = pltpu.VMEM
    line = vm((piece, 3 * width), BF16)
    return pl.pallas_call(
        finish_body,
        name="finish",
        out_shape=(shape((toks, width), BF16), shape((piece, 3 * width), BF16), shape(vec.shape, F32)),
        in_specs=[VM] * 7,
        out_specs=(VM,) * 3,
        scratch_shapes=[
            vm((4, toks, 3 * width // 4), BF16),
            vm((4, toks, width), BF16), vm((4, half, width), BF16), vm((2, half, width), BF16),
            vm((4, piece, 3 * width // 4), BF16), vm((4, piece, 3 * width // 4), BF16), vm((4, piece, 3 * width // 4), F32),
            vm((4, piece, 3 * width // 4), BF16),
            line, line, line, line, line,
            vm(vec.shape, F32), vm((9,) + vec.shape, F32),
            pltpu.SemaphoreType.DMA((64,)), pltpu.SemaphoreType.DMA((64,)), pltpu.SemaphoreType.DMA((8,)),
        ],
        compiler_params=pltpu.CompilerParams(collective_id=2, has_side_effects=True, vmem_limit_bytes=48 << 20),
    )(dq, dk, dv, xs, w_full, branch_grad, vec)


def local_tensor(tokens, segment_ids, qkv_weight, out_weight, up_weight, down_weight, proj_bias, hidden_bias, norm_gain, norm_shift, cotangent):
    inputs = tokens[0]
    toks, width = inputs.shape
    scale = (width // HEADS) ** (-0.5)
    own = lax.axis_index("fsdp")
    chip = own // 2
    ff = up_weight.shape[1] // 4
    piece = up_weight.shape[0]

    def for_chip(mask):
        cols = lax.dynamic_slice_in_dim(up_weight, lax.bitwise_xor(chip, mask // 2) * ff, ff, axis=1)
        return jnp.concatenate([cols, out_weight], axis=0)

    got_x, got_y, got_d = (lax.ppermute(for_chip(m), "fsdp", [(i, i ^ m) for i in range(8)]) for m in (2, 4, 6))
    queries, key_rows, value_rows, xs, w_full = project(inputs, qkv_weight, proj_bias)
    attended, attended_low, lse = attn_fwd(scale, segment_ids, queries, key_rows, value_rows)
    output, branch_grad, grad_heads, vec, down_part, upout_part = middle(
        attended_low, inputs, cotangent[0], up_weight, out_weight, down_weight, got_x, got_y, got_d,
        proj_bias, hidden_bias[None], norm_gain, norm_shift,
    )
    back_x, back_y, back_d = (
        lax.ppermute(lax.dynamic_index_in_dim(upout_part, lax.bitwise_xor(chip, m // 2), keepdims=False), "fsdp", [(i, i ^ m) for i in range(8)])
        for m in (2, 4, 6)
    )
    kept = lax.dynamic_index_in_dim(upout_part, chip, keepdims=False)
    up_sum = jnp.zeros((piece, 4 * ff), BF16)
    for m, block in ((0, kept), (2, back_x), (4, back_y), (6, back_d)):
        up_sum = lax.dynamic_update_slice_in_dim(up_sum, block[0], lax.bitwise_xor(chip, m // 2) * ff, axis=1)
    out_sum = sum(b[1].astype(F32) for b in (kept, back_x, back_y, back_d)).astype(BF16)
    down_total, up_total, out_total = lax.psum((down_part, up_sum, out_sum), "rep")
    query_grad, key_grad, value_grad = attn_bwd(scale, segment_ids, queries, key_rows, value_rows, grad_heads, attended, lse)
    input_grad, qkv_total, vec_total = finish(query_grad, key_grad, value_grad, xs, w_full, branch_grad, vec)
    grad_scale = (toks * lax.axis_size("fsdp") * lax.axis_size("rep")) ** (-0.5)
    scaled = vec_total * grad_scale
    return (
        output[None],
        input_grad[None],
        qkv_total.astype(F32) * grad_scale,
        out_total.astype(F32) * grad_scale,
        up_total.astype(F32) * grad_scale,
        down_total.astype(F32) * grad_scale,
        scaled[0:4],
        scaled[8:12].reshape(4 * width),
        scaled[4:6],
        scaled[6:8],
    )


def normalize(hidden, gain, shift):
    center = hidden - jnp.mean(hidden, axis=-1, keepdims=True)
    spread = jnp.mean(center * center, axis=-1, keepdims=True)
    return center * lax.rsqrt(spread + 1e-05) * gain + shift


def exact_gelu(value):
    return jax.nn.gelu(value, approximate=False)


def gather_attention(qkv_weight, out_weight):
    return (
        lax.all_gather(qkv_weight, "fsdp", axis=0, tiled=True),
        lax.all_gather(out_weight, "fsdp", axis=0, tiled=True),
    )


def gather_feedforward(up_weight, down_weight):
    return (
        lax.all_gather(up_weight, "fsdp", axis=0, tiled=True),
        lax.all_gather(down_weight, "fsdp", axis=0, tiled=True),
    )


def block_plan(row_count):
    block_rows = math.gcd(row_count, 1024)
    return (block_rows, row_count // block_rows)


def split_heads(matrix):
    return matrix.reshape(matrix.shape[0], HEADS, matrix.shape[1] // HEADS)


def join_heads(stacked):
    return jnp.transpose(stacked, (1, 0, 2)).reshape(
        stacked.shape[1], stacked.shape[0] * stacked.shape[2]
    )


def local_gather(
    tokens,
    segment_ids,
    qkv_weight,
    out_weight,
    up_weight,
    down_weight,
    proj_bias,
    hidden_bias,
    norm_gain,
    norm_shift,
    cotangent,
):
    inputs = tokens[0]
    tok_count, model_width = inputs.shape
    head_dim = model_width // HEADS
    score_scale = head_dim ** (-0.5)
    doc_ids = segment_ids[0]
    own_index = lax.axis_index("fsdp")
    own_docs = lax.dynamic_slice_in_dim(doc_ids, own_index * tok_count, tok_count)
    qkv_full, out_full = gather_attention(qkv_weight, out_weight)
    projected = jnp.dot(inputs, qkv_full, preferred_element_type=jnp.float32)
    queries = (projected[:, :model_width] + proj_bias[0]).astype(jnp.bfloat16)
    key_rows = projected[:, model_width : 2 * model_width].astype(jnp.bfloat16)
    value_rows = (projected[:, 2 * model_width :] + proj_bias[1]).astype(jnp.bfloat16)
    query_heads = split_heads(queries)
    key_own = split_heads(key_rows)
    value_own = split_heads(value_rows)
    initial = (
        jnp.zeros((HEADS, tok_count, head_dim), jnp.float32),
        jnp.full((HEADS, tok_count), NEGATIVE, jnp.float32),
        jnp.zeros((HEADS, tok_count), jnp.float32),
    )
    key_piece = lax.all_gather(key_rows, "fsdp", axis=0, tiled=True)
    value_piece = lax.all_gather(value_rows, "fsdp", axis=0, tiled=True)
    block_rows, blocks = block_plan(key_piece.shape[0])

    def forward_advance(block_index, running_state):
        weighted, running, denominator = running_state
        offset = block_index * block_rows
        key_block = split_heads(lax.dynamic_slice_in_dim(key_piece, offset, block_rows))
        value_block = split_heads(lax.dynamic_slice_in_dim(value_piece, offset, block_rows))
        block_docs = lax.dynamic_slice_in_dim(doc_ids, offset, block_rows)
        scores = (
            jnp.einsum("qhd,khd->hqk", query_heads, key_block, preferred_element_type=jnp.float32)
            * score_scale
        )
        same_doc = (own_docs[:, None] == block_docs[None, :])[None]
        highest = jnp.maximum(running, jnp.max(jnp.where(same_doc, scores, NEGATIVE), axis=2))
        factor = jnp.exp(running - highest)
        weights = jnp.where(same_doc, jnp.exp(scores - highest[:, :, None]), 0.0)
        denominator = denominator * factor + jnp.sum(weights, axis=2)
        weighted = weighted * factor[:, :, None] + jnp.einsum(
            "hqk,khd->hqd",
            weights.astype(jnp.bfloat16),
            value_block,
            preferred_element_type=jnp.float32,
        )
        return (weighted, highest, denominator)

    weighted, running, denominator = lax.fori_loop(0, blocks, forward_advance, initial)
    attended_heads = weighted / denominator[:, :, None]
    log_total = running + jnp.log(denominator)
    attended_low = join_heads(attended_heads).astype(jnp.bfloat16)
    branch = jnp.dot(attended_low, out_full, preferred_element_type=jnp.float32) + proj_bias[2]
    first_norm, norm_one_back = jax.vjp(
        normalize, inputs.astype(jnp.float32) + branch, norm_gain[0], norm_shift[0]
    )
    first_low = first_norm.astype(jnp.bfloat16)
    up_full, down_full = gather_feedforward(up_weight, down_weight)
    hidden_pre = jnp.dot(first_low, up_full, preferred_element_type=jnp.float32) + hidden_bias
    activated, gelu_back = jax.vjp(exact_gelu, hidden_pre)
    activated_low = activated.astype(jnp.bfloat16)
    second = jnp.dot(activated_low, down_full, preferred_element_type=jnp.float32) + proj_bias[3]
    output, norm_two_back = jax.vjp(normalize, first_norm + second, norm_gain[1], norm_shift[1])
    up_back, down_back = gather_feedforward(up_weight, down_weight)
    qkv_back, out_back = gather_attention(qkv_weight, out_weight)
    grad_second, gain_two, shift_two = norm_two_back(cotangent[0].astype(jnp.float32))
    second_low = grad_second.astype(jnp.bfloat16)
    down_term = jnp.einsum(
        "tf,td->fd", activated_low, second_low, preferred_element_type=jnp.float32
    )
    activated_grad = jnp.einsum(
        "td,fd->tf", second_low, down_back, preferred_element_type=jnp.float32
    )
    (pre_grad,) = gelu_back(activated_grad)
    pre_low = pre_grad.astype(jnp.bfloat16)
    up_term = jnp.einsum("td,tf->df", first_low, pre_low, preferred_element_type=jnp.float32)
    first_grad = grad_second + jnp.einsum(
        "tf,df->td", pre_low, up_back, preferred_element_type=jnp.float32
    )
    branch_grad, gain_one, shift_one = norm_one_back(first_grad)
    branch_low = branch_grad.astype(jnp.bfloat16)
    out_term = jnp.einsum("te,td->ed", attended_low, branch_low, preferred_element_type=jnp.float32)
    attended_grad = jnp.einsum(
        "td,ed->te", branch_low, out_back, preferred_element_type=jnp.float32
    ).astype(jnp.bfloat16)
    grad_heads = split_heads(attended_grad)
    correction = jnp.einsum("qhd,hqd->hq", grad_heads.astype(jnp.float32), attended_heads)
    lse_all, correction_all = (
        lax.all_gather(log_total, "fsdp", axis=1, tiled=True),
        lax.all_gather(correction, "fsdp", axis=1, tiled=True),
    )
    query_key_piece = lax.all_gather(key_rows, "fsdp", axis=0, tiled=True)
    query_value_piece = lax.all_gather(value_rows, "fsdp", axis=0, tiled=True)
    query_block_rows, blocks = block_plan(query_key_piece.shape[0])

    def query_advance(block_index, query_state):
        offset = block_index * query_block_rows
        key_block = split_heads(lax.dynamic_slice_in_dim(query_key_piece, offset, query_block_rows))
        value_block = split_heads(
            lax.dynamic_slice_in_dim(query_value_piece, offset, query_block_rows)
        )
        block_docs = lax.dynamic_slice_in_dim(doc_ids, offset, query_block_rows)
        scores = (
            jnp.einsum("qhd,khd->hqk", query_heads, key_block, preferred_element_type=jnp.float32)
            * score_scale
        )
        same_doc = (own_docs[:, None] == block_docs[None, :])[None]
        probabilities = jnp.where(same_doc, jnp.exp(scores - log_total[:, :, None]), 0.0)
        prob_grad = jnp.einsum(
            "qhd,khd->hqk", grad_heads, value_block, preferred_element_type=jnp.float32
        )
        score_grad = (probabilities * (prob_grad - correction[:, :, None])).astype(jnp.bfloat16)
        return query_state + jnp.einsum(
            "hqk,khd->hqd", score_grad, key_block, preferred_element_type=jnp.float32
        )

    query_acc = lax.fori_loop(
        0, blocks, query_advance, jnp.zeros((HEADS, tok_count, head_dim), jnp.float32)
    )
    query_grad = (join_heads(query_acc) * score_scale).astype(jnp.bfloat16)
    empty_heads = jnp.zeros((HEADS, tok_count, head_dim), jnp.float32)
    query_piece = lax.all_gather(queries, "fsdp", axis=0, tiled=True)
    grad_piece = lax.all_gather(attended_grad, "fsdp", axis=0, tiled=True)
    key_block_rows, blocks = block_plan(query_piece.shape[0])

    def key_advance(block_index, key_state):
        key_acc, value_acc = key_state
        offset = block_index * key_block_rows
        query_block = split_heads(lax.dynamic_slice_in_dim(query_piece, offset, key_block_rows))
        grad_block = split_heads(lax.dynamic_slice_in_dim(grad_piece, offset, key_block_rows))
        block_docs = lax.dynamic_slice_in_dim(doc_ids, offset, key_block_rows)
        lse_block = lax.dynamic_slice_in_dim(lse_all, offset, key_block_rows, axis=1)
        corr_block = lax.dynamic_slice_in_dim(correction_all, offset, key_block_rows, axis=1)
        scores = (
            jnp.einsum("qhd,khd->hqk", query_block, key_own, preferred_element_type=jnp.float32)
            * score_scale
        )
        same_doc = (block_docs[:, None] == own_docs[None, :])[None]
        probabilities = jnp.where(same_doc, jnp.exp(scores - lse_block[:, :, None]), 0.0)
        value_acc = value_acc + jnp.einsum(
            "hqk,qhd->hkd",
            probabilities.astype(jnp.bfloat16),
            grad_block,
            preferred_element_type=jnp.float32,
        )
        prob_grad = jnp.einsum(
            "qhd,khd->hqk", grad_block, value_own, preferred_element_type=jnp.float32
        )
        score_grad = (probabilities * (prob_grad - corr_block[:, :, None])).astype(jnp.bfloat16)
        key_acc = key_acc + jnp.einsum(
            "hqk,qhd->hkd", score_grad, query_block, preferred_element_type=jnp.float32
        )
        return (key_acc, value_acc)

    key_acc, value_acc = lax.fori_loop(0, blocks, key_advance, (empty_heads, empty_heads))
    key_grad = (join_heads(key_acc) * score_scale).astype(jnp.bfloat16)
    value_grad = join_heads(value_acc).astype(jnp.bfloat16)
    qkv_grad_low = jnp.concatenate([query_grad, key_grad, value_grad], axis=1)
    qkv_term = jnp.einsum("td,te->de", inputs, qkv_grad_low, preferred_element_type=jnp.float32)
    input_grad = branch_grad + jnp.einsum(
        "te,de->td", qkv_grad_low, qkv_back, preferred_element_type=jnp.float32
    )
    bias_term = jnp.stack(
        [
            jnp.sum(query_grad.astype(jnp.float32), axis=0),
            jnp.sum(value_grad.astype(jnp.float32), axis=0),
            jnp.sum(branch_low.astype(jnp.float32), axis=0),
            jnp.sum(second_low.astype(jnp.float32), axis=0),
        ]
    )
    hidden_term = jnp.sum(pre_low.astype(jnp.float32), axis=0)
    gain_term = jnp.stack([gain_one, gain_two])
    shift_term = jnp.stack([shift_one, shift_two])
    bias_total, hidden_total, gain_total, shift_total = lax.psum(
        (bias_term, hidden_term, gain_term, shift_term), ("rep", "fsdp")
    )
    up_sum, down_sum = (
        lax.psum_scatter(up_term, "fsdp", scatter_dimension=0, tiled=True),
        lax.psum_scatter(down_term, "fsdp", scatter_dimension=0, tiled=True),
    )
    qkv_sum, out_sum = (
        lax.psum_scatter(qkv_term, "fsdp", scatter_dimension=0, tiled=True),
        lax.psum_scatter(out_term, "fsdp", scatter_dimension=0, tiled=True),
    )
    qkv_total, out_total, up_total, down_total = lax.psum(
        (qkv_sum, out_sum, up_sum, down_sum), "rep"
    )
    grad_scale = (tok_count * lax.axis_size("fsdp") * lax.axis_size("rep")) ** (-0.5)
    return (
        output.astype(jnp.bfloat16)[None],
        input_grad.astype(jnp.bfloat16)[None],
        qkv_total * grad_scale,
        out_total * grad_scale,
        up_total * grad_scale,
        down_total * grad_scale,
        bias_total * grad_scale,
        hidden_total * grad_scale,
        gain_total * grad_scale,
        shift_total * grad_scale,
    )


def solution(mesh):
    small = mesh.shape["fsdp"] == 8 and mesh.shape["rep"] == 4
    local = local_tensor if small else local_gather
    return jax.shard_map(
        local,
        mesh=mesh,
        in_specs=(
            P("rep", "fsdp", None),
            P("rep", None),
            P("fsdp", None),
            P("fsdp", None),
            P("fsdp", None),
            P("fsdp", None),
            P(),
            P(),
            P(),
            P(),
            P("rep", "fsdp", None),
        ),
        out_specs=(
            P("rep", "fsdp", None),
            P("rep", "fsdp", None),
            P("fsdp", None),
            P("fsdp", None),
            P("fsdp", None),
            P("fsdp", None),
            P(),
            P(),
            P(),
            P(),
        ),
        check_vma=False,
    )
```

```python
import functools
import math

import jax
import jax.numpy as jnp
from jax import lax
from jax.experimental import pallas as pl
from jax.experimental.pallas import tpu as pltpu
from jax.sharding import PartitionSpec as P

HEADS = 16

NEGATIVE = -1e30
BQ = 256
BK = 512
VM = pl.BlockSpec(memory_space=pltpu.VMEM)
SM = pl.BlockSpec(memory_space=pltpu.SMEM)


def nt(a, b):
    return lax.dot_general(a, b, (((1,), (1,)), ((), ())), preferred_element_type=jnp.float32)


def nn(a, b):
    return jnp.dot(a, b, preferred_element_type=jnp.float32)


def block_range(seg_s, start, size, blk, n):
    first = seg_s[0, start]
    last = seg_s[0, start + size - 1]
    lo = jnp.int32(0)
    hi = jnp.int32(0)
    for j in range(n):
        lo = lo + (seg_s[0, j * blk + blk - 1] < first).astype(jnp.int32)
        hi = hi + (seg_s[0, j * blk] <= last).astype(jnp.int32)
    return lo, hi


def head_lanes(shape, half):
    return lax.broadcasted_iota(jnp.int32, shape, 1) < half


def rows_of(index, size):
    return pl.ds(pl.multiple_of(index * size, size), size)


def seg_columns(seg_v, seg_c):
    length = seg_c.shape[0]

    @pl.loop(0, length // BQ)
    def _(i):
        rows = rows_of(i, BQ)
        seg_c[rows, :] = jnp.transpose(jnp.broadcast_to(seg_v[:, rows].astype(jnp.float32), (128, BQ)))


def wide(column, lanes):
    return jnp.concatenate([column] * (lanes // 128), axis=1)


def attn_fwd_body(scale, seg_s, seg_v, q_ref, k_ref, v_ref, o_ref, a_ref, lse_ref, vt, seg_c):
    length, width = q_ref.shape
    half = width // 2
    n = length // BQ
    first = head_lanes((BQ, width), half)
    seg_columns(seg_v, seg_c)

    @pl.loop(0, n)
    def _(i):
        rows = rows_of(i, BQ)
        t = jnp.transpose(v_ref[rows, :])
        for h in range(2):
            vt[h, 0:half, rows] = t[h * half : (h + 1) * half]
            vt[h, half : half + 16, rows] = jnp.ones((16, BQ), jnp.bfloat16)

    sides = []
    heads = (lax.broadcasted_iota(jnp.int32, (16, width), 1) < half) == (lax.broadcasted_iota(jnp.int32, (16, width), 0) < 8)
    heads = heads.astype(jnp.float32).astype(jnp.bfloat16)
    for ref in (q_ref, k_ref):
        squares = nt(heads, ref[...] * ref[...])
        sides.append((jnp.max(squares[0:8]), jnp.max(squares[8:16])))
    bound = (40.0 / scale) ** 2
    small = jnp.logical_and(sides[0][0] * sides[1][0] <= bound, sides[0][1] * sides[1][1] <= bound)

    @pl.loop(0, n)
    def _(i):
        lo, hi = block_range(seg_s, i * BQ, BQ, BK, length // BK)
        rows = rows_of(i, BQ)
        q = q_ref[rows, :] * jnp.bfloat16(scale)
        zero = jnp.zeros_like(q)
        qs = (jnp.where(first, q, zero), jnp.where(first, zero, q))
        seg_q = seg_v[:, rows].astype(jnp.float32)


        def masked(cols, h):
            same = wide(seg_c[cols, :], BQ) == seg_q
            return jnp.where(same, nt(k_ref[cols, :], qs[h]), NEGATIVE)

        def store(tops, accs):
            o = []
            for h in range(2):
                total = accs[h][half : half + 1]
                o.append(accs[h][0:half] / total)
                lse_ref[h : h + 1, rows] = tops[h] + jnp.log(total)
            o = jnp.transpose(jnp.concatenate(o, axis=0))
            o_ref[rows, :] = o
            a_ref[rows, :] = o.astype(jnp.bfloat16)

        def direct(count):
            base = jnp.minimum(lo, length // BK - count)
            accs = [jnp.zeros((half + 16, BQ), jnp.float32)] * 2
            for j in range(count):
                cols = rows_of(base + j, BK)
                for h in range(2):
                    accs[h] = accs[h] + nn(vt[h, :, cols], jnp.exp(masked(cols, h)).astype(jnp.bfloat16))
            store([jnp.zeros((1, BQ), jnp.float32)] * 2, accs)

        def running():
            def step(j, state):
                cols = rows_of(j, BK)
                out = []
                for h in range(2):
                    m, acc = state[h]
                    s = masked(cols, h)
                    top = jnp.maximum(m, jnp.max(s, axis=0, keepdims=True))
                    p = jnp.exp(s - top).astype(jnp.bfloat16)
                    out.append((top, acc * jnp.exp(m - top) + nn(vt[h, :, cols], p)))
                return tuple(out)

            one = (jnp.full((1, BQ), NEGATIVE, jnp.float32), jnp.zeros((half + 16, BQ), jnp.float32))
            state = lax.fori_loop(lo, hi, step, (one, one))
            store([state[h][0] for h in range(2)], [state[h][1] for h in range(2)])

        for count in range(1, length // BK + 1):
            pl.when(jnp.logical_and(small, hi - lo == count))(functools.partial(direct, count))
        pl.when(jnp.logical_not(small))(running)


def attn_fwd(scale, seg, q, k, v):
    length, width = q.shape
    return pl.pallas_call(
        functools.partial(attn_fwd_body, scale),
        name="attn_fwd",
        out_shape=(
            jax.ShapeDtypeStruct((length, width), jnp.float32),
            jax.ShapeDtypeStruct((length, width), jnp.bfloat16),
            jax.ShapeDtypeStruct((8, length), jnp.float32),
        ),
        in_specs=[SM, VM, VM, VM, VM],
        out_specs=(VM, VM, VM),
        scratch_shapes=[pltpu.VMEM((2, width // 2 + 16, length), jnp.bfloat16), pltpu.VMEM((length, 128), jnp.float32)],
        compiler_params=pltpu.CompilerParams(vmem_limit_bytes=32 << 20),
        cost_estimate=pl.CostEstimate(flops=4 * length * length * width, bytes_accessed=6 * length * width, transcendentals=2 * length * length),
    )(seg, seg, q, k, v)


def attn_bwd_body(scale, seg_s, seg_v, q_ref, k_ref, v_ref, g_ref, o_ref, lse_ref, dq_ref, dk_ref, dv_ref, corr, kt, dk_acc, dv_acc, dqt, seg_c):
    length, width = q_ref.shape
    half = width // 2
    n = length // BQ
    first = head_lanes((BQ, width), half)
    seg_columns(seg_v, seg_c)

    @pl.loop(0, n)
    def _(i):
        rows = rows_of(i, BQ)
        prod = jnp.transpose(g_ref[rows, :].astype(jnp.float32) * o_ref[rows, :])
        corr[0:1, rows] = jnp.sum(prod[:half], axis=0, keepdims=True)
        corr[1:2, rows] = jnp.sum(prod[half:], axis=0, keepdims=True)
        kt[:, rows] = jnp.transpose(k_ref[rows, :])
        dk_acc[rows, :] = jnp.zeros((BQ, width), jnp.float32)
        dv_acc[rows, :] = jnp.zeros((BQ, width), jnp.float32)

    @pl.loop(0, n)
    def _(i):
        lo, hi = block_range(seg_s, i * BQ, BQ, BK, length // BK)
        rows = rows_of(i, BQ)
        qb = q_ref[rows, :] * jnp.bfloat16(scale)
        gb = g_ref[rows, :]
        zero = jnp.zeros_like(qb)
        qs = (jnp.where(first, qb, zero), jnp.where(first, zero, qb))
        gs = (jnp.where(first, gb, zero), jnp.where(first, zero, gb))
        qz = jnp.concatenate(qs, axis=0)
        gz = jnp.concatenate(gs, axis=0)
        seg_q = seg_v[:, rows].astype(jnp.float32)

        def term(cols, dq):
            kb = k_ref[cols, :]
            vb = v_ref[cols, :]
            same = wide(seg_c[cols, :], BQ) == seg_q
            ps, ds = [], []
            for h in range(2):
                s = jnp.where(same, nt(kb, qs[h]), NEGATIVE)
                p = jnp.exp(s - lse_ref[h : h + 1, rows])
                dp = nt(vb, gs[h])
                d = (p * (dp - corr[h : h + 1, rows])).astype(jnp.bfloat16)
                ps.append(p.astype(jnp.bfloat16))
                ds.append(d)
                dq[h] = dq[h] + nn(kt[h * half : (h + 1) * half, cols], d)
            dv_acc[cols, :] += nn(jnp.concatenate(ps, axis=1), gz)
            dk_acc[cols, :] += nn(jnp.concatenate(ds, axis=1), qz)
            return dq

        def run(count):
            base = jnp.minimum(lo, length // BK - count)
            dq = [jnp.zeros((half, BQ), jnp.float32)] * 2
            for j in range(count):
                dq = term(rows_of(base + j, BK), dq)
            dqt[0:half, :] = dq[0]
            dqt[half:, :] = dq[1]

        for count in range(1, length // BK + 1):
            pl.when(hi - lo == count)(functools.partial(run, count))
        dq_ref[lax.rem(i, 2), i // 2] = (jnp.transpose(dqt[...]) * scale).astype(jnp.bfloat16)

    @pl.loop(0, n)
    def _(i):
        rows = rows_of(i, BQ)
        dk_ref[lax.rem(i, 2), i // 2] = dk_acc[rows, :].astype(jnp.bfloat16)
        dv_ref[lax.rem(i, 2), i // 2] = dv_acc[rows, :].astype(jnp.bfloat16)


def attn_bwd(scale, seg, q, k, v, g, o, lse):
    length, width = q.shape
    return pl.pallas_call(
        functools.partial(attn_bwd_body, scale),
        name="attn_bwd",
        out_shape=tuple(jax.ShapeDtypeStruct((2, length // BQ // 2, BQ, width), jnp.bfloat16) for _ in range(3)),
        in_specs=[SM, VM, VM, VM, VM, VM, VM, VM],
        out_specs=(VM, VM, VM),
        scratch_shapes=[
            pltpu.VMEM((8, length), jnp.float32),
            pltpu.VMEM((width, length), jnp.bfloat16),
            pltpu.VMEM((length, width), jnp.float32),
            pltpu.VMEM((length, width), jnp.float32),
            pltpu.VMEM((width, BQ), jnp.float32),
            pltpu.VMEM((length, 128), jnp.float32),
        ],
        compiler_params=pltpu.CompilerParams(vmem_limit_bytes=32 << 20),
        cost_estimate=pl.CostEstimate(flops=10 * length * length * width, bytes_accessed=14 * length * width, transcendentals=2 * length * length),
    )(seg, seg, q, k, v, g, o, lse)


MESH = pl.DeviceIdType.MESH
HBM = pl.BlockSpec(memory_space=pltpu.HBM)
F32 = jnp.float32
BF16 = jnp.bfloat16


def tn(a, b):
    return lax.dot_general(a, b, (((0,), (0,)), ((), ())), preferred_element_type=F32)


def fold_rows(v):
    return jnp.sum(v.reshape(v.shape[0] // 8, 8, v.shape[1]), axis=0)


class Wires:
    def __init__(self, send_sems, recv_sems, local_sems):
        self.send_sems, self.recv_sems, self.local_sems = send_sems, recv_sems, local_sems
        self.count = 0
        self.local_count = 0
        self.sent = []
        self.rep = lax.axis_index("rep")
        self.own = lax.axis_index("fsdp")

    def remote(self, src, dst, peer, rep=None):
        i = self.count
        self.count = i + 1
        return pltpu.make_async_remote_copy(
            src_ref=src, dst_ref=dst, send_sem=self.send_sems.at[i], recv_sem=self.recv_sems.at[i],
            device_id=(self.rep if rep is None else rep, peer), device_id_type=MESH,
        )

    def send(self, src, dst, peer):
        copy = self.remote(src, dst, peer)
        copy.start()
        self.sent.append(copy)
        return copy

    def local(self, src, dst):
        copy = pltpu.make_async_copy(src, dst, self.local_sems.at[self.local_count])
        self.local_count += 1
        copy.start()
        return copy

    def greet(self, peers):
        barrier = pltpu.get_barrier_semaphore()
        for rep, peer in peers:
            pl.semaphore_signal(barrier, inc=1, device_id=(rep, peer), device_id_type=MESH)
        pl.semaphore_wait(barrier, len(peers))

    def finish(self):
        for copy in self.sent:
            copy.wait_send()


class Line:
    def __init__(self, wires, own, land, far, count):
        self.own, self.land, self.far = own, land, far
        rep, dev = wires.rep, wires.own
        size = own.shape[0] // count
        self.rows = [pl.ds(i * size, size) for i in range(count)]
        self.inner = jnp.logical_or(rep == 1, rep == 2)
        self.outer = jnp.logical_not(self.inner)
        near, across = lax.bitwise_xor(rep, 1), lax.bitwise_xor(rep, 3)
        self.first = [wires.remote(own.at[r], land.at[r], dev, near) for r in self.rows]
        self.middle = [wires.remote(own.at[r], far.at[r], dev, across) for r in self.rows]
        self.back = [wires.remote(land.at[r], land.at[r], dev, near) for r in self.rows]

    def start(self):
        @pl.when(self.outer)
        def _():
            for copy in self.first:
                copy.start()

    def collect(self, which):
        @pl.when(self.inner)
        def _():
            for i in which:
                r = self.rows[i]
                self.first[i].wait_recv()
                self.own[r, :] = (self.own[r, :].astype(F32) + self.land[r, :].astype(F32)).astype(BF16)
                self.middle[i].start()

    def total(self, which):
        @pl.when(self.inner)
        def _():
            for i in which:
                r = self.rows[i]
                self.middle[i].wait_recv()
                self.land[r, :] = (self.own[r, :].astype(F32) + self.far[r, :].astype(F32)).astype(BF16)
                self.back[i].start()

    def arrive(self, which):
        @pl.when(self.outer)
        def _():
            for i in which:
                self.back[i].wait_recv()

    def finish(self):
        @pl.when(self.outer)
        def _():
            for copy in self.first:
                copy.wait_send()

        @pl.when(self.inner)
        def _():
            for i in range(len(self.rows)):
                self.middle[i].wait_send()
                self.back[i].wait_send()


class Spread:
    def __init__(self, wires, slots, half):
        self.wires, self.slots, self.half = wires, slots, half
        self.chip = wires.own // 2
        self.x, self.y = lax.bitwise_xor(wires.own, 2), lax.bitwise_xor(wires.own, 4)
        self.cx, self.cy, self.cd = (lax.bitwise_xor(self.chip, m) for m in (1, 2, 3))
        self.a, self.b = pl.ds(0, half), pl.ds(half, half)

    def piece(self, chip, part):
        return self.slots.at[chip, part]

    def put(self, chip, part, peer):
        return self.wires.send(self.piece(chip, part), self.piece(chip, part), peer)

    def first_half(self):
        self.xa = self.put(self.chip, self.a, self.x)
        self.ya = self.put(self.chip, self.a, self.y)

    def second_half(self):
        self.yb = self.put(self.chip, self.b, self.y)
        self.xb = self.put(self.chip, self.b, self.x)

    def relay(self):
        self.xa.wait_recv()
        self.da = self.put(self.cx, self.a, self.y)
        self.yb.wait_recv()
        self.db = self.put(self.cy, self.b, self.x)

    def wait_sides(self):
        self.xb.wait_recv()
        self.ya.wait_recv()

    def wait_diagonal(self):
        self.da.wait_recv()
        self.db.wait_recv()


class Gather:
    def __init__(self, wires, part, side, last, half):
        self.wires, self.part, self.side, self.last, self.half = wires, part, side, last, half
        self.chip = wires.own // 2
        self.x, self.y = lax.bitwise_xor(wires.own, 2), lax.bitwise_xor(wires.own, 4)
        self.cx, self.cy, self.cd = (lax.bitwise_xor(self.chip, m) for m in (1, 2, 3))
        self.a, self.b = pl.ds(0, half), pl.ds(half, half)

    def send_x(self):
        self.x_own = self.wires.send(self.part.at[self.cx, self.a], self.side.at[0], self.x)

    def send_y(self):
        self.y_own = self.wires.send(self.part.at[self.cy, self.b], self.side.at[1], self.y)

    def send_diagonal(self):
        self.x_far = self.wires.send(self.part.at[self.cd, self.a], self.side.at[2], self.x)
        self.y_far = self.wires.send(self.part.at[self.cd, self.b], self.side.at[3], self.y)

    def relay(self):
        step = 32

        def add(chip, start, slot):
            @pl.loop(0, self.half // step)
            def _(t):
                rows = pl.ds(pl.multiple_of(start + t * step, step), step)
                near = self.part[chip, rows, :].astype(F32) + self.side[slot, rows_of(t, step), :].astype(F32)
                self.part[chip, rows, :] = near.astype(BF16)

        self.x_far.wait_recv()
        add(self.cy, 0, 2)
        self.y_last = self.wires.send(self.part.at[self.cy, self.a], self.last.at[0], self.y)
        self.y_far.wait_recv()
        add(self.cx, self.half, 3)
        self.x_last = self.wires.send(self.part.at[self.cx, self.b], self.last.at[1], self.x)

    def wait_first(self):
        self.x_own.wait_recv()
        self.y_last.wait_recv()

    def wait_second(self):
        self.y_own.wait_recv()
        self.x_last.wait_recv()

    def total(self, which, offset, size):
        rows = pl.ds(pl.multiple_of(which * self.half + offset, size), size)
        here = pl.ds(pl.multiple_of(offset, size), size)
        return self.part[self.chip, rows, :].astype(F32) + self.side[which, here, :].astype(F32) + self.last[which, here, :].astype(F32)


def middle_body(
    grad_scale, heads, x, cot, upout, down_w, proj_bias, hidden_bias, gain, shift,
    output, branch_grad, grad_heads, vec, down_grad, keep, to_x, to_y, to_d,
    att, out_full, up_full, down_full, h1, z1, r1, gs, fl, act, slope, part, side, last, sl, pre, part2, side2, last2,
    branch_low, agl, acc, d_send, d_recv, d_keep, d_own, d_land, d_far, u_send, u_recv, u_keep, o_send, o_recv, o_keep,
    send_sems, recv_sems, local_sems,
):
    w = Wires(send_sems, recv_sems, local_sems)
    own = w.own
    core, chip = lax.rem(own, 2), own // 2
    mate = lax.bitwise_xor(own, 1)
    cx, cy, cd = (lax.bitwise_xor(chip, m) for m in (1, 2, 3))
    toks, width = x.shape
    ff = up_full.shape[1]
    head_width = heads.shape[1]
    half = toks // 2
    piece = upout.shape[2]
    tile = 256
    w.greet([(w.rep, lax.bitwise_xor(own, m)) for m in range(1, 8)] + [(lax.bitwise_xor(w.rep, m), own) for m in (1, 3)])

    swaps = []
    for m in (6, 2, 4, 1, 3, 5, 7):
        peer = lax.bitwise_xor(own, m)
        swaps.append(w.send(heads.at[rows_of(peer, toks)], att.at[:, rows_of(own, head_width)], peer))
    weights = []
    for k in range(4):
        dst = rows_of(2 * k + core, piece)
        for s, full in ((upout.at[k, 1], out_full), (upout.at[k, 0], up_full)):
            weights.append((w.local(s, full.at[dst]), w.send(s, full.at[dst], mate)))
    dst = rows_of(core, ff // 2)
    weights.append((w.local(down_w, down_full.at[dst]), w.send(down_w, down_full.at[dst], mate)))
    att[:, rows_of(own, head_width)] = heads[rows_of(own, toks), :]
    for copy in swaps:
        copy.wait_recv()
    for here, there in weights:
        here.wait()
        there.wait_recv()

    @pl.loop(0, width // tile)
    def _(n):
        cols = rows_of(n, tile)
        h1[:, cols] = nn(att[...], out_full[:, cols]) + proj_bias[2:3, cols] + x[:, cols].astype(F32)

    step = 32
    acc[...] = jnp.zeros_like(acc)

    def first_rows(t):
        rows = rows_of(t, step)
        v = h1[rows, :]
        center = v - jnp.mean(v, axis=1, keepdims=True)
        inv = lax.rsqrt(jnp.mean(center * center, axis=1, keepdims=True) + 1e-05)
        z = center * inv
        z1[rows, :] = z
        r1[rows, :] = jnp.broadcast_to(inv, (step, 128))
        fl[chip, rows, :] = (z * gain[0:1, :] + shift[0:1, :]).astype(BF16)

    spread = Spread(w, fl, half)
    pl.loop(0, half // step)(first_rows)
    spread.first_half()
    pl.loop(half // step, toks // step)(first_rows)
    spread.second_half()

    def forward(k):
        @pl.loop(0, ff // tile)
        def _(n):
            cols = rows_of(n, tile)
            hidden = nn(fl[k], up_full[:, cols]) + hidden_bias[:, pl.ds(pl.multiple_of(chip * ff + n * tile, tile), tile)]
            slope[k, :, cols] = hidden
            act[k, :, cols] = (hidden * (0.5 * (1.0 + lax.erf(hidden * (2.0**-0.5))))).astype(BF16)

        @pl.loop(0, width // tile)
        def _(n):
            cols = rows_of(n, tile)
            part[k, :, cols] = nn(act[k], down_full[:, cols]).astype(BF16)

    forward(chip)
    gather = Gather(w, part, side, last, half)
    spread.relay()
    spread.wait_sides()
    forward(cx)
    gather.send_x()
    forward(cy)
    gather.send_y()
    spread.wait_diagonal()
    forward(cd)
    gather.send_diagonal()

    def slopes(k):
        @pl.loop(0, toks // 32)
        def _(t):
            rows = rows_of(t, 32)
            hidden = slope[k, rows, :]
            cdf = 0.5 * (1.0 + lax.erf(hidden * (2.0**-0.5)))
            slope[k, rows, :] = cdf + hidden * (jnp.exp(-0.5 * hidden * hidden) * ((2.0 * math.pi) ** -0.5))

    slopes(0)
    slopes(1)
    gather.relay()
    slopes(2)
    slopes(3)

    def second_rows(which, t):
        rows = pl.ds(pl.multiple_of(which * half + t * step, step), step)
        v = z1[rows, :] * gain[0:1, :] + shift[0:1, :] + gather.total(which, t * step, step) + proj_bias[3:4, :]
        center = v - jnp.mean(v, axis=1, keepdims=True)
        inv = lax.rsqrt(jnp.mean(center * center, axis=1, keepdims=True) + 1e-05)
        z = center * inv
        output[rows, :] = (z * gain[1:2, :] + shift[1:2, :]).astype(BF16)
        c = cot[rows, :].astype(F32)
        e = c * gain[1:2, :]
        grad = inv * (e - jnp.mean(e, axis=1, keepdims=True) - z * jnp.mean(e * z, axis=1, keepdims=True))
        gs[rows, :] = grad
        low = grad.astype(BF16)
        sl[chip, rows, :] = low
        acc[0] += fold_rows(c * z)
        acc[1] += fold_rows(c)
        acc[2] += fold_rows(low.astype(F32))

    spread2 = Spread(w, sl, half)
    gather.wait_first()
    pl.loop(0, half // step)(functools.partial(second_rows, 0))
    spread2.first_half()
    gather.wait_second()
    pl.loop(0, half // step)(functools.partial(second_rows, 1))
    spread2.second_half()

    def backward(k):
        @pl.loop(0, ff // tile)
        def _(n):
            cols = rows_of(n, tile)
            grad = nt(sl[k], down_full[cols, :]) * slope[k, :, cols]
            low = grad.astype(BF16)
            pre[k, :, cols] = low
            acc[3, :, cols] += fold_rows(low.astype(F32))

        @pl.loop(0, width // tile)
        def _(n):
            cols = rows_of(n, tile)
            part2[k, :, cols] = nt(pre[k], up_full[cols, :]).astype(BF16)

    backward(chip)
    gather2 = Gather(w, part2, side2, last2, half)
    spread2.relay()
    spread2.wait_sides()
    backward(cx)
    gather2.send_x()
    backward(cy)
    gather2.send_y()
    spread2.wait_diagonal()
    backward(cd)
    gather2.send_diagonal()

    def down_rows(which, n):
        cols = pl.ds(pl.multiple_of(which * (ff // 2) + n * tile, tile), tile)
        lhs = act[:, :, cols].reshape(4 * toks, tile)
        return tn(lhs, sl[...].reshape(4 * toks, width))

    @pl.loop(0, ff // 2 // tile)
    def _(n):
        d_send[rows_of(n, tile), :] = down_rows(1 - core, n).astype(BF16)

    d_copy = w.send(d_send, d_recv, mate)

    @pl.loop(0, ff // 2 // tile)
    def _(n):
        d_keep[rows_of(n, tile), :] = down_rows(core, n)

    gather2.relay()
    d_copy.wait_recv()

    @pl.loop(0, ff // 2 // 64)
    def _(t):
        rows = rows_of(t, 64)
        d_own[rows, :] = (d_keep[rows, :] + d_recv[rows, :].astype(F32)).astype(BF16)

    line = Line(w, d_own, d_land, d_far, 8)
    line.start()

    def up_rows(which, k):
        cols = pl.ds(pl.multiple_of((2 * k + which) * piece, piece), piece)
        lhs = fl[:, :, cols].reshape(4 * toks, piece)
        return tn(lhs, pre[...].reshape(4 * toks, ff))

    @pl.loop(0, 4)
    def _(k):
        u_send[k] = up_rows(1 - core, k).astype(BF16)

    u_copy = w.send(u_send, u_recv, mate)

    def branch_rows(which, t):
        rows = pl.ds(pl.multiple_of(which * half + t * step, step), step)
        grad = gs[rows, :] + gather2.total(which, t * step, step)
        z = z1[rows, :]
        e = grad * gain[0:1, :]
        out = r1[rows, 0:1] * (e - jnp.mean(e, axis=1, keepdims=True) - z * jnp.mean(e * z, axis=1, keepdims=True))
        branch_grad[rows, :] = out
        low = out.astype(BF16)
        branch_low[rows, :] = low
        acc[4] += fold_rows(grad * z)
        acc[5] += fold_rows(grad)
        acc[6] += fold_rows(low.astype(F32))

    gather2.wait_first()
    pl.loop(0, half // step)(functools.partial(branch_rows, 0))
    line.collect((0, 1))
    gather2.wait_second()
    pl.loop(0, half // step)(functools.partial(branch_rows, 1))

    @pl.loop(0, width // tile)
    def _(n):
        cols = rows_of(n, tile)
        agl[:, cols] = nt(branch_low[...], out_full[cols, :]).astype(BF16)

    backs = []
    for m in (6, 2, 4, 1, 3, 5, 7):
        peer = lax.bitwise_xor(own, m)
        backs.append(w.send(agl.at[:, rows_of(peer, head_width)], grad_heads.at[rows_of(own, toks)], peer))
    grad_heads[rows_of(own, toks), :] = agl[:, rows_of(own, head_width)]
    line.collect((2, 3))
    line.total((0, 1))

    def out_rows(which, k):
        cols = pl.ds(pl.multiple_of((2 * k + which) * piece, piece), piece)
        return tn(att[:, cols], branch_low[...])

    @pl.loop(0, 4)
    def _(k):
        o_send[k] = out_rows(1 - core, k).astype(BF16)

    o_copy = w.send(o_send, o_recv, mate)
    line.collect((4,))
    line.total((2,))

    @pl.loop(0, 4)
    def _(k):
        u_keep[k] = up_rows(core, k)
        o_keep[k] = out_rows(core, k)

    line.collect((5,))
    line.total((3,))
    u_copy.wait_recv()
    o_copy.wait_recv()
    for m, ref in enumerate((keep, to_x, to_y, to_d)):
        k = lax.bitwise_xor(chip, m)
        ref[0] = (u_keep[k] + u_recv[k].astype(F32)).astype(BF16)
        ref[1] = (o_keep[k] + o_recv[k].astype(F32)).astype(BF16)
    line.collect((6, 7))
    line.total((4, 5, 6, 7))
    vec[...] = jnp.zeros_like(vec)
    for row, slot in ((2, 6), (3, 2), (4, 4), (5, 0), (6, 5), (7, 1)):
        vec[row : row + 1, :] = jnp.sum(acc[slot], axis=0, keepdims=True)
    hidden_sum = jnp.sum(acc[3], axis=0, keepdims=True)
    for k in range(4):
        vec[8 + k : 9 + k, :] = jnp.where(chip == k, hidden_sum, jnp.zeros_like(hidden_sum))
    for copy in backs:
        copy.wait_recv()
    for i in range(8):
        line.arrive((i,))
        rows = line.rows[i]
        down_grad[rows, :] = d_land[rows, :].astype(F32) * grad_scale
    line.finish()
    w.finish()


def middle(grad_scale, heads, x, cot, upout, down_w, proj_bias, hidden_bias, gain, shift):
    toks, width = x.shape
    piece = upout.shape[2]
    ff = 2 * down_w.shape[0]
    half = toks // 2
    shape = jax.ShapeDtypeStruct
    vm = pltpu.VMEM
    return pl.pallas_call(
        functools.partial(middle_body, grad_scale),
        name="middle",
        out_shape=(
            shape((toks, width), BF16),
            shape((toks, width), F32),
            shape(heads.shape, BF16),
            shape((16, width), F32),
            shape((ff // 2, width), F32),
        )
        + (shape((2, piece, width), BF16),) * 4,
        in_specs=[VM, VM, VM, HBM, HBM] + [VM] * 4,
        out_specs=(VM,) * 9,
        scratch_shapes=[
            vm((toks, width), BF16), vm((width, width), BF16), vm((width, ff), BF16), vm((ff, width), BF16),
            vm((toks, width), F32), vm((toks, width), F32), vm((toks, 128), F32), vm((toks, width), F32),
            vm((4, toks, width), BF16), vm((4, toks, ff), BF16), vm((4, toks, ff), F32),
            vm((4, toks, width), BF16), vm((4, half, width), BF16), vm((2, half, width), BF16),
            vm((4, toks, width), BF16), vm((4, toks, ff), BF16),
            vm((4, toks, width), BF16), vm((4, half, width), BF16), vm((2, half, width), BF16),
            vm((toks, width), BF16), vm((toks, width), BF16), vm((8, 8, width), F32),
            vm((ff // 2, width), BF16), vm((ff // 2, width), BF16), vm((ff // 2, width), F32),
            vm((ff // 2, width), BF16), vm((ff // 2, width), BF16), vm((ff // 2, width), BF16),
            vm((4, piece, ff), BF16), vm((4, piece, ff), BF16), vm((4, piece, ff), F32),
            vm((4, piece, width), BF16), vm((4, piece, width), BF16), vm((4, piece, width), F32),
            pltpu.SemaphoreType.DMA((96,)), pltpu.SemaphoreType.DMA((96,)), pltpu.SemaphoreType.DMA((16,)),
        ],
        compiler_params=pltpu.CompilerParams(collective_id=1, has_side_effects=True, vmem_limit_bytes=60 << 20),
    )(heads, x, cot, upout, down_w, proj_bias, hidden_bias, gain, shift)


def project_body(x, qkv_w, up_w, out_w, proj_bias, q_out, k_out, v_out, xs, w_full, upout, stage, send_sems, recv_sems, local_sems):
    w = Wires(send_sems, recv_sems, local_sems)
    own = w.own
    core, chip = lax.rem(own, 2), own // 2
    mate = lax.bitwise_xor(own, 1)
    toks, width = x.shape
    piece = qkv_w.shape[0]
    share = width // 4
    head_width = share // 2
    rep = w.rep
    reps = 4
    w.greet([(rep, lax.bitwise_xor(own, m)) for m in (1, 2, 4, 6)] + [(lax.rem(rep + 1, reps), own), (lax.rem(rep + reps - 1, reps), own)])
    mine = rows_of(own, piece)
    quarter = piece // reps

    def source(part, to_chip):
        return qkv_w.at[:, pl.ds(pl.multiple_of(part * width + to_chip * share, share), share)]

    arrivals = []
    for m in (6, 2, 4):
        peer = lax.bitwise_xor(own, m)
        copies = [w.send(source(p, lax.bitwise_xor(chip, m // 2)), w_full.at[mine, pl.ds(p * share, share)], peer) for p in range(3)]
        arrivals.append((peer, copies))
    fetched = []
    for m in (6, 2, 4):
        peer, to_chip = lax.bitwise_xor(own, m), lax.bitwise_xor(chip, m // 2)
        some = rows_of(rep, quarter)
        fetched.append(w.send(up_w.at[some, rows_of(to_chip, width)], upout.at[chip, 0, some], peer))
        fetched.append(w.send(out_w.at[some], upout.at[chip, 1, some], peer))
    kept = [w.local(up_w.at[:, rows_of(chip, width)], upout.at[chip, 0]), w.local(out_w, upout.at[chip, 1])]
    others = [lax.bitwise_xor(chip, m) for m in (3, 1, 2)]
    hops = []
    for hop in range(1, reps):
        for step in (1, -1):
            index = rep - step * (hop - 1)
            to = rep + step
            going = jnp.logical_and(jnp.logical_and(index >= 0, index < reps), jnp.logical_and(to >= 0, to < reps))
            come = rep - step * hop
            coming = jnp.logical_and(come >= 0, come < reps)
            some = rows_of(jnp.clip(index, 0, reps - 1), quarter)
            copies = [w.remote(upout.at[c, :, some], upout.at[c, :, some], own, jnp.clip(to, 0, reps - 1)) for c in others]
            hops.append((hop, going, coming, copies))

    def hop_start(which):
        for hop, going, coming, copies in hops:
            if hop == which:

                @pl.when(going)
                def _():
                    for copy in copies:
                        copy.start()

    def hop_wait(which):
        for hop, going, coming, copies in hops:
            if hop == which:

                @pl.when(coming)
                def _():
                    for copy in copies:
                        copy.wait_recv()

    xs[chip] = x[...]
    spread = Spread(w, xs, toks // 2)
    spread.first_half()
    spread.second_half()
    here = [w.local(source(p, chip), w_full.at[mine, pl.ds(p * share, share)]) for p in range(3)]
    theirs = [w.send(source(p, chip), w_full.at[mine, pl.ds(p * share, share)], mate) for p in range(3)]
    for peer, copies in arrivals:
        for copy in copies:
            copy.wait_recv()
        rows = rows_of(peer, piece)
        theirs.append(w.send(w_full.at[rows], w_full.at[rows], mate))
    for copy in here:
        copy.wait()
    for copy in theirs:
        copy.wait_recv()
    outs = (q_out, k_out, v_out)
    swaps = []

    def block(k):
        rows = rows_of(2 * k + core, toks)
        for p in range(3):
            r = nn(xs[k], w_full[:, pl.ds(p * share, share)])
            if p != 1:
                r = r + proj_bias[p // 2 : p // 2 + 1, rows_of(chip, share)]
            stage[k, :, pl.ds(p * share, share)] = r.astype(BF16)
            swaps.append(w.send(stage.at[k, :, pl.ds(pl.multiple_of(p * share + (1 - core) * head_width, head_width), head_width)], outs[p].at[rows], mate))
            outs[p][rows, :] = stage[k, :, pl.ds(pl.multiple_of(p * share + core * head_width, head_width), head_width)]

    for copy in fetched:
        copy.wait_recv()
    hop_start(1)
    block(chip)
    spread.relay()
    hop_wait(1)
    hop_start(2)
    spread.wait_sides()
    block(spread.cx)
    block(spread.cy)
    hop_wait(2)
    hop_start(3)
    spread.wait_diagonal()
    block(spread.cd)
    for copy in swaps:
        copy.wait_recv()
    hop_wait(3)
    for copy in kept:
        copy.wait()
    for hop, going, coming, copies in hops:

        @pl.when(going)
        def _():
            for copy in copies:
                copy.wait_send()

    w.finish()


def project(x, qkv_w, up_w, out_w, proj_bias):
    toks, width = x.shape
    piece = qkv_w.shape[0]
    shape = jax.ShapeDtypeStruct
    vm = pltpu.VMEM
    heads = shape((8 * toks, width // 8), BF16)
    return pl.pallas_call(
        project_body,
        name="project",
        out_shape=(heads, heads, heads, shape((4, toks, width), BF16), shape((8 * piece, 3 * width // 4), BF16), shape((4, 2, piece, width), BF16)),
        in_specs=[VM, VM, HBM, HBM, VM],
        out_specs=(VM,) * 5 + (HBM,),
        scratch_shapes=[
            vm((4, toks, 3 * width // 4), BF16),
            pltpu.SemaphoreType.DMA((72,)), pltpu.SemaphoreType.DMA((72,)), pltpu.SemaphoreType.DMA((8,)),
        ],
        compiler_params=pltpu.CompilerParams(collective_id=0, has_side_effects=True, vmem_limit_bytes=40 << 20),
    )(x, qkv_w, up_w, out_w, proj_bias)


CHUNKS = 8


def finish_body(
    grad_scale, dq, dk, dv, xs, w_full, branch_grad, vec, keep, got_x, got_y, got_d,
    input_grad, qkv_total, out_total, up_total, bias_total, hidden_total, gain_total, shift_total,
    grads, part, side, last, q_send, q_recv, q_keep, q_piece, z_own, z_in, z_far, y_own, y_in, y_far, v_sum, v_recv,
    send_sems, recv_sems, local_sems,
):
    w = Wires(send_sems, recv_sems, local_sems)
    own, rep = w.own, w.rep
    core, chip = lax.rem(own, 2), own // 2
    mate = lax.bitwise_xor(own, 1)
    toks, width = branch_grad.shape
    share = width // 4
    head_width = share // 2
    piece = q_keep.shape[1]
    half = toks // 2
    tile = 256
    z1, z2, z3 = (lax.bitwise_xor(rep, m) for m in (1, 2, 3))
    w.greet([(rep, lax.bitwise_xor(own, m)) for m in (1, 2, 4, 6)] + [(z1, own), (z2, own), (z3, own)])

    for m, ref in enumerate((keep, got_x, got_y, got_d)):
        y_own[m * piece : (m + 1) * piece, :] = ref[0]
    y_own[4 * piece :, :] = (keep[1].astype(F32) + got_x[1].astype(F32) + got_y[1].astype(F32) + got_d[1].astype(F32)).astype(BF16)
    early = Line(w, y_own, y_in, y_far, 10)
    early.start()
    swaps = []
    for p, g in enumerate((dq, dk, dv)):
        cols = pl.ds(pl.multiple_of(p * share + core * head_width, head_width), head_width)
        swaps.append(w.send(g.at[1 - core], grads.at[:, :, cols], mate))
        grads[:, :, cols] = g[core]
    v_sum[...] = vec[...]
    for row, g in ((0, dq), (1, dv)):
        total = jnp.sum(g[...].reshape(8 * toks, head_width).astype(F32), axis=0, keepdims=True)
        v_sum[row : row + 1, rows_of(own, head_width)] = total
    rounds = [(None, mate), (None, lax.bitwise_xor(own, 2)), (None, lax.bitwise_xor(own, 4)), (z1, own), (z2, own)]
    flying = []

    def vec_start(i):
        copy = w.remote(v_sum.at[...] if i == 0 else v_recv.at[4 + i], v_recv.at[i], rounds[i][1], rounds[i][0])
        copy.start()
        w.sent.append(copy)
        flying.append(copy)

    def vec_step(i):
        flying[i].wait_recv()
        base = v_sum[...] if i == 0 else v_recv[4 + i]
        if i < 4:
            v_recv[5 + i] = base + v_recv[i]
            vec_start(i + 1)
        else:
            final = (base + v_recv[i]) * grad_scale
            bias_total[...] = final[0:4]
            gain_total[...] = final[4:6]
            shift_total[...] = final[6:8]
            for k in range(4):
                hidden_total[:, k * width : (k + 1) * width] = final[8 + k : 9 + k]

    vec_start(0)
    for copy in swaps:
        copy.wait_recv()

    def qkv_rows(which, k):
        cols = pl.ds(pl.multiple_of((2 * k + which) * piece, piece), piece)
        return tn(xs[:, :, cols].reshape(4 * toks, piece), grads[...].reshape(4 * toks, 3 * share))

    @pl.loop(0, 4)
    def _(k):
        q_send[k] = qkv_rows(1 - core, k).astype(BF16)

    q_copy = w.send(q_send, q_recv, mate)
    early.collect((0,))

    @pl.loop(0, 4)
    def _(k):
        q_keep[k] = qkv_rows(core, k)

    early.collect((1,))
    q_copy.wait_recv()

    @pl.loop(0, 4)
    def _(k):
        q_piece[k] = (q_keep[k] + q_recv[k].astype(F32)).astype(BF16)

    moved = []
    for m in (6, 2, 4):
        peer = lax.bitwise_xor(own, m)
        for p in range(3):
            dst = z_own.at[:, pl.ds(pl.multiple_of(p * width + chip * share, share), share)]
            moved.append(w.send(q_piece.at[lax.bitwise_xor(chip, m // 2), :, pl.ds(p * share, share)], dst, peer))
    for p in range(3):
        z_own[:, pl.ds(pl.multiple_of(p * width + chip * share, share), share)] = q_piece[chip, :, pl.ds(p * share, share)]
    vec_step(0)

    def partial(k):
        @pl.loop(0, width // tile)
        def _(n):
            cols = rows_of(n, tile)
            part[k, :, cols] = nt(grads[k], w_full[cols, :]).astype(BF16)

    gather = Gather(w, part, side, last, half)
    partial(gather.cd)
    gather.send_diagonal()
    early.collect((2,))
    early.total((0,))
    partial(gather.cx)
    gather.send_x()
    partial(gather.cy)
    gather.send_y()
    early.collect((3,))
    early.total((1,))
    partial(chip)
    vec_step(1)
    for copy in moved:
        copy.wait_recv()
    late = Line(w, z_own, z_in, z_far, CHUNKS)
    late.start()
    early.collect((4,))
    early.total((2,))
    gather.relay()
    vec_step(2)
    early.collect((5, 6))
    early.total((3, 4))
    step = 32

    def final_rows(which, t):
        rows = pl.ds(pl.multiple_of(which * half + t * step, step), step)
        input_grad[rows, :] = (branch_grad[rows, :] + gather.total(which, t * step, step)).astype(BF16)

    gather.wait_first()
    pl.loop(0, half // step)(functools.partial(final_rows, 0))
    vec_step(3)
    early.collect((7,))
    early.total((5,))
    gather.wait_second()
    pl.loop(0, half // step)(functools.partial(final_rows, 1))
    vec_step(4)
    early.collect((8, 9))
    early.total((6, 7))
    late.collect((0,))
    early.total((8,))
    late.collect((1,))
    early.total((9,))
    for i in range(2, CHUNKS):
        late.collect((i,))
        late.total((i - 2,))
    late.total((CHUNKS - 2, CHUNKS - 1))
    for m in range(4):
        for i in (2 * m, 2 * m + 1):
            early.arrive((i,))
        up_total[:, rows_of(lax.bitwise_xor(chip, m), width)] = y_in[m * piece : (m + 1) * piece, :].astype(F32) * grad_scale
    early.arrive((8, 9))
    out_total[...] = y_in[4 * piece :, :].astype(F32) * grad_scale
    for i in range(CHUNKS):
        late.arrive((i,))
        rows = late.rows[i]
        qkv_total[rows, :] = z_in[rows, :].astype(F32) * grad_scale
    early.finish()
    late.finish()
    w.finish()


def finish(grad_scale, dq, dk, dv, xs, w_full, branch_grad, vec, keep, got_x, got_y, got_d):
    toks, width = branch_grad.shape
    piece = w_full.shape[0] // 8
    half = toks // 2
    shape = jax.ShapeDtypeStruct
    vm = pltpu.VMEM
    line = vm((piece, 3 * width), BF16)
    five = vm((5 * piece, width), BF16)
    return pl.pallas_call(
        functools.partial(finish_body, grad_scale),
        name="finish",
        out_shape=(
            shape((toks, width), BF16), shape((piece, 3 * width), F32), shape((piece, width), F32), shape((piece, 4 * width), F32),
            shape((4, width), F32), shape((1, 4 * width), F32), shape((2, width), F32), shape((2, width), F32),
        ),
        in_specs=[VM] * 11,
        out_specs=(VM,) * 8,
        scratch_shapes=[
            vm((4, toks, 3 * width // 4), BF16),
            vm((4, toks, width), BF16), vm((4, half, width), BF16), vm((2, half, width), BF16),
            vm((4, piece, 3 * width // 4), BF16), vm((4, piece, 3 * width // 4), BF16), vm((4, piece, 3 * width // 4), F32),
            vm((4, piece, 3 * width // 4), BF16),
            line, line, line, five, five, five,
            vm(vec.shape, F32), vm((9,) + vec.shape, F32),
            pltpu.SemaphoreType.DMA((96,)), pltpu.SemaphoreType.DMA((96,)), pltpu.SemaphoreType.DMA((8,)),
        ],
        compiler_params=pltpu.CompilerParams(collective_id=2, has_side_effects=True, vmem_limit_bytes=48 << 20),
    )(dq, dk, dv, xs, w_full, branch_grad, vec, keep, got_x, got_y, got_d)


def local_tensor(tokens, segment_ids, qkv_weight, out_weight, up_weight, down_weight, proj_bias, hidden_bias, norm_gain, norm_shift, cotangent):
    inputs = tokens[0]
    toks, width = inputs.shape
    scale = (width // HEADS) ** (-0.5)
    grad_scale = (toks * lax.axis_size("fsdp") * lax.axis_size("rep")) ** (-0.5)
    queries, key_rows, value_rows, xs, w_full, upout = project(inputs, qkv_weight, up_weight, out_weight, proj_bias)
    attended, attended_low, lse = attn_fwd(scale, segment_ids, queries, key_rows, value_rows)
    output, branch_grad, grad_heads, vec, down_total, keep, to_x, to_y, to_d = middle(
        grad_scale, attended_low, inputs, cotangent[0], upout, down_weight, proj_bias, hidden_bias[None], norm_gain, norm_shift
    )
    got_x, got_y, got_d = (lax.ppermute(block, "fsdp", [(i, i ^ m) for i in range(8)]) for block, m in ((to_x, 2), (to_y, 4), (to_d, 6)))
    query_grad, key_grad, value_grad = attn_bwd(scale, segment_ids, queries, key_rows, value_rows, grad_heads, attended, lse)
    input_grad, qkv_total, out_total, up_total, bias_total, hidden_total, gain_total, shift_total = finish(
        grad_scale, query_grad, key_grad, value_grad, xs, w_full, branch_grad, vec, keep, got_x, got_y, got_d
    )
    return (
        output[None],
        input_grad[None],
        qkv_total,
        out_total,
        up_total,
        down_total,
        bias_total,
        hidden_total.reshape(4 * width),
        gain_total,
        shift_total,
    )


def normalize(hidden, gain, shift):
    center = hidden - jnp.mean(hidden, axis=-1, keepdims=True)
    spread = jnp.mean(center * center, axis=-1, keepdims=True)
    return center * lax.rsqrt(spread + 1e-05) * gain + shift


def exact_gelu(value):
    return jax.nn.gelu(value, approximate=False)


def gather_attention(qkv_weight, out_weight):
    return (
        lax.all_gather(qkv_weight, "fsdp", axis=0, tiled=True),
        lax.all_gather(out_weight, "fsdp", axis=0, tiled=True),
    )


def gather_feedforward(up_weight, down_weight):
    return (
        lax.all_gather(up_weight, "fsdp", axis=0, tiled=True),
        lax.all_gather(down_weight, "fsdp", axis=0, tiled=True),
    )


def block_plan(row_count):
    block_rows = math.gcd(row_count, 1024)
    return (block_rows, row_count // block_rows)


def split_heads(matrix):
    return matrix.reshape(matrix.shape[0], HEADS, matrix.shape[1] // HEADS)


def join_heads(stacked):
    return jnp.transpose(stacked, (1, 0, 2)).reshape(
        stacked.shape[1], stacked.shape[0] * stacked.shape[2]
    )


def local_gather(
    tokens,
    segment_ids,
    qkv_weight,
    out_weight,
    up_weight,
    down_weight,
    proj_bias,
    hidden_bias,
    norm_gain,
    norm_shift,
    cotangent,
):
    inputs = tokens[0]
    tok_count, model_width = inputs.shape
    head_dim = model_width // HEADS
    score_scale = head_dim ** (-0.5)
    doc_ids = segment_ids[0]
    own_index = lax.axis_index("fsdp")
    own_docs = lax.dynamic_slice_in_dim(doc_ids, own_index * tok_count, tok_count)
    qkv_full, out_full = gather_attention(qkv_weight, out_weight)
    projected = jnp.dot(inputs, qkv_full, preferred_element_type=jnp.float32)
    queries = (projected[:, :model_width] + proj_bias[0]).astype(jnp.bfloat16)
    key_rows = projected[:, model_width : 2 * model_width].astype(jnp.bfloat16)
    value_rows = (projected[:, 2 * model_width :] + proj_bias[1]).astype(jnp.bfloat16)
    query_heads = split_heads(queries)
    key_own = split_heads(key_rows)
    value_own = split_heads(value_rows)
    initial = (
        jnp.zeros((HEADS, tok_count, head_dim), jnp.float32),
        jnp.full((HEADS, tok_count), NEGATIVE, jnp.float32),
        jnp.zeros((HEADS, tok_count), jnp.float32),
    )
    key_piece = lax.all_gather(key_rows, "fsdp", axis=0, tiled=True)
    value_piece = lax.all_gather(value_rows, "fsdp", axis=0, tiled=True)
    block_rows, blocks = block_plan(key_piece.shape[0])

    def forward_advance(block_index, running_state):
        weighted, running, denominator = running_state
        offset = block_index * block_rows
        key_block = split_heads(lax.dynamic_slice_in_dim(key_piece, offset, block_rows))
        value_block = split_heads(lax.dynamic_slice_in_dim(value_piece, offset, block_rows))
        block_docs = lax.dynamic_slice_in_dim(doc_ids, offset, block_rows)
        scores = (
            jnp.einsum("qhd,khd->hqk", query_heads, key_block, preferred_element_type=jnp.float32)
            * score_scale
        )
        same_doc = (own_docs[:, None] == block_docs[None, :])[None]
        highest = jnp.maximum(running, jnp.max(jnp.where(same_doc, scores, NEGATIVE), axis=2))
        factor = jnp.exp(running - highest)
        weights = jnp.where(same_doc, jnp.exp(scores - highest[:, :, None]), 0.0)
        denominator = denominator * factor + jnp.sum(weights, axis=2)
        weighted = weighted * factor[:, :, None] + jnp.einsum(
            "hqk,khd->hqd",
            weights.astype(jnp.bfloat16),
            value_block,
            preferred_element_type=jnp.float32,
        )
        return (weighted, highest, denominator)

    weighted, running, denominator = lax.fori_loop(0, blocks, forward_advance, initial)
    attended_heads = weighted / denominator[:, :, None]
    log_total = running + jnp.log(denominator)
    attended_low = join_heads(attended_heads).astype(jnp.bfloat16)
    branch = jnp.dot(attended_low, out_full, preferred_element_type=jnp.float32) + proj_bias[2]
    first_norm, norm_one_back = jax.vjp(
        normalize, inputs.astype(jnp.float32) + branch, norm_gain[0], norm_shift[0]
    )
    first_low = first_norm.astype(jnp.bfloat16)
    up_full, down_full = gather_feedforward(up_weight, down_weight)
    hidden_pre = jnp.dot(first_low, up_full, preferred_element_type=jnp.float32) + hidden_bias
    activated, gelu_back = jax.vjp(exact_gelu, hidden_pre)
    activated_low = activated.astype(jnp.bfloat16)
    second = jnp.dot(activated_low, down_full, preferred_element_type=jnp.float32) + proj_bias[3]
    output, norm_two_back = jax.vjp(normalize, first_norm + second, norm_gain[1], norm_shift[1])
    up_back, down_back = gather_feedforward(up_weight, down_weight)
    qkv_back, out_back = gather_attention(qkv_weight, out_weight)
    grad_second, gain_two, shift_two = norm_two_back(cotangent[0].astype(jnp.float32))
    second_low = grad_second.astype(jnp.bfloat16)
    down_term = jnp.einsum(
        "tf,td->fd", activated_low, second_low, preferred_element_type=jnp.float32
    )
    activated_grad = jnp.einsum(
        "td,fd->tf", second_low, down_back, preferred_element_type=jnp.float32
    )
    (pre_grad,) = gelu_back(activated_grad)
    pre_low = pre_grad.astype(jnp.bfloat16)
    up_term = jnp.einsum("td,tf->df", first_low, pre_low, preferred_element_type=jnp.float32)
    first_grad = grad_second + jnp.einsum(
        "tf,df->td", pre_low, up_back, preferred_element_type=jnp.float32
    )
    branch_grad, gain_one, shift_one = norm_one_back(first_grad)
    branch_low = branch_grad.astype(jnp.bfloat16)
    out_term = jnp.einsum("te,td->ed", attended_low, branch_low, preferred_element_type=jnp.float32)
    attended_grad = jnp.einsum(
        "td,ed->te", branch_low, out_back, preferred_element_type=jnp.float32
    ).astype(jnp.bfloat16)
    grad_heads = split_heads(attended_grad)
    correction = jnp.einsum("qhd,hqd->hq", grad_heads.astype(jnp.float32), attended_heads)
    lse_all, correction_all = (
        lax.all_gather(log_total, "fsdp", axis=1, tiled=True),
        lax.all_gather(correction, "fsdp", axis=1, tiled=True),
    )
    query_key_piece = lax.all_gather(key_rows, "fsdp", axis=0, tiled=True)
    query_value_piece = lax.all_gather(value_rows, "fsdp", axis=0, tiled=True)
    query_block_rows, blocks = block_plan(query_key_piece.shape[0])

    def query_advance(block_index, query_state):
        offset = block_index * query_block_rows
        key_block = split_heads(lax.dynamic_slice_in_dim(query_key_piece, offset, query_block_rows))
        value_block = split_heads(
            lax.dynamic_slice_in_dim(query_value_piece, offset, query_block_rows)
        )
        block_docs = lax.dynamic_slice_in_dim(doc_ids, offset, query_block_rows)
        scores = (
            jnp.einsum("qhd,khd->hqk", query_heads, key_block, preferred_element_type=jnp.float32)
            * score_scale
        )
        same_doc = (own_docs[:, None] == block_docs[None, :])[None]
        probabilities = jnp.where(same_doc, jnp.exp(scores - log_total[:, :, None]), 0.0)
        prob_grad = jnp.einsum(
            "qhd,khd->hqk", grad_heads, value_block, preferred_element_type=jnp.float32
        )
        score_grad = (probabilities * (prob_grad - correction[:, :, None])).astype(jnp.bfloat16)
        return query_state + jnp.einsum(
            "hqk,khd->hqd", score_grad, key_block, preferred_element_type=jnp.float32
        )

    query_acc = lax.fori_loop(
        0, blocks, query_advance, jnp.zeros((HEADS, tok_count, head_dim), jnp.float32)
    )
    query_grad = (join_heads(query_acc) * score_scale).astype(jnp.bfloat16)
    empty_heads = jnp.zeros((HEADS, tok_count, head_dim), jnp.float32)
    query_piece = lax.all_gather(queries, "fsdp", axis=0, tiled=True)
    grad_piece = lax.all_gather(attended_grad, "fsdp", axis=0, tiled=True)
    key_block_rows, blocks = block_plan(query_piece.shape[0])

    def key_advance(block_index, key_state):
        key_acc, value_acc = key_state
        offset = block_index * key_block_rows
        query_block = split_heads(lax.dynamic_slice_in_dim(query_piece, offset, key_block_rows))
        grad_block = split_heads(lax.dynamic_slice_in_dim(grad_piece, offset, key_block_rows))
        block_docs = lax.dynamic_slice_in_dim(doc_ids, offset, key_block_rows)
        lse_block = lax.dynamic_slice_in_dim(lse_all, offset, key_block_rows, axis=1)
        corr_block = lax.dynamic_slice_in_dim(correction_all, offset, key_block_rows, axis=1)
        scores = (
            jnp.einsum("qhd,khd->hqk", query_block, key_own, preferred_element_type=jnp.float32)
            * score_scale
        )
        same_doc = (block_docs[:, None] == own_docs[None, :])[None]
        probabilities = jnp.where(same_doc, jnp.exp(scores - lse_block[:, :, None]), 0.0)
        value_acc = value_acc + jnp.einsum(
            "hqk,qhd->hkd",
            probabilities.astype(jnp.bfloat16),
            grad_block,
            preferred_element_type=jnp.float32,
        )
        prob_grad = jnp.einsum(
            "qhd,khd->hqk", grad_block, value_own, preferred_element_type=jnp.float32
        )
        score_grad = (probabilities * (prob_grad - corr_block[:, :, None])).astype(jnp.bfloat16)
        key_acc = key_acc + jnp.einsum(
            "hqk,qhd->hkd", score_grad, query_block, preferred_element_type=jnp.float32
        )
        return (key_acc, value_acc)

    key_acc, value_acc = lax.fori_loop(0, blocks, key_advance, (empty_heads, empty_heads))
    key_grad = (join_heads(key_acc) * score_scale).astype(jnp.bfloat16)
    value_grad = join_heads(value_acc).astype(jnp.bfloat16)
    qkv_grad_low = jnp.concatenate([query_grad, key_grad, value_grad], axis=1)
    qkv_term = jnp.einsum("td,te->de", inputs, qkv_grad_low, preferred_element_type=jnp.float32)
    input_grad = branch_grad + jnp.einsum(
        "te,de->td", qkv_grad_low, qkv_back, preferred_element_type=jnp.float32
    )
    bias_term = jnp.stack(
        [
            jnp.sum(query_grad.astype(jnp.float32), axis=0),
            jnp.sum(value_grad.astype(jnp.float32), axis=0),
            jnp.sum(branch_low.astype(jnp.float32), axis=0),
            jnp.sum(second_low.astype(jnp.float32), axis=0),
        ]
    )
    hidden_term = jnp.sum(pre_low.astype(jnp.float32), axis=0)
    gain_term = jnp.stack([gain_one, gain_two])
    shift_term = jnp.stack([shift_one, shift_two])
    bias_total, hidden_total, gain_total, shift_total = lax.psum(
        (bias_term, hidden_term, gain_term, shift_term), ("rep", "fsdp")
    )
    up_sum, down_sum = (
        lax.psum_scatter(up_term, "fsdp", scatter_dimension=0, tiled=True),
        lax.psum_scatter(down_term, "fsdp", scatter_dimension=0, tiled=True),
    )
    qkv_sum, out_sum = (
        lax.psum_scatter(qkv_term, "fsdp", scatter_dimension=0, tiled=True),
        lax.psum_scatter(out_term, "fsdp", scatter_dimension=0, tiled=True),
    )
    qkv_total, out_total, up_total, down_total = lax.psum(
        (qkv_sum, out_sum, up_sum, down_sum), "rep"
    )
    grad_scale = (tok_count * lax.axis_size("fsdp") * lax.axis_size("rep")) ** (-0.5)
    return (
        output.astype(jnp.bfloat16)[None],
        input_grad.astype(jnp.bfloat16)[None],
        qkv_total * grad_scale,
        out_total * grad_scale,
        up_total * grad_scale,
        down_total * grad_scale,
        bias_total * grad_scale,
        hidden_total * grad_scale,
        gain_total * grad_scale,
        shift_total * grad_scale,
    )


def solution(mesh):
    small = mesh.shape["fsdp"] == 8 and mesh.shape["rep"] == 4
    local = local_tensor if small else local_gather
    return jax.shard_map(
        local,
        mesh=mesh,
        in_specs=(
            P("rep", "fsdp", None),
            P("rep", None),
            P("fsdp", None),
            P("fsdp", None),
            P("fsdp", None),
            P("fsdp", None),
            P(),
            P(),
            P(),
            P(),
            P("rep", "fsdp", None),
        ),
        out_specs=(
            P("rep", "fsdp", None),
            P("rep", "fsdp", None),
            P("fsdp", None),
            P("fsdp", None),
            P("fsdp", None),
            P("fsdp", None),
            P(),
            P(),
            P(),
            P(),
        ),
        check_vma=False,
    )
```

```python
import functools
import math

import jax
import jax.numpy as jnp
from jax import lax
from jax.experimental import pallas as pl
from jax.experimental.pallas import tpu as pltpu
from jax.sharding import PartitionSpec as P

HEADS = 16

NEGATIVE = -1e30
BQ = 256
BK = 512
VM = pl.BlockSpec(memory_space=pltpu.VMEM)
SM = pl.BlockSpec(memory_space=pltpu.SMEM)


def nt(a, b):
    return lax.dot_general(a, b, (((1,), (1,)), ((), ())), preferred_element_type=jnp.float32)


def nn(a, b):
    return jnp.dot(a, b, preferred_element_type=jnp.float32)


def block_range(seg_s, start, size, blk, n):
    first = seg_s[0, start]
    last = seg_s[0, start + size - 1]
    lo = jnp.int32(0)
    hi = jnp.int32(0)
    for j in range(n):
        lo = lo + (seg_s[0, j * blk + blk - 1] < first).astype(jnp.int32)
        hi = hi + (seg_s[0, j * blk] <= last).astype(jnp.int32)
    return lo, hi


def head_lanes(shape, half):
    return lax.broadcasted_iota(jnp.int32, shape, 1) < half


def rows_of(index, size):
    return pl.ds(pl.multiple_of(index * size, size), size)


def seg_columns(seg_v, seg_c):
    length = seg_c.shape[0]

    @pl.loop(0, length // BQ)
    def _(i):
        rows = rows_of(i, BQ)
        seg_c[rows, :] = jnp.transpose(jnp.broadcast_to(seg_v[:, rows].astype(jnp.float32), (128, BQ)))


def wide(column, lanes):
    return jnp.concatenate([column] * (lanes // 128), axis=1)


def attn_fwd_body(scale, seg_s, seg_v, q_ref, k_ref, v_ref, o_ref, a_ref, lse_ref, vt, seg_c):
    length, width = q_ref.shape
    half = width // 2
    n = length // BQ
    first = head_lanes((BQ, width), half)
    seg_columns(seg_v, seg_c)

    @pl.loop(0, n)
    def _(i):
        rows = rows_of(i, BQ)
        t = jnp.transpose(v_ref[rows, :])
        for h in range(2):
            vt[h, 0:half, rows] = t[h * half : (h + 1) * half]
            vt[h, half : half + 16, rows] = jnp.ones((16, BQ), jnp.bfloat16)

    sides = []
    heads = (lax.broadcasted_iota(jnp.int32, (16, width), 1) < half) == (lax.broadcasted_iota(jnp.int32, (16, width), 0) < 8)
    heads = heads.astype(jnp.float32).astype(jnp.bfloat16)
    for ref in (q_ref, k_ref):
        squares = nt(heads, ref[...] * ref[...])
        sides.append((jnp.max(squares[0:8]), jnp.max(squares[8:16])))
    bound = (40.0 / scale) ** 2
    small = jnp.logical_and(sides[0][0] * sides[1][0] <= bound, sides[0][1] * sides[1][1] <= bound)

    @pl.loop(0, n)
    def _(i):
        lo, hi = block_range(seg_s, i * BQ, BQ, BK, length // BK)
        rows = rows_of(i, BQ)
        q = q_ref[rows, :] * jnp.bfloat16(scale)
        zero = jnp.zeros_like(q)
        qs = (jnp.where(first, q, zero), jnp.where(first, zero, q))
        seg_q = seg_v[:, rows].astype(jnp.float32)


        def masked(cols, h):
            same = wide(seg_c[cols, :], BQ) == seg_q
            return jnp.where(same, nt(k_ref[cols, :], qs[h]), NEGATIVE)

        def store(tops, accs):
            o = []
            for h in range(2):
                total = accs[h][half : half + 1]
                o.append(accs[h][0:half] / total)
                lse_ref[h : h + 1, rows] = tops[h] + jnp.log(total)
            o = jnp.transpose(jnp.concatenate(o, axis=0))
            o_ref[rows, :] = o
            a_ref[rows, :] = o.astype(jnp.bfloat16)

        def direct(count):
            base = jnp.minimum(lo, length // BK - count)
            accs = [jnp.zeros((half + 16, BQ), jnp.float32)] * 2
            for j in range(count):
                cols = rows_of(base + j, BK)
                for h in range(2):
                    accs[h] = accs[h] + nn(vt[h, :, cols], jnp.exp(masked(cols, h)).astype(jnp.bfloat16))
            store([jnp.zeros((1, BQ), jnp.float32)] * 2, accs)

        def running():
            def step(j, state):
                cols = rows_of(j, BK)
                out = []
                for h in range(2):
                    m, acc = state[h]
                    s = masked(cols, h)
                    top = jnp.maximum(m, jnp.max(s, axis=0, keepdims=True))
                    p = jnp.exp(s - top).astype(jnp.bfloat16)
                    out.append((top, acc * jnp.exp(m - top) + nn(vt[h, :, cols], p)))
                return tuple(out)

            one = (jnp.full((1, BQ), NEGATIVE, jnp.float32), jnp.zeros((half + 16, BQ), jnp.float32))
            state = lax.fori_loop(lo, hi, step, (one, one))
            store([state[h][0] for h in range(2)], [state[h][1] for h in range(2)])

        for count in range(1, length // BK + 1):
            pl.when(jnp.logical_and(small, hi - lo == count))(functools.partial(direct, count))
        pl.when(jnp.logical_not(small))(running)


def attn_fwd(scale, seg, q, k, v):
    length, width = q.shape
    return pl.pallas_call(
        functools.partial(attn_fwd_body, scale),
        name="attn_fwd",
        out_shape=(
            jax.ShapeDtypeStruct((length, width), jnp.float32),
            jax.ShapeDtypeStruct((length, width), jnp.bfloat16),
            jax.ShapeDtypeStruct((8, length), jnp.float32),
        ),
        in_specs=[SM, VM, VM, VM, VM],
        out_specs=(VM, VM, VM),
        scratch_shapes=[pltpu.VMEM((2, width // 2 + 16, length), jnp.bfloat16), pltpu.VMEM((length, 128), jnp.float32)],
        compiler_params=pltpu.CompilerParams(vmem_limit_bytes=32 << 20),
        cost_estimate=pl.CostEstimate(flops=4 * length * length * width, bytes_accessed=6 * length * width, transcendentals=2 * length * length),
    )(seg, seg, q, k, v)


MESH = pl.DeviceIdType.MESH
HBM = pl.BlockSpec(memory_space=pltpu.HBM)
F32 = jnp.float32
BF16 = jnp.bfloat16


def tn(a, b):
    return lax.dot_general(a, b, (((0,), (0,)), ((), ())), preferred_element_type=F32)


def fold_rows(v):
    return jnp.sum(v.reshape(v.shape[0] // 8, 8, v.shape[1]), axis=0)


class Wires:
    def __init__(self, send_sems, recv_sems, local_sems):
        self.send_sems, self.recv_sems, self.local_sems = send_sems, recv_sems, local_sems
        self.count = 0
        self.local_count = 0
        self.sent = []
        self.rep = lax.axis_index("rep")
        self.own = lax.axis_index("fsdp")

    def remote(self, src, dst, peer, rep=None):
        i = self.count
        self.count = i + 1
        return pltpu.make_async_remote_copy(
            src_ref=src, dst_ref=dst, send_sem=self.send_sems.at[i], recv_sem=self.recv_sems.at[i],
            device_id=(self.rep if rep is None else rep, peer), device_id_type=MESH,
        )

    def send(self, src, dst, peer):
        copy = self.remote(src, dst, peer)
        copy.start()
        self.sent.append(copy)
        return copy

    def local(self, src, dst):
        copy = pltpu.make_async_copy(src, dst, self.local_sems.at[self.local_count])
        self.local_count += 1
        copy.start()
        return copy

    def greet(self, peers):
        barrier = pltpu.get_barrier_semaphore()
        for rep, peer in peers:
            pl.semaphore_signal(barrier, inc=1, device_id=(rep, peer), device_id_type=MESH)
        pl.semaphore_wait(barrier, len(peers))

    def finish(self):
        for copy in self.sent:
            copy.wait_send()


class Line:
    def __init__(self, wires, own, land, far, count):
        self.own, self.land, self.far = own, land, far
        rep, dev = wires.rep, wires.own
        size = own.shape[0] // count
        self.rows = [pl.ds(i * size, size) for i in range(count)]
        self.inner = jnp.logical_or(rep == 1, rep == 2)
        self.outer = jnp.logical_not(self.inner)
        near, across = lax.bitwise_xor(rep, 1), lax.bitwise_xor(rep, 3)
        self.first = [wires.remote(own.at[r], land.at[r], dev, near) for r in self.rows]
        self.middle = [wires.remote(own.at[r], far.at[r], dev, across) for r in self.rows]
        self.back = [wires.remote(land.at[r], land.at[r], dev, near) for r in self.rows]

    def start(self):
        @pl.when(self.outer)
        def _():
            for copy in self.first:
                copy.start()

    def collect(self, which):
        @pl.when(self.inner)
        def _():
            for i in which:
                r = self.rows[i]
                self.first[i].wait_recv()
                self.own[r, :] = (self.own[r, :].astype(F32) + self.land[r, :].astype(F32)).astype(BF16)
                self.middle[i].start()

    def total(self, which):
        @pl.when(self.inner)
        def _():
            for i in which:
                r = self.rows[i]
                self.middle[i].wait_recv()
                self.land[r, :] = (self.own[r, :].astype(F32) + self.far[r, :].astype(F32)).astype(BF16)
                self.back[i].start()

    def arrive(self, which):
        @pl.when(self.outer)
        def _():
            for i in which:
                self.back[i].wait_recv()

    def finish(self):
        @pl.when(self.outer)
        def _():
            for copy in self.first:
                copy.wait_send()

        @pl.when(self.inner)
        def _():
            for i in range(len(self.rows)):
                self.middle[i].wait_send()
                self.back[i].wait_send()


class Hops:
    def __init__(self, wires, view):
        rep, reps = wires.rep, 4
        self.all = []
        for hop in range(1, reps):
            for step in (1, -1):
                index, to, come = rep - step * (hop - 1), rep + step, rep - step * hop
                going = (index >= 0) & (index < reps) & (to >= 0) & (to < reps)
                coming = (come >= 0) & (come < reps)
                refs = view(jnp.clip(index, 0, reps - 1))
                copies = [wires.remote(ref, ref, wires.own, jnp.clip(to, 0, reps - 1)) for ref in refs]
                self.all.append((hop, going, coming, copies))

    def each(self, hop, kind):
        for at, going, coming, copies in self.all:
            if hop in (0, at):

                @pl.when(coming if kind == "wait_recv" else going)
                def _():
                    for copy in copies:
                        getattr(copy, kind)()

    def start(self, hop):
        self.each(hop, "start")

    def wait(self, hop):
        self.each(hop, "wait_recv")

    def finish(self):
        self.each(0, "wait_send")


class Spread:
    def __init__(self, wires, slots, half):
        self.wires, self.slots, self.half = wires, slots, half
        self.chip = wires.own // 2
        self.x, self.y = lax.bitwise_xor(wires.own, 2), lax.bitwise_xor(wires.own, 4)
        self.cx, self.cy, self.cd = (lax.bitwise_xor(self.chip, m) for m in (1, 2, 3))
        self.a, self.b = pl.ds(0, half), pl.ds(half, half)

    def piece(self, chip, part):
        return self.slots.at[chip, part]

    def put(self, chip, part, peer):
        return self.wires.send(self.piece(chip, part), self.piece(chip, part), peer)

    def first_half(self):
        self.xa = self.put(self.chip, self.a, self.x)
        self.ya = self.put(self.chip, self.a, self.y)

    def second_half(self):
        self.yb = self.put(self.chip, self.b, self.y)
        self.xb = self.put(self.chip, self.b, self.x)

    def relay(self):
        self.xa.wait_recv()
        self.da = self.put(self.cx, self.a, self.y)
        self.yb.wait_recv()
        self.db = self.put(self.cy, self.b, self.x)

    def wait_sides(self):
        self.xb.wait_recv()
        self.ya.wait_recv()

    def wait_diagonal(self):
        self.da.wait_recv()
        self.db.wait_recv()


class Gather:
    def __init__(self, wires, part, side, last, half):
        self.wires, self.part, self.side, self.last, self.half = wires, part, side, last, half
        self.chip = wires.own // 2
        self.x, self.y = lax.bitwise_xor(wires.own, 2), lax.bitwise_xor(wires.own, 4)
        self.cx, self.cy, self.cd = (lax.bitwise_xor(self.chip, m) for m in (1, 2, 3))
        self.a, self.b = pl.ds(0, half), pl.ds(half, half)

    def send_x(self):
        self.x_own = self.wires.send(self.part.at[self.cx, self.a], self.side.at[0], self.x)

    def send_y(self):
        self.y_own = self.wires.send(self.part.at[self.cy, self.b], self.side.at[1], self.y)

    def send_diagonal(self):
        self.x_far = self.wires.send(self.part.at[self.cd, self.a], self.side.at[2], self.x)
        self.y_far = self.wires.send(self.part.at[self.cd, self.b], self.side.at[3], self.y)

    def relay(self):
        step = 32

        def add(chip, start, slot):
            @pl.loop(0, self.half // step)
            def _(t):
                rows = pl.ds(pl.multiple_of(start + t * step, step), step)
                near = self.part[chip, rows, :].astype(F32) + self.side[slot, rows_of(t, step), :].astype(F32)
                self.part[chip, rows, :] = near.astype(BF16)

        self.x_far.wait_recv()
        add(self.cy, 0, 2)
        self.y_last = self.wires.send(self.part.at[self.cy, self.a], self.last.at[0], self.y)
        self.y_far.wait_recv()
        add(self.cx, self.half, 3)
        self.x_last = self.wires.send(self.part.at[self.cx, self.b], self.last.at[1], self.x)

    def wait_first(self):
        self.x_own.wait_recv()
        self.y_last.wait_recv()

    def wait_second(self):
        self.y_own.wait_recv()
        self.x_last.wait_recv()

    def total(self, which, offset, size):
        rows = pl.ds(pl.multiple_of(which * self.half + offset, size), size)
        here = pl.ds(pl.multiple_of(offset, size), size)
        return self.part[self.chip, rows, :].astype(F32) + self.side[which, here, :].astype(F32) + self.last[which, here, :].astype(F32)


def middle_body(
    heads, x, cot, upout, down_w, proj_bias, hidden_bias, gain, shift,
    output, branch_grad, grad_heads, vec, down_grad, keep, to_x, to_y, to_d,
    att, out_full, up_full, down_full, h1, z1, r1, gs, fl, act, slope, part, side, last, sl, pre, part2, side2, last2,
    branch_low, agl, acc, d_send, d_recv, d_keep, u_send, u_recv, u_keep, o_send, o_recv, o_keep,
    send_sems, recv_sems, local_sems,
):
    w = Wires(send_sems, recv_sems, local_sems)
    own = w.own
    core, chip = lax.rem(own, 2), own // 2
    mate = lax.bitwise_xor(own, 1)
    cx, cy, cd = (lax.bitwise_xor(chip, m) for m in (1, 2, 3))
    toks, width = x.shape
    ff = up_full.shape[1]
    head_width = heads.shape[1]
    half = toks // 2
    piece = upout.shape[2]
    tile = 256
    w.greet(
        [(w.rep, lax.bitwise_xor(own, m)) for m in range(1, 8)] + [(lax.rem(w.rep + 1, 4), own), (lax.rem(w.rep + 3, 4), own)]
    )

    swaps = []
    for m in (6, 2, 4, 1, 3, 5, 7):
        peer = lax.bitwise_xor(own, m)
        swaps.append(w.send(heads.at[rows_of(peer, toks)], att.at[:, rows_of(own, head_width)], peer))
    quarter = piece // 4
    some = rows_of(w.rep, quarter)

    def up_piece(k, r):
        return up_full.at[pl.ds(pl.multiple_of((2 * k + core) * piece + r * quarter, quarter), quarter)]

    others = (cd, cx, cy)
    seeds = [w.local(upout.at[k, 0, some], up_piece(k, w.rep)) for k in others]
    hops = Hops(w, lambda r: [up_piece(k, r) for k in others])
    weights = []
    for k in range(4):
        dst = rows_of(2 * k + core, piece)
        weights.append((w.local(upout.at[k, 1], out_full.at[dst]), w.send(upout.at[k, 1], out_full.at[dst], mate)))
    dst = rows_of(own, piece)
    weights.append((w.local(upout.at[chip, 0], up_full.at[dst]), w.send(upout.at[chip, 0], up_full.at[dst], mate)))
    dst = rows_of(core, ff // 2)
    weights.append((w.local(down_w, down_full.at[dst]), w.send(down_w, down_full.at[dst], mate)))
    for copy in seeds:
        copy.wait()
    hops.start(1)
    att[:, rows_of(own, head_width)] = heads[rows_of(own, toks), :]
    hops.wait(1)
    hops.start(2)
    for copy in swaps:
        copy.wait_recv()
    for here, there in weights:
        here.wait()
        there.wait_recv()

    @pl.loop(0, width // tile)
    def _(n):
        cols = rows_of(n, tile)
        h1[:, cols] = nn(att[...], out_full[:, cols]) + proj_bias[2:3, cols] + x[:, cols].astype(F32)

    step = 32
    acc[...] = jnp.zeros_like(acc)
    hops.wait(2)
    hops.start(3)

    def first_rows(t):
        rows = rows_of(t, step)
        v = h1[rows, :]
        center = v - jnp.mean(v, axis=1, keepdims=True)
        inv = lax.rsqrt(jnp.mean(center * center, axis=1, keepdims=True) + 1e-05)
        z = center * inv
        z1[rows, :] = z
        r1[rows, :] = jnp.broadcast_to(inv, (step, 128))
        fl[chip, rows, :] = (z * gain[0:1, :] + shift[0:1, :]).astype(BF16)

    spread = Spread(w, fl, half)
    pl.loop(0, half // step)(first_rows)
    spread.first_half()
    pl.loop(half // step, toks // step)(first_rows)
    spread.second_half()

    def forward(k):
        @pl.loop(0, ff // tile)
        def _(n):
            cols = rows_of(n, tile)
            hidden = nn(fl[k], up_full[:, cols]) + hidden_bias[:, pl.ds(pl.multiple_of(chip * ff + n * tile, tile), tile)]
            slope[k, :, cols] = hidden
            act[k, :, cols] = (hidden * (0.5 * (1.0 + lax.erf(hidden * (2.0**-0.5))))).astype(BF16)

        @pl.loop(0, width // tile)
        def _(n):
            cols = rows_of(n, tile)
            part[k, :, cols] = nn(act[k], down_full[:, cols]).astype(BF16)

    hops.wait(3)
    passed = []
    for k in others:
        dst = rows_of(2 * k + core, piece)
        passed.append(w.send(up_full.at[dst], up_full.at[dst], mate))
    for copy in passed:
        copy.wait_recv()
    forward(chip)
    gather = Gather(w, part, side, last, half)
    spread.relay()
    spread.wait_sides()
    forward(cx)
    gather.send_x()
    forward(cy)
    gather.send_y()
    spread.wait_diagonal()
    forward(cd)
    gather.send_diagonal()

    def slopes(k):
        @pl.loop(0, toks // 32)
        def _(t):
            rows = rows_of(t, 32)
            hidden = slope[k, rows, :]
            cdf = 0.5 * (1.0 + lax.erf(hidden * (2.0**-0.5)))
            slope[k, rows, :] = cdf + hidden * (jnp.exp(-0.5 * hidden * hidden) * ((2.0 * math.pi) ** -0.5))

    slopes(0)
    slopes(1)
    gather.relay()
    slopes(2)
    slopes(3)

    def second_rows(which, t):
        rows = pl.ds(pl.multiple_of(which * half + t * step, step), step)
        v = z1[rows, :] * gain[0:1, :] + shift[0:1, :] + gather.total(which, t * step, step) + proj_bias[3:4, :]
        center = v - jnp.mean(v, axis=1, keepdims=True)
        inv = lax.rsqrt(jnp.mean(center * center, axis=1, keepdims=True) + 1e-05)
        z = center * inv
        output[rows, :] = (z * gain[1:2, :] + shift[1:2, :]).astype(BF16)
        c = cot[rows, :].astype(F32)
        e = c * gain[1:2, :]
        grad = inv * (e - jnp.mean(e, axis=1, keepdims=True) - z * jnp.mean(e * z, axis=1, keepdims=True))
        gs[rows, :] = grad
        low = grad.astype(BF16)
        sl[chip, rows, :] = low
        acc[0] += fold_rows(c * z)
        acc[1] += fold_rows(c)
        acc[2] += fold_rows(low.astype(F32))

    spread2 = Spread(w, sl, half)
    gather.wait_first()
    pl.loop(0, half // step)(functools.partial(second_rows, 0))
    spread2.first_half()
    gather.wait_second()
    pl.loop(0, half // step)(functools.partial(second_rows, 1))
    spread2.second_half()

    def backward(k):
        @pl.loop(0, ff // tile)
        def _(n):
            cols = rows_of(n, tile)
            grad = nt(sl[k], down_full[cols, :]) * slope[k, :, cols]
            low = grad.astype(BF16)
            pre[k, :, cols] = low
            acc[3, :, cols] += fold_rows(low.astype(F32))

        @pl.loop(0, width // tile)
        def _(n):
            cols = rows_of(n, tile)
            part2[k, :, cols] = nt(pre[k], up_full[cols, :]).astype(BF16)

    backward(chip)
    gather2 = Gather(w, part2, side2, last2, half)
    spread2.relay()
    spread2.wait_sides()
    backward(cx)
    gather2.send_x()
    backward(cy)
    gather2.send_y()
    spread2.wait_diagonal()
    backward(cd)
    gather2.send_diagonal()

    def down_rows(which, n):
        cols = pl.ds(pl.multiple_of(which * (ff // 2) + n * tile, tile), tile)
        lhs = act[:, :, cols].reshape(4 * toks, tile)
        return tn(lhs, sl[...].reshape(4 * toks, width))

    @pl.loop(0, ff // 2 // tile)
    def _(n):
        d_send[rows_of(n, tile), :] = down_rows(1 - core, n).astype(BF16)

    d_copy = w.send(d_send, d_recv, mate)

    @pl.loop(0, ff // 2 // tile)
    def _(n):
        d_keep[rows_of(n, tile), :] = down_rows(core, n)

    gather2.relay()
    d_copy.wait_recv()

    @pl.loop(0, ff // 2 // 64)
    def _(t):
        rows = rows_of(t, 64)
        down_grad[rows, :] = (d_keep[rows, :] + d_recv[rows, :].astype(F32)).astype(BF16)

    def up_rows(which, k):
        cols = pl.ds(pl.multiple_of((2 * k + which) * piece, piece), piece)
        lhs = fl[:, :, cols].reshape(4 * toks, piece)
        return tn(lhs, pre[...].reshape(4 * toks, ff))

    @pl.loop(0, 4)
    def _(k):
        u_send[k] = up_rows(1 - core, k).astype(BF16)

    u_copy = w.send(u_send, u_recv, mate)

    def branch_rows(which, t):
        rows = pl.ds(pl.multiple_of(which * half + t * step, step), step)
        grad = gs[rows, :] + gather2.total(which, t * step, step)
        z = z1[rows, :]
        e = grad * gain[0:1, :]
        out = r1[rows, 0:1] * (e - jnp.mean(e, axis=1, keepdims=True) - z * jnp.mean(e * z, axis=1, keepdims=True))
        branch_grad[rows, :] = out
        low = out.astype(BF16)
        branch_low[rows, :] = low
        acc[4] += fold_rows(grad * z)
        acc[5] += fold_rows(grad)
        acc[6] += fold_rows(low.astype(F32))

    gather2.wait_first()
    pl.loop(0, half // step)(functools.partial(branch_rows, 0))
    gather2.wait_second()
    pl.loop(0, half // step)(functools.partial(branch_rows, 1))

    @pl.loop(0, width // tile)
    def _(n):
        cols = rows_of(n, tile)
        agl[:, cols] = nt(branch_low[...], out_full[cols, :]).astype(BF16)

    backs = []
    for m in (6, 2, 4, 1, 3, 5, 7):
        peer = lax.bitwise_xor(own, m)
        backs.append(w.send(agl.at[:, rows_of(peer, head_width)], grad_heads.at[rows_of(own, toks)], peer))
    grad_heads[rows_of(own, toks), :] = agl[:, rows_of(own, head_width)]

    def out_rows(which, k):
        cols = pl.ds(pl.multiple_of((2 * k + which) * piece, piece), piece)
        return tn(att[:, cols], branch_low[...])

    @pl.loop(0, 4)
    def _(k):
        o_send[k] = out_rows(1 - core, k).astype(BF16)

    o_copy = w.send(o_send, o_recv, mate)

    @pl.loop(0, 4)
    def _(k):
        u_keep[k] = up_rows(core, k)
        o_keep[k] = out_rows(core, k)

    u_copy.wait_recv()
    o_copy.wait_recv()
    for m, ref in enumerate((keep, to_x, to_y, to_d)):
        k = lax.bitwise_xor(chip, m)
        ref[0] = (u_keep[k] + u_recv[k].astype(F32)).astype(BF16)
        ref[1] = (o_keep[k] + o_recv[k].astype(F32)).astype(BF16)
    vec[...] = jnp.zeros_like(vec)
    for row, slot in ((2, 6), (3, 2), (4, 4), (5, 0), (6, 5), (7, 1)):
        vec[row : row + 1, :] = jnp.sum(acc[slot], axis=0, keepdims=True)
    hidden_sum = jnp.sum(acc[3], axis=0, keepdims=True)
    for k in range(4):
        vec[8 + k : 9 + k, :] = jnp.where(chip == k, hidden_sum, jnp.zeros_like(hidden_sum))
    for copy in backs:
        copy.wait_recv()
    hops.finish()
    w.finish()


def middle(heads, x, cot, upout, down_w, proj_bias, hidden_bias, gain, shift):
    toks, width = x.shape
    piece = upout.shape[2]
    ff = 2 * down_w.shape[0]
    half = toks // 2
    shape = jax.ShapeDtypeStruct
    vm = pltpu.VMEM
    return pl.pallas_call(
        middle_body,
        name="middle",
        out_shape=(
            shape((toks, width), BF16),
            shape((toks, width), F32),
            shape(heads.shape, BF16),
            shape((16, width), F32),
            shape((ff // 2, width), BF16),
        )
        + (shape((2, piece, width), BF16),) * 4,
        in_specs=[VM, VM, VM, HBM, HBM] + [VM] * 4,
        out_specs=(VM,) * 9,
        scratch_shapes=[
            vm((toks, width), BF16), vm((width, width), BF16), vm((width, ff), BF16), vm((ff, width), BF16),
            vm((toks, width), F32), vm((toks, width), F32), vm((toks, 128), F32), vm((toks, width), F32),
            vm((4, toks, width), BF16), vm((4, toks, ff), BF16), vm((4, toks, ff), F32),
            vm((4, toks, width), BF16), vm((4, half, width), BF16), vm((2, half, width), BF16),
            vm((4, toks, width), BF16), vm((4, toks, ff), BF16),
            vm((4, toks, width), BF16), vm((4, half, width), BF16), vm((2, half, width), BF16),
            vm((toks, width), BF16), vm((toks, width), BF16), vm((8, 8, width), F32),
            vm((ff // 2, width), BF16), vm((ff // 2, width), BF16), vm((ff // 2, width), F32),
            vm((4, piece, ff), BF16), vm((4, piece, ff), BF16), vm((4, piece, ff), F32),
            vm((4, piece, width), BF16), vm((4, piece, width), BF16), vm((4, piece, width), F32),
            pltpu.SemaphoreType.DMA((96,)), pltpu.SemaphoreType.DMA((96,)), pltpu.SemaphoreType.DMA((16,)),
        ],
        compiler_params=pltpu.CompilerParams(collective_id=1, has_side_effects=True, vmem_limit_bytes=44 << 20),
    )(heads, x, cot, upout, down_w, proj_bias, hidden_bias, gain, shift)


def project_body(x, qkv_w, up_w, out_w, proj_bias, q_out, k_out, v_out, xs, w_full, upout, stage, send_sems, recv_sems, local_sems):
    w = Wires(send_sems, recv_sems, local_sems)
    own = w.own
    core, chip = lax.rem(own, 2), own // 2
    mate = lax.bitwise_xor(own, 1)
    toks, width = x.shape
    piece = qkv_w.shape[0]
    share = width // 4
    head_width = share // 2
    rep = w.rep
    reps = 4
    w.greet([(rep, lax.bitwise_xor(own, m)) for m in (1, 2, 4, 6)] + [(lax.rem(rep + 1, reps), own), (lax.rem(rep + reps - 1, reps), own)])
    mine = rows_of(own, piece)
    quarter = piece // reps

    def source(part, to_chip):
        return qkv_w.at[:, pl.ds(pl.multiple_of(part * width + to_chip * share, share), share)]

    arrivals = []
    for m in (6, 2, 4):
        peer = lax.bitwise_xor(own, m)
        copies = [w.send(source(p, lax.bitwise_xor(chip, m // 2)), w_full.at[mine, pl.ds(p * share, share)], peer) for p in range(3)]
        arrivals.append((peer, copies))
    fetched = []
    for m in (6, 2, 4):
        peer, to_chip = lax.bitwise_xor(own, m), lax.bitwise_xor(chip, m // 2)
        some = rows_of(rep, quarter)
        fetched.append(w.send(up_w.at[some, rows_of(to_chip, width)], upout.at[chip, 0, some], peer))
        fetched.append(w.send(out_w.at[some], upout.at[chip, 1, some], peer))
    kept = [w.local(up_w.at[:, rows_of(chip, width)], upout.at[chip, 0]), w.local(out_w, upout.at[chip, 1])]
    others = [lax.bitwise_xor(chip, m) for m in (3, 1, 2)]
    hops = Hops(w, lambda r: [upout.at[c, 1, rows_of(r, quarter)] for c in others])
    xs[chip] = x[...]
    spread = Spread(w, xs, toks // 2)
    spread.first_half()
    spread.second_half()
    here = [w.local(source(p, chip), w_full.at[mine, pl.ds(p * share, share)]) for p in range(3)]
    theirs = [w.send(source(p, chip), w_full.at[mine, pl.ds(p * share, share)], mate) for p in range(3)]
    for peer, copies in arrivals:
        for copy in copies:
            copy.wait_recv()
        rows = rows_of(peer, piece)
        theirs.append(w.send(w_full.at[rows], w_full.at[rows], mate))
    for copy in fetched:
        copy.wait_recv()
    hops.start(1)
    for copy in here:
        copy.wait()
    for copy in theirs:
        copy.wait_recv()
    outs = (q_out, k_out, v_out)
    swaps = []

    def block(k):
        rows = rows_of(2 * k + core, toks)
        for p in range(3):
            r = nn(xs[k], w_full[:, pl.ds(p * share, share)])
            if p != 1:
                r = r + proj_bias[p // 2 : p // 2 + 1, rows_of(chip, share)]
            stage[k, :, pl.ds(p * share, share)] = r.astype(BF16)
            swaps.append(w.send(stage.at[k, :, pl.ds(pl.multiple_of(p * share + (1 - core) * head_width, head_width), head_width)], outs[p].at[rows], mate))
            outs[p][rows, :] = stage[k, :, pl.ds(pl.multiple_of(p * share + core * head_width, head_width), head_width)]

    block(chip)
    spread.relay()
    hops.wait(1)
    hops.start(2)
    spread.wait_sides()
    block(spread.cx)
    block(spread.cy)
    hops.wait(2)
    hops.start(3)
    spread.wait_diagonal()
    block(spread.cd)
    for copy in swaps:
        copy.wait_recv()
    hops.wait(3)
    for copy in kept:
        copy.wait()
    hops.finish()
    w.finish()


def project(x, qkv_w, up_w, out_w, proj_bias):
    toks, width = x.shape
    piece = qkv_w.shape[0]
    shape = jax.ShapeDtypeStruct
    vm = pltpu.VMEM
    heads = shape((8 * toks, width // 8), BF16)
    return pl.pallas_call(
        project_body,
        name="project",
        out_shape=(heads, heads, heads, shape((4, toks, width), BF16), shape((8 * piece, 3 * width // 4), BF16), shape((4, 2, piece, width), BF16)),
        in_specs=[VM, VM, HBM, HBM, VM],
        out_specs=(VM,) * 5 + (HBM,),
        scratch_shapes=[
            vm((4, toks, 3 * width // 4), BF16),
            pltpu.SemaphoreType.DMA((72,)), pltpu.SemaphoreType.DMA((72,)), pltpu.SemaphoreType.DMA((8,)),
        ],
        compiler_params=pltpu.CompilerParams(collective_id=0, has_side_effects=True, vmem_limit_bytes=40 << 20),
    )(x, qkv_w, up_w, out_w, proj_bias)


def backward_body(
    scale, seg, q, k, v, g, o, lse, xs, w_full, branch_grad, vec, down, keep, to_x, to_y, to_d,
    input_grad, qkv_sum, upout_sum, down_sum, vec_sum,
    corr, kt, dk_acc, dv_acc, dqt, seg_c, heads, grads, part, side, last, q_send, q_recv, q_keep, q_piece, l_own, l_far,
    d_own, d_far, got, y_own, y_far, v_sum, v_recv,
    send_sems, recv_sems, local_sems,
):
    w = Wires(send_sems, recv_sems, local_sems)
    own, rep = w.own, w.rep
    core, chip = lax.rem(own, 2), own // 2
    mate = lax.bitwise_xor(own, 1)
    toks, width = branch_grad.shape
    share = width // 4
    head_width = share // 2
    piece = keep.shape[1]
    half = toks // 2
    tile = 256
    z1, z2, z3 = (lax.bitwise_xor(rep, m) for m in (1, 2, 3))
    w.greet([(rep, lax.bitwise_xor(own, m)) for m in (1, 2, 4, 6)] + [(z1, own), (z2, own), (z3, own)])

    spread = [w.send(ref, got.at[i], lax.bitwise_xor(own, m)) for i, (m, ref) in enumerate(((6, to_d), (2, to_x), (4, to_y)))]
    d_own[...] = down[...]
    down_line = Line(w, d_own, down_sum, d_far, 8)
    down_line.start()
    upout_line = Line(w, y_own, upout_sum, y_far, 10)
    lines = [Line(w, l_own.at[p], qkv_sum.at[p], l_far.at[p], 4) for p in range(3)]

    def upout_start():
        for copy in spread:
            copy.wait_recv()
        for i, ref in enumerate((keep, got.at[1], got.at[2], got.at[0])):
            y_own[i * piece : (i + 1) * piece, :] = ref[0]
        y_own[4 * piece :, :] = (keep[1].astype(F32) + got[0, 1].astype(F32) + got[1, 1].astype(F32) + got[2, 1].astype(F32)).astype(BF16)
        upout_line.start()

    hooks = {
        0: lambda: down_line.collect((0,)),
        1: lambda: (down_line.collect((1,)), down_line.total((0,))),
        2: lambda: (down_line.collect((2, 3)), down_line.total((1,))),
        3: lambda: (down_line.collect((4,)), down_line.total((2, 3))),
        4: lambda: (down_line.collect((5, 6)), down_line.total((4,))),
        5: lambda: (upout_start(), down_line.collect((7,)), down_line.total((5, 6))),
        6: lambda: (down_line.total((7,)), upout_line.collect((0,))),
        7: lambda: (upout_line.collect((1,)), upout_line.total((0,))),
    }

    length, head_cols = q.shape
    headd = head_cols // 2
    blocks = length // BQ
    first = head_lanes((BQ, head_cols), headd)
    seg_columns(seg, seg_c)

    @pl.loop(0, blocks)
    def _(i):
        rows = rows_of(i, BQ)
        prod = jnp.transpose(g[rows, :].astype(F32) * o[rows, :])
        corr[0:1, rows] = jnp.sum(prod[:headd], axis=0, keepdims=True)
        corr[1:2, rows] = jnp.sum(prod[headd:], axis=0, keepdims=True)
        kt[:, rows] = jnp.transpose(k[rows, :])
        dk_acc[rows, :] = jnp.zeros((BQ, head_cols), F32)
        dv_acc[rows, :] = jnp.zeros((BQ, head_cols), F32)

    @pl.loop(0, blocks)
    def _(i):
        rows = rows_of(i, BQ)
        qb = q[rows, :] * jnp.bfloat16(scale)
        gb = g[rows, :]
        zero = jnp.zeros_like(qb)
        qs = (jnp.where(first, qb, zero), jnp.where(first, zero, qb))
        gs = (jnp.where(first, gb, zero), jnp.where(first, zero, gb))
        qz = jnp.concatenate(qs, axis=0)
        gz = jnp.concatenate(gs, axis=0)
        seg_q = seg[:, rows].astype(F32)
        dq = [jnp.zeros((headd, BQ), F32)] * 2
        for j in range(length // BK):
            cols = pl.ds(j * BK, BK)
            kb = k[cols, :]
            vb = v[cols, :]
            same = wide(seg_c[cols, :], BQ) == seg_q
            ps, ds = [], []
            for h in range(2):
                s = jnp.where(same, nt(kb, qs[h]), NEGATIVE)
                p = jnp.exp(s - lse[h : h + 1, rows])
                dp = nt(vb, gs[h])
                dscore = (p * (dp - corr[h : h + 1, rows])).astype(BF16)
                ps.append(p.astype(BF16))
                ds.append(dscore)
                dq[h] = dq[h] + nn(kt[h * headd : (h + 1) * headd, cols], dscore)
            dv_acc[cols, :] += nn(jnp.concatenate(ps, axis=1), gz)
            dk_acc[cols, :] += nn(jnp.concatenate(ds, axis=1), qz)
        dqt[0:headd, :] = dq[0]
        dqt[headd:, :] = dq[1]
        heads[0, lax.rem(i, 2), i // 2] = (jnp.transpose(dqt[...]) * scale).astype(BF16)
        for at, hook in hooks.items():

            @pl.when(i == at)
            def _(hook=hook):
                hook()

    @pl.loop(0, blocks)
    def _(i):
        rows = rows_of(i, BQ)
        heads[1, lax.rem(i, 2), i // 2] = dk_acc[rows, :].astype(BF16)
        heads[2, lax.rem(i, 2), i // 2] = dv_acc[rows, :].astype(BF16)

    swaps = []
    for p in range(3):
        cols = pl.ds(pl.multiple_of(p * share + core * head_width, head_width), head_width)
        swaps.append(w.send(heads.at[p, 1 - core], grads.at[:, :, cols], mate))
        grads[:, :, cols] = heads[p, core]
    upout_line.collect((2,))
    v_sum[...] = vec[...]
    for row, p in ((0, 0), (1, 2)):
        total = jnp.sum(heads[p].reshape(8 * toks, head_width).astype(F32), axis=0, keepdims=True)
        v_sum[row : row + 1, rows_of(own, head_width)] = total
    rounds = [(None, mate), (None, lax.bitwise_xor(own, 2)), (None, lax.bitwise_xor(own, 4)), (z1, own), (z2, own)]
    flying = []

    def vec_start(i):
        copy = w.remote(v_sum.at[...] if i == 0 else v_recv.at[4 + i], v_recv.at[i], rounds[i][1], rounds[i][0])
        copy.start()
        w.sent.append(copy)
        flying.append(copy)

    def vec_step(i):
        flying[i].wait_recv()
        base = v_sum[...] if i == 0 else v_recv[4 + i]
        if i < 4:
            v_recv[5 + i] = base + v_recv[i]
            vec_start(i + 1)
        else:
            vec_sum[...] = base + v_recv[i]

    vec_start(0)

    def qkv_rows(which, kk, p):
        cols = pl.ds(pl.multiple_of((2 * kk + which) * piece, piece), piece)
        return tn(xs[:, :, cols].reshape(4 * toks, piece), grads[:, :, p * share : (p + 1) * share].reshape(4 * toks, share))

    def theirs(p):
        @pl.loop(0, 4)
        def _(kk):
            q_send[p, kk] = qkv_rows(1 - core, kk, p).astype(BF16)

        return w.send(q_send.at[p], q_recv.at[p], mate)

    def ours(p):
        @pl.loop(0, 4)
        def _(kk):
            q_keep[p, kk] = qkv_rows(core, kk, p)

    moved = []

    def pieces(p, copy):
        copy.wait_recv()

        @pl.loop(0, 4)
        def _(kk):
            q_piece[p, kk] = (q_keep[p, kk] + q_recv[p, kk].astype(F32)).astype(BF16)

        cols = rows_of(chip, share)
        moved.append([w.send(q_piece.at[p, lax.bitwise_xor(chip, m // 2)], l_own.at[p, :, cols], lax.bitwise_xor(own, m)) for m in (6, 2, 4)])
        l_own[p, :, cols] = q_piece[p, chip]

    def line_start(p):
        for copy in moved[p]:
            copy.wait_recv()
        lines[p].start()

    swaps[0].wait_recv()
    copies = [theirs(0)]
    ours(0)
    upout_line.collect((3,))
    upout_line.total((1,))
    swaps[1].wait_recv()
    copies.append(theirs(1))
    pieces(0, copies[0])
    upout_line.collect((4,))
    upout_line.total((2,))
    ours(1)
    swaps[2].wait_recv()
    copies.append(theirs(2))
    upout_line.collect((5,))
    upout_line.total((3,))
    pieces(1, copies[1])
    ours(2)
    upout_line.collect((6,))
    upout_line.total((4,))
    pieces(2, copies[2])
    vec_step(0)

    def partial(kk):
        @pl.loop(0, width // tile)
        def _(n):
            cols = rows_of(n, tile)
            part[kk, :, cols] = nt(grads[kk], w_full[cols, :]).astype(BF16)

    gather = Gather(w, part, side, last, half)
    partial(gather.cd)
    gather.send_diagonal()
    line_start(0)
    partial(gather.cx)
    gather.send_x()
    line_start(1)
    upout_line.collect((7,))
    upout_line.total((5, 6))
    partial(gather.cy)
    gather.send_y()
    line_start(2)
    partial(chip)
    upout_line.collect((8,))
    upout_line.total((7,))
    vec_step(1)
    upout_line.collect((9,))
    gather.relay()
    upout_line.total((8, 9))
    vec_step(2)
    step = 32

    def final_rows(which, t):
        rows = pl.ds(pl.multiple_of(which * half + t * step, step), step)
        input_grad[rows, :] = (branch_grad[rows, :] + gather.total(which, t * step, step)).astype(BF16)

    order = [(p, i) for p in range(3) for i in range(4)]

    def hop(at):
        if at < len(order):
            lines[order[at][0]].collect((order[at][1],))
        if at >= 2:
            lines[order[at - 2][0]].total((order[at - 2][1],))

    for at in range(5):
        hop(at)
    vec_step(3)
    gather.wait_first()
    pl.loop(0, half // step)(functools.partial(final_rows, 0))
    for at in range(5, 8):
        hop(at)
    vec_step(4)
    gather.wait_second()
    pl.loop(0, half // step)(functools.partial(final_rows, 1))
    for at in range(8, len(order) + 2):
        hop(at)
    down_line.arrive(range(8))
    upout_line.arrive(range(10))
    for line in lines:
        line.arrive(range(4))
    for line in [down_line, upout_line] + lines:
        line.finish()
    w.finish()


def backward(scale, seg, q, k, v, g, o, lse, xs, w_full, branch_grad, vec, down, keep, to_x, to_y, to_d):
    toks, width = branch_grad.shape
    length, head_cols = q.shape
    piece = keep.shape[1]
    share = width // 4
    half = toks // 2
    shape = jax.ShapeDtypeStruct
    vm = pltpu.VMEM
    small = vm((3, 4, piece, share), BF16)
    five = vm((5 * piece, width), BF16)
    line = vm((3, piece, width), BF16)
    return pl.pallas_call(
        functools.partial(backward_body, scale),
        name="backward",
        out_shape=(
            shape((toks, width), BF16), shape((3, piece, width), BF16), shape((5 * piece, width), BF16), shape(down.shape, BF16), shape(vec.shape, F32),
        ),
        in_specs=[VM] * 16,
        out_specs=(VM,) * 5,
        scratch_shapes=[
            vm((8, length), F32), vm((head_cols, length), BF16), vm((length, head_cols), F32), vm((length, head_cols), F32),
            vm((head_cols, BQ), F32), vm((length, 128), F32), vm((3, 2, 4, toks, head_cols), BF16),
            vm((4, toks, 3 * share), BF16),
            vm((4, toks, width), BF16), vm((4, half, width), BF16), vm((2, half, width), BF16),
            small, small, vm((3, 4, piece, share), F32), small, line, line,
            vm(down.shape, BF16), vm(down.shape, BF16), vm((3, 2, piece, width), BF16), five, five,
            vm(vec.shape, F32), vm((9,) + vec.shape, F32),
            pltpu.SemaphoreType.DMA((160,)), pltpu.SemaphoreType.DMA((160,)), pltpu.SemaphoreType.DMA((8,)),
        ],
        compiler_params=pltpu.CompilerParams(collective_id=2, has_side_effects=True, vmem_limit_bytes=34 << 20),
    )(seg, q, k, v, g, o, lse, xs, w_full, branch_grad, vec, down, keep, to_x, to_y, to_d)


def emit_body(
    grad_scale, who, low, grad, qkv_sum, upout_sum, down_sum, vec_sum,
    output, input_grad, qkv_total, out_total, up_total, down_total, bias_total, hidden_total, gain_total, shift_total,
):
    width = low.shape[1]
    piece = qkv_sum.shape[1]
    output[...] = low[...]
    input_grad[...] = grad[...]
    for p in range(3):
        qkv_total[:, p * width : (p + 1) * width] = qkv_sum[p].astype(F32) * grad_scale
    chip = who[0]
    for m in range(4):
        up_total[:, rows_of(lax.bitwise_xor(chip, m), width)] = upout_sum[m * piece : (m + 1) * piece, :].astype(F32) * grad_scale
    out_total[...] = upout_sum[4 * piece :, :].astype(F32) * grad_scale
    down_total[...] = down_sum[...].astype(F32) * grad_scale
    bias_total[...] = vec_sum[0:4] * grad_scale
    gain_total[...] = vec_sum[4:6] * grad_scale
    shift_total[...] = vec_sum[6:8] * grad_scale
    for kk in range(4):
        hidden_total[:, kk * width : (kk + 1) * width] = vec_sum[8 + kk : 9 + kk] * grad_scale


def emit(grad_scale, who, low, grad, qkv_sum, upout_sum, down_sum, vec_sum):
    toks, width = low.shape
    piece = qkv_sum.shape[1]
    shape = jax.ShapeDtypeStruct
    return pl.pallas_call(
        functools.partial(emit_body, grad_scale),
        name="emit",
        out_shape=(
            shape((toks, width), BF16), shape((toks, width), BF16), shape((piece, 3 * width), F32), shape((piece, width), F32), shape((piece, 4 * width), F32),
            shape(down_sum.shape, F32), shape((4, width), F32), shape((1, 4 * width), F32), shape((2, width), F32), shape((2, width), F32),
        ),
        in_specs=[SM] + [VM] * 6,
        out_specs=(VM,) * 10,
        compiler_params=pltpu.CompilerParams(vmem_limit_bytes=32 << 20),
    )(who, low, grad, qkv_sum, upout_sum, down_sum, vec_sum)


def local_tensor(tokens, segment_ids, qkv_weight, out_weight, up_weight, down_weight, proj_bias, hidden_bias, norm_gain, norm_shift, cotangent):
    inputs = tokens[0]
    toks, width = inputs.shape
    scale = (width // HEADS) ** (-0.5)
    grad_scale = (toks * lax.axis_size("fsdp") * lax.axis_size("rep")) ** (-0.5)
    queries, key_rows, value_rows, xs, w_full, upout = project(inputs, qkv_weight, up_weight, out_weight, proj_bias)
    attended, attended_low, lse = attn_fwd(scale, segment_ids, queries, key_rows, value_rows)
    low, branch_grad, grad_heads, vec, down, keep, to_x, to_y, to_d = middle(
        attended_low, inputs, cotangent[0], upout, down_weight, proj_bias, hidden_bias[None], norm_gain, norm_shift
    )
    grad, qkv_sum, upout_sum, down_sum, vec_sum = backward(
        scale, segment_ids, queries, key_rows, value_rows, grad_heads, attended, lse, xs, w_full, branch_grad, vec, down, keep, to_x, to_y, to_d
    )
    output, input_grad, qkv_total, out_total, up_total, down_total, bias_total, hidden_total, gain_total, shift_total = emit(
        grad_scale, (lax.axis_index("fsdp") // 2).reshape(1), low, grad, qkv_sum, upout_sum, down_sum, vec_sum
    )
    return (
        output[None],
        input_grad[None],
        qkv_total,
        out_total,
        up_total,
        down_total,
        bias_total,
        hidden_total.reshape(4 * width),
        gain_total,
        shift_total,
    )


def normalize(hidden, gain, shift):
    center = hidden - jnp.mean(hidden, axis=-1, keepdims=True)
    spread = jnp.mean(center * center, axis=-1, keepdims=True)
    return center * lax.rsqrt(spread + 1e-05) * gain + shift


def exact_gelu(value):
    return jax.nn.gelu(value, approximate=False)


def gather_attention(qkv_weight, out_weight):
    return (
        lax.all_gather(qkv_weight, "fsdp", axis=0, tiled=True),
        lax.all_gather(out_weight, "fsdp", axis=0, tiled=True),
    )


def gather_feedforward(up_weight, down_weight):
    return (
        lax.all_gather(up_weight, "fsdp", axis=0, tiled=True),
        lax.all_gather(down_weight, "fsdp", axis=0, tiled=True),
    )


def block_plan(row_count):
    block_rows = math.gcd(row_count, 1024)
    return (block_rows, row_count // block_rows)


def split_heads(matrix):
    return matrix.reshape(matrix.shape[0], HEADS, matrix.shape[1] // HEADS)


def join_heads(stacked):
    return jnp.transpose(stacked, (1, 0, 2)).reshape(
        stacked.shape[1], stacked.shape[0] * stacked.shape[2]
    )


def local_gather(
    tokens,
    segment_ids,
    qkv_weight,
    out_weight,
    up_weight,
    down_weight,
    proj_bias,
    hidden_bias,
    norm_gain,
    norm_shift,
    cotangent,
):
    inputs = tokens[0]
    tok_count, model_width = inputs.shape
    head_dim = model_width // HEADS
    score_scale = head_dim ** (-0.5)
    doc_ids = segment_ids[0]
    own_index = lax.axis_index("fsdp")
    own_docs = lax.dynamic_slice_in_dim(doc_ids, own_index * tok_count, tok_count)
    qkv_full, out_full = gather_attention(qkv_weight, out_weight)
    projected = jnp.dot(inputs, qkv_full, preferred_element_type=jnp.float32)
    queries = (projected[:, :model_width] + proj_bias[0]).astype(jnp.bfloat16)
    key_rows = projected[:, model_width : 2 * model_width].astype(jnp.bfloat16)
    value_rows = (projected[:, 2 * model_width :] + proj_bias[1]).astype(jnp.bfloat16)
    query_heads = split_heads(queries)
    key_own = split_heads(key_rows)
    value_own = split_heads(value_rows)
    initial = (
        jnp.zeros((HEADS, tok_count, head_dim), jnp.float32),
        jnp.full((HEADS, tok_count), NEGATIVE, jnp.float32),
        jnp.zeros((HEADS, tok_count), jnp.float32),
    )
    key_piece = lax.all_gather(key_rows, "fsdp", axis=0, tiled=True)
    value_piece = lax.all_gather(value_rows, "fsdp", axis=0, tiled=True)
    block_rows, blocks = block_plan(key_piece.shape[0])

    def forward_advance(block_index, running_state):
        weighted, running, denominator = running_state
        offset = block_index * block_rows
        key_block = split_heads(lax.dynamic_slice_in_dim(key_piece, offset, block_rows))
        value_block = split_heads(lax.dynamic_slice_in_dim(value_piece, offset, block_rows))
        block_docs = lax.dynamic_slice_in_dim(doc_ids, offset, block_rows)
        scores = (
            jnp.einsum("qhd,khd->hqk", query_heads, key_block, preferred_element_type=jnp.float32)
            * score_scale
        )
        same_doc = (own_docs[:, None] == block_docs[None, :])[None]
        highest = jnp.maximum(running, jnp.max(jnp.where(same_doc, scores, NEGATIVE), axis=2))
        factor = jnp.exp(running - highest)
        weights = jnp.where(same_doc, jnp.exp(scores - highest[:, :, None]), 0.0)
        denominator = denominator * factor + jnp.sum(weights, axis=2)
        weighted = weighted * factor[:, :, None] + jnp.einsum(
            "hqk,khd->hqd",
            weights.astype(jnp.bfloat16),
            value_block,
            preferred_element_type=jnp.float32,
        )
        return (weighted, highest, denominator)

    weighted, running, denominator = lax.fori_loop(0, blocks, forward_advance, initial)
    attended_heads = weighted / denominator[:, :, None]
    log_total = running + jnp.log(denominator)
    attended_low = join_heads(attended_heads).astype(jnp.bfloat16)
    branch = jnp.dot(attended_low, out_full, preferred_element_type=jnp.float32) + proj_bias[2]
    first_norm, norm_one_back = jax.vjp(
        normalize, inputs.astype(jnp.float32) + branch, norm_gain[0], norm_shift[0]
    )
    first_low = first_norm.astype(jnp.bfloat16)
    up_full, down_full = gather_feedforward(up_weight, down_weight)
    hidden_pre = jnp.dot(first_low, up_full, preferred_element_type=jnp.float32) + hidden_bias
    activated, gelu_back = jax.vjp(exact_gelu, hidden_pre)
    activated_low = activated.astype(jnp.bfloat16)
    second = jnp.dot(activated_low, down_full, preferred_element_type=jnp.float32) + proj_bias[3]
    output, norm_two_back = jax.vjp(normalize, first_norm + second, norm_gain[1], norm_shift[1])
    up_back, down_back = gather_feedforward(up_weight, down_weight)
    qkv_back, out_back = gather_attention(qkv_weight, out_weight)
    grad_second, gain_two, shift_two = norm_two_back(cotangent[0].astype(jnp.float32))
    second_low = grad_second.astype(jnp.bfloat16)
    down_term = jnp.einsum(
        "tf,td->fd", activated_low, second_low, preferred_element_type=jnp.float32
    )
    activated_grad = jnp.einsum(
        "td,fd->tf", second_low, down_back, preferred_element_type=jnp.float32
    )
    (pre_grad,) = gelu_back(activated_grad)
    pre_low = pre_grad.astype(jnp.bfloat16)
    up_term = jnp.einsum("td,tf->df", first_low, pre_low, preferred_element_type=jnp.float32)
    first_grad = grad_second + jnp.einsum(
        "tf,df->td", pre_low, up_back, preferred_element_type=jnp.float32
    )
    branch_grad, gain_one, shift_one = norm_one_back(first_grad)
    branch_low = branch_grad.astype(jnp.bfloat16)
    out_term = jnp.einsum("te,td->ed", attended_low, branch_low, preferred_element_type=jnp.float32)
    attended_grad = jnp.einsum(
        "td,ed->te", branch_low, out_back, preferred_element_type=jnp.float32
    ).astype(jnp.bfloat16)
    grad_heads = split_heads(attended_grad)
    correction = jnp.einsum("qhd,hqd->hq", grad_heads.astype(jnp.float32), attended_heads)
    lse_all, correction_all = (
        lax.all_gather(log_total, "fsdp", axis=1, tiled=True),
        lax.all_gather(correction, "fsdp", axis=1, tiled=True),
    )
    query_key_piece = lax.all_gather(key_rows, "fsdp", axis=0, tiled=True)
    query_value_piece = lax.all_gather(value_rows, "fsdp", axis=0, tiled=True)
    query_block_rows, blocks = block_plan(query_key_piece.shape[0])

    def query_advance(block_index, query_state):
        offset = block_index * query_block_rows
        key_block = split_heads(lax.dynamic_slice_in_dim(query_key_piece, offset, query_block_rows))
        value_block = split_heads(
            lax.dynamic_slice_in_dim(query_value_piece, offset, query_block_rows)
        )
        block_docs = lax.dynamic_slice_in_dim(doc_ids, offset, query_block_rows)
        scores = (
            jnp.einsum("qhd,khd->hqk", query_heads, key_block, preferred_element_type=jnp.float32)
            * score_scale
        )
        same_doc = (own_docs[:, None] == block_docs[None, :])[None]
        probabilities = jnp.where(same_doc, jnp.exp(scores - log_total[:, :, None]), 0.0)
        prob_grad = jnp.einsum(
            "qhd,khd->hqk", grad_heads, value_block, preferred_element_type=jnp.float32
        )
        score_grad = (probabilities * (prob_grad - correction[:, :, None])).astype(jnp.bfloat16)
        return query_state + jnp.einsum(
            "hqk,khd->hqd", score_grad, key_block, preferred_element_type=jnp.float32
        )

    query_acc = lax.fori_loop(
        0, blocks, query_advance, jnp.zeros((HEADS, tok_count, head_dim), jnp.float32)
    )
    query_grad = (join_heads(query_acc) * score_scale).astype(jnp.bfloat16)
    empty_heads = jnp.zeros((HEADS, tok_count, head_dim), jnp.float32)
    query_piece = lax.all_gather(queries, "fsdp", axis=0, tiled=True)
    grad_piece = lax.all_gather(attended_grad, "fsdp", axis=0, tiled=True)
    key_block_rows, blocks = block_plan(query_piece.shape[0])

    def key_advance(block_index, key_state):
        key_acc, value_acc = key_state
        offset = block_index * key_block_rows
        query_block = split_heads(lax.dynamic_slice_in_dim(query_piece, offset, key_block_rows))
        grad_block = split_heads(lax.dynamic_slice_in_dim(grad_piece, offset, key_block_rows))
        block_docs = lax.dynamic_slice_in_dim(doc_ids, offset, key_block_rows)
        lse_block = lax.dynamic_slice_in_dim(lse_all, offset, key_block_rows, axis=1)
        corr_block = lax.dynamic_slice_in_dim(correction_all, offset, key_block_rows, axis=1)
        scores = (
            jnp.einsum("qhd,khd->hqk", query_block, key_own, preferred_element_type=jnp.float32)
            * score_scale
        )
        same_doc = (block_docs[:, None] == own_docs[None, :])[None]
        probabilities = jnp.where(same_doc, jnp.exp(scores - lse_block[:, :, None]), 0.0)
        value_acc = value_acc + jnp.einsum(
            "hqk,qhd->hkd",
            probabilities.astype(jnp.bfloat16),
            grad_block,
            preferred_element_type=jnp.float32,
        )
        prob_grad = jnp.einsum(
            "qhd,khd->hqk", grad_block, value_own, preferred_element_type=jnp.float32
        )
        score_grad = (probabilities * (prob_grad - corr_block[:, :, None])).astype(jnp.bfloat16)
        key_acc = key_acc + jnp.einsum(
            "hqk,qhd->hkd", score_grad, query_block, preferred_element_type=jnp.float32
        )
        return (key_acc, value_acc)

    key_acc, value_acc = lax.fori_loop(0, blocks, key_advance, (empty_heads, empty_heads))
    key_grad = (join_heads(key_acc) * score_scale).astype(jnp.bfloat16)
    value_grad = join_heads(value_acc).astype(jnp.bfloat16)
    qkv_grad_low = jnp.concatenate([query_grad, key_grad, value_grad], axis=1)
    qkv_term = jnp.einsum("td,te->de", inputs, qkv_grad_low, preferred_element_type=jnp.float32)
    input_grad = branch_grad + jnp.einsum(
        "te,de->td", qkv_grad_low, qkv_back, preferred_element_type=jnp.float32
    )
    bias_term = jnp.stack(
        [
            jnp.sum(query_grad.astype(jnp.float32), axis=0),
            jnp.sum(value_grad.astype(jnp.float32), axis=0),
            jnp.sum(branch_low.astype(jnp.float32), axis=0),
            jnp.sum(second_low.astype(jnp.float32), axis=0),
        ]
    )
    hidden_term = jnp.sum(pre_low.astype(jnp.float32), axis=0)
    gain_term = jnp.stack([gain_one, gain_two])
    shift_term = jnp.stack([shift_one, shift_two])
    bias_total, hidden_total, gain_total, shift_total = lax.psum(
        (bias_term, hidden_term, gain_term, shift_term), ("rep", "fsdp")
    )
    up_sum, down_sum = (
        lax.psum_scatter(up_term, "fsdp", scatter_dimension=0, tiled=True),
        lax.psum_scatter(down_term, "fsdp", scatter_dimension=0, tiled=True),
    )
    qkv_sum, out_sum = (
        lax.psum_scatter(qkv_term, "fsdp", scatter_dimension=0, tiled=True),
        lax.psum_scatter(out_term, "fsdp", scatter_dimension=0, tiled=True),
    )
    qkv_total, out_total, up_total, down_total = lax.psum(
        (qkv_sum, out_sum, up_sum, down_sum), "rep"
    )
    grad_scale = (tok_count * lax.axis_size("fsdp") * lax.axis_size("rep")) ** (-0.5)
    return (
        output.astype(jnp.bfloat16)[None],
        input_grad.astype(jnp.bfloat16)[None],
        qkv_total * grad_scale,
        out_total * grad_scale,
        up_total * grad_scale,
        down_total * grad_scale,
        bias_total * grad_scale,
        hidden_total * grad_scale,
        gain_total * grad_scale,
        shift_total * grad_scale,
    )


def solution(mesh):
    small = mesh.shape["fsdp"] == 8 and mesh.shape["rep"] == 4
    local = local_tensor if small else local_gather
    return jax.shard_map(
        local,
        mesh=mesh,
        in_specs=(
            P("rep", "fsdp", None),
            P("rep", None),
            P("fsdp", None),
            P("fsdp", None),
            P("fsdp", None),
            P("fsdp", None),
            P(),
            P(),
            P(),
            P(),
            P("rep", "fsdp", None),
        ),
        out_specs=(
            P("rep", "fsdp", None),
            P("rep", "fsdp", None),
            P("fsdp", None),
            P("fsdp", None),
            P("fsdp", None),
            P("fsdp", None),
            P(),
            P(),
            P(),
            P(),
        ),
        check_vma=False,
    )
```

```python
import functools
import math

import jax
import jax.numpy as jnp
from jax import lax
from jax.experimental import pallas as pl
from jax.experimental.pallas import tpu as pltpu
from jax.sharding import PartitionSpec as P

HEADS = 16

NEGATIVE = -1e30
BQ = 256
BK = 512
VM = pl.BlockSpec(memory_space=pltpu.VMEM)
SM = pl.BlockSpec(memory_space=pltpu.SMEM)


def nt(a, b):
    return lax.dot_general(a, b, (((1,), (1,)), ((), ())), preferred_element_type=jnp.float32)


def nn(a, b):
    return jnp.dot(a, b, preferred_element_type=jnp.float32)


def head_lanes(shape, half):
    return lax.broadcasted_iota(jnp.int32, shape, 1) < half


def rows_of(index, size):
    return pl.ds(pl.multiple_of(index * size, size), size)


def seg_columns(seg_v, seg_c):
    length = seg_c.shape[0]

    @pl.loop(0, length // BQ)
    def _(i):
        rows = rows_of(i, BQ)
        seg_c[rows, :] = jnp.transpose(jnp.broadcast_to(seg_v[:, rows].astype(jnp.float32), (128, BQ)))


def wide(column, lanes):
    return jnp.concatenate([column] * (lanes // 128), axis=1)


MESH = pl.DeviceIdType.MESH
HBM = pl.BlockSpec(memory_space=pltpu.HBM)
F32 = jnp.float32
BF16 = jnp.bfloat16


def tn(a, b):
    return lax.dot_general(a, b, (((0,), (0,)), ((), ())), preferred_element_type=F32)


def fold_rows(v):
    return jnp.sum(v.reshape(v.shape[0] // 8, 8, v.shape[1]), axis=0)


class Wires:
    def __init__(self, send_sems, recv_sems, local_sems):
        self.send_sems, self.recv_sems, self.local_sems = send_sems, recv_sems, local_sems
        self.count = 0
        self.local_count = 0
        self.sent = []
        self.rep = lax.axis_index("rep")
        self.own = lax.axis_index("fsdp")

    def remote(self, src, dst, peer, rep=None):
        i = self.count
        self.count = i + 1
        return pltpu.make_async_remote_copy(
            src_ref=src, dst_ref=dst, send_sem=self.send_sems.at[i], recv_sem=self.recv_sems.at[i],
            device_id=(self.rep if rep is None else rep, peer), device_id_type=MESH,
        )

    def send(self, src, dst, peer):
        copy = self.remote(src, dst, peer)
        copy.start()
        self.sent.append(copy)
        return copy

    def local(self, src, dst):
        copy = pltpu.make_async_copy(src, dst, self.local_sems.at[self.local_count])
        self.local_count += 1
        copy.start()
        return copy

    def greet(self, peers):
        barrier = pltpu.get_barrier_semaphore()
        for rep, peer in peers:
            pl.semaphore_signal(barrier, inc=1, device_id=(rep, peer), device_id_type=MESH)
        pl.semaphore_wait(barrier, len(peers))

    def drain(self, copies):
        for copy in copies:
            copy.wait_send()
            self.sent = [other for other in self.sent if other is not copy]

    def finish(self):
        for copy in self.sent:
            copy.wait_send()


class Line:
    def __init__(self, wires, own, land, far, count, size=None):
        self.own, self.land, self.far = own, land, far
        rep, dev = wires.rep, wires.own
        size = own.shape[0] // count if size is None else size
        self.rows = [pl.ds(i * size, size) for i in range(count)]
        self.inner = jnp.logical_or(rep == 1, rep == 2)
        self.outer = jnp.logical_not(self.inner)
        near, across = lax.bitwise_xor(rep, 1), lax.bitwise_xor(rep, 3)
        self.first = [wires.remote(own.at[r], land.at[r], dev, near) for r in self.rows]
        self.middle = [wires.remote(own.at[r], far.at[r], dev, across) for r in self.rows]
        self.back = [wires.remote(land.at[r], land.at[r], dev, near) for r in self.rows]

    def start(self):
        @pl.when(self.outer)
        def _():
            for copy in self.first:
                copy.start()

    def collect(self, which):
        @pl.when(self.inner)
        def _():
            for i in which:
                r = self.rows[i]
                self.first[i].wait_recv()
                self.own[r, :] = (self.own[r, :].astype(F32) + self.land[r, :].astype(F32)).astype(BF16)
                self.middle[i].start()

    def total(self, which):
        @pl.when(self.inner)
        def _():
            for i in which:
                r = self.rows[i]
                self.middle[i].wait_recv()
                self.land[r, :] = (self.own[r, :].astype(F32) + self.far[r, :].astype(F32)).astype(BF16)
                self.back[i].start()

    def arrive(self, which):
        @pl.when(self.outer)
        def _():
            for i in which:
                self.back[i].wait_recv()

    def finish(self):
        @pl.when(self.outer)
        def _():
            for copy in self.first:
                copy.wait_send()

        @pl.when(self.inner)
        def _():
            for i in range(len(self.rows)):
                self.middle[i].wait_send()
                self.back[i].wait_send()


class Hops:
    def __init__(self, wires, view):
        rep, reps = wires.rep, 4
        self.all = []
        for hop in range(1, reps):
            for step in (1, -1):
                index, to, come = rep - step * (hop - 1), rep + step, rep - step * hop
                going = (index >= 0) & (index < reps) & (to >= 0) & (to < reps)
                coming = (come >= 0) & (come < reps)
                refs = view(jnp.clip(index, 0, reps - 1))
                copies = [wires.remote(ref, ref, wires.own, jnp.clip(to, 0, reps - 1)) for ref in refs]
                self.all.append((hop, going, coming, copies))

    def each(self, hop, kind):
        for at, going, coming, copies in self.all:
            if hop in (0, at):

                @pl.when(coming if kind == "wait_recv" else going)
                def _():
                    for copy in copies:
                        getattr(copy, kind)()

    def start(self, hop):
        self.each(hop, "start")

    def wait(self, hop):
        self.each(hop, "wait_recv")

    def finish(self):
        self.each(0, "wait_send")


class Spread:
    def __init__(self, wires, slots, half):
        self.wires, self.slots, self.half = wires, slots, half
        self.chip = wires.own // 2
        self.x, self.y = lax.bitwise_xor(wires.own, 2), lax.bitwise_xor(wires.own, 4)
        self.cx, self.cy, self.cd = (lax.bitwise_xor(self.chip, m) for m in (1, 2, 3))
        self.a, self.b = pl.ds(0, half), pl.ds(half, half)

    def piece(self, chip, part):
        return self.slots.at[chip, part]

    def put(self, chip, part, peer):
        return self.wires.send(self.piece(chip, part), self.piece(chip, part), peer)

    def first_half(self):
        self.xa = self.put(self.chip, self.a, self.x)
        self.ya = self.put(self.chip, self.a, self.y)

    def second_half(self):
        self.yb = self.put(self.chip, self.b, self.y)
        self.xb = self.put(self.chip, self.b, self.x)

    def relay(self):
        self.xa.wait_recv()
        self.da = self.put(self.cx, self.a, self.y)
        self.yb.wait_recv()
        self.db = self.put(self.cy, self.b, self.x)

    def wait_sides(self):
        self.xb.wait_recv()
        self.ya.wait_recv()

    def wait_diagonal(self):
        self.da.wait_recv()
        self.db.wait_recv()


class Gather:
    def __init__(self, wires, part, side, last, half):
        self.wires, self.part, self.side, self.last, self.half = wires, part, side, last, half
        self.chip = wires.own // 2
        self.x, self.y = lax.bitwise_xor(wires.own, 2), lax.bitwise_xor(wires.own, 4)
        self.cx, self.cy, self.cd = (lax.bitwise_xor(self.chip, m) for m in (1, 2, 3))
        self.a, self.b = pl.ds(0, half), pl.ds(half, half)

    def send_x(self):
        self.x_own = self.wires.send(self.part.at[self.cx, self.a], self.side.at[0], self.x)

    def send_y(self):
        self.y_own = self.wires.send(self.part.at[self.cy, self.b], self.side.at[1], self.y)

    def send_diagonal(self):
        self.x_far = self.wires.send(self.part.at[self.cd, self.a], self.side.at[2], self.x)
        self.y_far = self.wires.send(self.part.at[self.cd, self.b], self.side.at[3], self.y)

    def relay(self):
        step = 32

        def add(chip, start, slot):
            @pl.loop(0, self.half // step)
            def _(t):
                rows = pl.ds(pl.multiple_of(start + t * step, step), step)
                near = self.part[chip, rows, :].astype(F32) + self.side[slot, rows_of(t, step), :].astype(F32)
                self.part[chip, rows, :] = near.astype(BF16)

        self.x_far.wait_recv()
        add(self.cy, 0, 2)
        self.y_last = self.wires.send(self.part.at[self.cy, self.a], self.last.at[0], self.y)
        self.y_far.wait_recv()
        add(self.cx, self.half, 3)
        self.x_last = self.wires.send(self.part.at[self.cx, self.b], self.last.at[1], self.x)

    def drain(self):
        for copy in (self.x_own, self.y_own, self.x_far, self.y_far, self.x_last, self.y_last):
            copy.wait_send()
            self.wires.sent = [other for other in self.wires.sent if other is not copy]

    def wait_first(self):
        self.x_own.wait_recv()
        self.y_last.wait_recv()

    def wait_second(self):
        self.y_own.wait_recv()
        self.x_last.wait_recv()

    def total(self, which, offset, size):
        rows = pl.ds(pl.multiple_of(which * self.half + offset, size), size)
        here = pl.ds(pl.multiple_of(offset, size), size)
        return self.part[self.chip, rows, :].astype(F32) + self.side[which, here, :].astype(F32) + self.last[which, here, :].astype(F32)


def layer_body(
    scale, seg, x, cot, qkv_w, up_w, out_w, down_w, proj_bias, hidden_bias, gain, shift,
    h_output, h_input_grad, h_qkv, h_upout, h_down, h_vec,
    q_out, k_out, v_out, o_out, lse, xs, w_full, output, branch_grad, grad_heads, vec, down_grad, sends,
    stage, vt, seg_c, low, att, out_full, up_full, down_full, h1, z1, r1, fl, act, slope, part, side, last, sl, pre,
    branch_low, agl, acc, d_send, d_recv, d_far, down_sum, u_send, u_recv, o_send, o_recv,
    corr, dv_acc, dqt, q_send, q_recv, q_piece, l_own, l_far, got, y_own, y_far, upout_sum, qkv_sum, input_grad, v_sum, v_recv, vec_sum,
    send_sems, recv_sems, local_sems,
):
    w = Wires(send_sems, recv_sems, local_sems)
    own, rep = w.own, w.rep
    core, chip = lax.rem(own, 2), own // 2
    mate = lax.bitwise_xor(own, 1)
    cx, cy, cd = (lax.bitwise_xor(chip, m) for m in (1, 2, 3))
    others = (cd, cx, cy)
    toks, width = x.shape
    ff = up_full.shape[1]
    share = width // 4
    head_width = share // 2
    half = toks // 2
    piece = up_w.shape[0]
    quarter = piece // 4
    tile = 256
    w.greet(
        [(rep, lax.bitwise_xor(own, m)) for m in range(1, 8)]
        + [(lax.bitwise_xor(rep, m), own) for m in (1, 2, 3)]
    )

    mine, some = rows_of(own, piece), rows_of(rep, quarter)

    def quarter_of(full, k, r, cols=slice(None)):
        return full.at[pl.ds(pl.multiple_of((2 * k + core) * piece + r * quarter, quarter), quarter), cols]

    def qkv_cols(p, to_chip):
        return pl.ds(pl.multiple_of(p * width + to_chip * share, share), share)

    first_fetch = []
    for mask in (6, 2, 4):
        peer, to_chip = lax.bitwise_xor(own, mask), lax.bitwise_xor(chip, mask // 2)
        for p in range(3):
            first_fetch.append(w.send(qkv_w.at[some, qkv_cols(p, to_chip)], quarter_of(w_full, chip, rep, pl.ds(p * share, share)), peer))
    xs[chip] = x[...]
    spread0 = Spread(w, xs, half)
    spread0.first_half()
    spread0.second_half()
    fetch = []
    for mask in (6, 2, 4):
        peer, to_chip = lax.bitwise_xor(own, mask), lax.bitwise_xor(chip, mask // 2)
        fetch.append(w.send(up_w.at[some, rows_of(to_chip, ff)], quarter_of(up_full, chip, rep), peer))
        fetch.append(w.send(out_w.at[some], quarter_of(out_full, chip, rep), peer))
    here, there = [], []
    for p in range(3):
        src, dst = qkv_w.at[:, qkv_cols(p, chip)], w_full.at[mine, pl.ds(p * share, share)]
        here.append(w.local(src, dst))
        there.append(w.send(src, dst, mate))
    kept = []
    for src, dst in ((up_w.at[:, rows_of(chip, ff)], up_full.at[mine]), (out_w, out_full.at[mine]), (down_w, down_full.at[rows_of(core, ff // 2)])):
        kept.append((w.local(src, dst), w.send(src, dst, mate)))
    qkv_hops = Hops(w, lambda r: [quarter_of(w_full, k, r) for k in others])
    hops = Hops(w, lambda r: [quarter_of(full, k, r) for full in (up_full, out_full) for k in others])
    for copy in first_fetch:
        copy.wait_recv()
    qkv_hops.start(1)
    seg_columns(seg, seg_c)
    qkv_hops.wait(1)
    qkv_hops.start(2)
    spread0.relay()
    qkv_hops.wait(2)
    qkv_hops.start(3)
    for copy in fetch:
        copy.wait_recv()
    hops.start(1)
    qkv_hops.wait(3)
    for k in others:
        rows = rows_of(2 * k + core, piece)
        there.append(w.send(w_full.at[rows], w_full.at[rows], mate))
    for copy in here:
        copy.wait()
    for copy in there:
        copy.wait_recv()

    outs = (q_out, k_out, v_out)
    trades = []

    def block(k):
        rows = rows_of(2 * k + core, toks)
        for p in range(3):
            r = nn(xs[k], w_full[:, pl.ds(p * share, share)])
            if p != 1:
                r = r + proj_bias[p // 2 : p // 2 + 1, rows_of(chip, share)]
            stage[k, :, pl.ds(p * share, share)] = r.astype(BF16)
            theirs = pl.ds(pl.multiple_of(p * share + (1 - core) * head_width, head_width), head_width)
            trades.append(w.send(stage.at[k, :, theirs], outs[p].at[rows], mate))
            outs[p][rows, :] = stage[k, :, pl.ds(pl.multiple_of(p * share + core * head_width, head_width), head_width)]

    block(chip)
    spread0.wait_sides()
    block(cx)
    block(cy)
    hops.wait(1)
    hops.start(2)
    spread0.wait_diagonal()
    block(cd)
    for copy in trades:
        copy.wait_recv()
    w.drain(trades)

    headd = head_width // 2
    blocks = q_out.shape[0] // BQ
    first = head_lanes((BQ, head_width), headd)

    @pl.loop(0, blocks)
    def _(i):
        rows = rows_of(i, BQ)
        t = jnp.transpose(v_out[rows, :])
        for h in range(2):
            vt[h, 0:headd, rows] = t[h * headd : (h + 1) * headd]
            vt[h, headd : headd + 16, rows] = jnp.ones((16, BQ), BF16)

    swaps = {}
    for mask in range(1, 8):
        peer = lax.bitwise_xor(own, mask)
        swaps[mask] = w.remote(low.at[rows_of(peer, toks)], att.at[:, rows_of(own, head_width)], peer)

    @pl.loop(0, blocks)
    def _(t):
        i = lax.bitwise_xor(own, 7 - t)
        rows = rows_of(i, BQ)
        qb = q_out[rows, :] * jnp.bfloat16(scale)
        zero = jnp.zeros_like(qb)
        qs = (jnp.where(first, qb, zero), jnp.where(first, zero, qb))
        seg_q = seg[:, rows].astype(F32)
        both = []
        for h in range(2):
            scores = []
            for j in range(blocks):
                cols = pl.ds(j * BQ, BQ)
                same = wide(seg_c[cols, :], BQ) == seg_q
                scores.append(jnp.where(same, nt(k_out[cols, :], qs[h]), NEGATIVE))
            top = functools.reduce(jnp.maximum, [jnp.max(s, axis=0, keepdims=True) for s in scores])
            total = jnp.zeros((headd + 16, BQ), F32)
            for j in range(blocks):
                total = total + nn(vt[h, :, pl.ds(j * BQ, BQ)], jnp.exp(scores[j] - top).astype(BF16))
            norm = total[headd : headd + 1]
            both.append(total[0:headd] / norm)
            lse[h : h + 1, rows] = top + jnp.log(norm)
        out = jnp.transpose(jnp.concatenate(both, axis=0))
        o_out[rows, :] = out
        low[rows, :] = out.astype(BF16)
        for mask in range(1, 8):

            @pl.when(t == 7 - mask)
            def _(mask=mask):
                swaps[mask].start()

        @pl.when(t == 2)
        def _():
            hops.wait(2)
            hops.start(3)

    w.sent.extend(swaps.values())
    att[:, rows_of(own, head_width)] = low[rows_of(own, toks), :]
    hops.wait(3)
    for k in others:
        rows = rows_of(2 * k + core, piece)
        for full in (out_full, up_full):
            kept.append((None, w.send(full.at[rows], full.at[rows], mate)))
    for local, remote in kept:
        if local is not None:
            local.wait()
        remote.wait_recv()
    for copy in swaps.values():
        copy.wait_recv()

    @pl.loop(0, width // tile)
    def _(n):
        cols = rows_of(n, tile)
        h1[:, cols] = nn(att[...], out_full[:, cols]) + proj_bias[2:3, cols] + x[:, cols].astype(F32)

    step = 32
    acc[...] = jnp.zeros_like(acc)

    def first_rows(t):
        rows = rows_of(t, step)
        v = h1[rows, :]
        center = v - jnp.mean(v, axis=1, keepdims=True)
        inv = lax.rsqrt(jnp.mean(center * center, axis=1, keepdims=True) + 1e-05)
        z = center * inv
        z1[rows, :] = z
        r1[rows, :] = jnp.broadcast_to(inv, (step, 128))
        fl[chip, rows, :] = (z * gain[0:1, :] + shift[0:1, :]).astype(BF16)

    spread = Spread(w, fl, half)
    pl.loop(0, half // step)(first_rows)
    spread.first_half()
    pl.loop(half // step, toks // step)(first_rows)
    spread.second_half()

    def forward(k):
        @pl.loop(0, ff // tile)
        def _(n):
            cols = rows_of(n, tile)
            hidden = nn(fl[k], up_full[:, cols]) + hidden_bias[:, pl.ds(pl.multiple_of(chip * ff + n * tile, tile), tile)]
            cdf = 0.5 * (1.0 + lax.erf(hidden * (2.0**-0.5)))
            act[k, :, cols] = (hidden * cdf).astype(BF16)
            slope[k, :, cols] = (cdf + hidden * (jnp.exp(-0.5 * hidden * hidden) * ((2.0 * math.pi) ** -0.5))).astype(BF16)

        @pl.loop(0, width // tile)
        def _(n):
            cols = rows_of(n, tile)
            part[k, :, cols] = nn(act[k], down_full[:, cols]).astype(BF16)

    forward(chip)
    gather = Gather(w, part, side, last, half)
    spread.relay()
    spread.wait_sides()
    forward(cx)
    gather.send_x()
    forward(cy)
    gather.send_y()
    spread.wait_diagonal()
    forward(cd)
    gather.send_diagonal()

    gather.relay()

    def second_rows(which, t):
        rows = pl.ds(pl.multiple_of(which * half + t * step, step), step)
        v = z1[rows, :] * gain[0:1, :] + shift[0:1, :] + gather.total(which, t * step, step) + proj_bias[3:4, :]
        center = v - jnp.mean(v, axis=1, keepdims=True)
        inv = lax.rsqrt(jnp.mean(center * center, axis=1, keepdims=True) + 1e-05)
        z = center * inv
        output[rows, :] = (z * gain[1:2, :] + shift[1:2, :]).astype(BF16)
        c = cot[rows, :].astype(F32)
        e = c * gain[1:2, :]
        grad = inv * (e - jnp.mean(e, axis=1, keepdims=True) - z * jnp.mean(e * z, axis=1, keepdims=True))
        h1[rows, :] = grad
        low = grad.astype(BF16)
        sl[chip, rows, :] = low
        acc[0] += fold_rows(c * z)
        acc[1] += fold_rows(c)
        acc[2] += fold_rows(low.astype(F32))

    spread2 = Spread(w, sl, half)
    gather.wait_first()
    pl.loop(0, half // step)(functools.partial(second_rows, 0))
    spread2.first_half()
    gather.wait_second()
    pl.loop(0, half // step)(functools.partial(second_rows, 1))
    spread2.second_half()

    def backward(k):
        @pl.loop(0, ff // tile)
        def _(n):
            cols = rows_of(n, tile)
            grad = nt(sl[k], down_full[cols, :]) * slope[k, :, cols].astype(F32)
            low = grad.astype(BF16)
            pre[k, :, cols] = low
            acc[3, :, cols] += fold_rows(low.astype(F32))

        @pl.loop(0, width // tile)
        def _(n):
            cols = rows_of(n, tile)
            part[k, :, cols] = nt(pre[k], up_full[cols, :]).astype(BF16)

    gather.drain()
    backward(chip)
    gather2 = Gather(w, part, side, last, half)
    spread2.relay()
    spread2.wait_sides()
    backward(cx)
    gather2.send_x()
    backward(cy)
    gather2.send_y()
    spread2.wait_diagonal()
    backward(cd)
    gather2.send_diagonal()

    def down_rows(which, n):
        cols = pl.ds(pl.multiple_of(which * (ff // 2) + n * tile, tile), tile)
        lhs = act[:, :, cols].reshape(4 * toks, tile)
        return tn(lhs, sl[...].reshape(4 * toks, width))

    @pl.loop(0, ff // 2 // tile)
    def _(n):
        d_send[rows_of(n, tile), :] = down_rows(1 - core, n).astype(BF16)

    d_copy = w.send(d_send, d_recv, mate)
    d_copy.wait_recv()

    @pl.loop(0, ff // 2 // tile)
    def _(n):
        rows = rows_of(n, tile)
        down_grad[rows, :] = (down_rows(core, n) + d_recv[rows, :].astype(F32)).astype(BF16)

    down_line = Line(w, down_grad, down_sum, d_far, 8)
    down_line.start()
    gather2.relay()

    def up_rows(which, k):
        cols = pl.ds(pl.multiple_of((2 * k + which) * piece, piece), piece)
        lhs = fl[:, :, cols].reshape(4 * toks, piece)
        return tn(lhs, pre[...].reshape(4 * toks, ff))

    @pl.loop(0, 4)
    def _(k):
        u_send[k] = up_rows(1 - core, k).astype(BF16)

    u_copy = w.send(u_send, u_recv, mate)
    down_line.collect((0,))

    def branch_rows(which, t):
        rows = pl.ds(pl.multiple_of(which * half + t * step, step), step)
        grad = h1[rows, :] + gather2.total(which, t * step, step)
        z = z1[rows, :]
        e = grad * gain[0:1, :]
        out = r1[rows, 0:1] * (e - jnp.mean(e, axis=1, keepdims=True) - z * jnp.mean(e * z, axis=1, keepdims=True))
        branch_grad[rows, :] = out
        low = out.astype(BF16)
        branch_low[rows, :] = low
        acc[4] += fold_rows(grad * z)
        acc[5] += fold_rows(grad)
        acc[6] += fold_rows(low.astype(F32))

    gather2.wait_first()
    pl.loop(0, half // step)(functools.partial(branch_rows, 0))
    down_line.collect((1,))
    gather2.wait_second()
    pl.loop(0, half // step)(functools.partial(branch_rows, 1))

    @pl.loop(0, width // tile)
    def _(n):
        cols = rows_of(n, tile)
        agl[:, cols] = nt(branch_low[...], out_full[cols, :]).astype(BF16)

    backs = []
    for m in (6, 2, 4, 1, 3, 5, 7):
        peer = lax.bitwise_xor(own, m)
        backs.append(w.send(agl.at[:, rows_of(peer, head_width)], grad_heads.at[rows_of(own, toks)], peer))
    grad_heads[rows_of(own, toks), :] = agl[:, rows_of(own, head_width)]

    down_line.collect((2,))
    down_line.total((0,))
    u_copy.wait_recv()
    spread_up, spread_out = [], []

    def up_piece(m):
        k = lax.bitwise_xor(chip, m)
        return (up_rows(core, k) + u_recv[k].astype(F32)).astype(BF16)

    y_own[0:piece, :] = up_piece(0)
    y_own[piece : 2 * piece, :] = up_piece(3)
    up_line = Line(w, y_own.at[pl.ds(0, 2 * piece)], upout_sum.at[pl.ds(0, 2 * piece)], y_far.at[pl.ds(0, 2 * piece)], 4)
    up_line.start()
    for i, m in ((1, 1), (2, 2)):
        sends[i, 0] = up_piece(m)
        spread_up.append(w.send(sends.at[i, 0], got.at[i, 0], lax.bitwise_xor(own, 2 * m)))
    down_line.collect((3,))
    down_line.total((1,))

    def out_rows(which, k):
        cols = pl.ds(pl.multiple_of((2 * k + which) * piece, piece), piece)
        return tn(att[:, cols], branch_low[...])

    @pl.loop(0, 4)
    def _(k):
        o_send[k] = out_rows(1 - core, k).astype(BF16)

    o_copy = w.send(o_send, o_recv, mate)
    o_copy.wait_recv()
    for i, m in enumerate((3, 1, 2, 0)):
        k = lax.bitwise_xor(chip, m)
        sends[i, 1] = (out_rows(core, k) + o_recv[k].astype(F32)).astype(BF16)
        if m:
            spread_out.append(w.send(sends.at[i, 1], got.at[i, 1], lax.bitwise_xor(own, 2 * m)))
    down_line.collect((4, 5))
    down_line.total((2, 3))

    vec[...] = jnp.zeros_like(vec)
    for row, slot in ((2, 6), (3, 2), (4, 4), (5, 0), (6, 5), (7, 1)):
        vec[row : row + 1, :] = jnp.sum(acc[slot], axis=0, keepdims=True)
    hidden_sum = jnp.sum(acc[3], axis=0, keepdims=True)
    for k in range(4):
        vec[8 + k : 9 + k, :] = jnp.where(chip == k, hidden_sum, jnp.zeros_like(hidden_sum))
    for copy in backs:
        copy.wait_recv()

    got_up, got_out = spread_up, spread_out
    side_line = Line(w, y_own.at[pl.ds(2 * piece, 2 * piece)], upout_sum.at[pl.ds(2 * piece, 2 * piece)], y_far.at[pl.ds(2 * piece, 2 * piece)], 4)
    out_line = Line(w, y_own.at[pl.ds(4 * piece, piece)], upout_sum.at[pl.ds(4 * piece, piece)], y_far.at[pl.ds(4 * piece, piece)], 2)
    lines = [Line(w, l_own.at[p], qkv_sum.at[p], l_far.at[p], 4) for p in range(3)]

    def side_start():
        for copy in got_up:
            copy.wait_recv()
        for row, i in ((2, 1), (3, 2)):
            y_own[row * piece : (row + 1) * piece, :] = got[i, 0]
        side_line.start()

    def out_start():
        for copy in got_out:
            copy.wait_recv()
        y_own[4 * piece :, :] = (sends[3, 1].astype(F32) + got[0, 1].astype(F32) + got[1, 1].astype(F32) + got[2, 1].astype(F32)).astype(BF16)
        out_line.start()

    hooks = {
        0: lambda: (down_line.collect((6, 7)), down_line.total((4, 5))),
        1: lambda: down_line.total((6,)),
        2: lambda: up_line.collect((0,)),
        3: lambda: (side_start(), down_line.total((7,))),
        4: lambda: (up_line.collect((1,)), up_line.total((0,))),
        6: lambda: (up_line.collect((2,)), up_line.total((1,))),
        7: lambda: (up_line.collect((3,)), up_line.total((2,))),
    }

    grads = stage

    def head_cols_of(p, core_index):
        return pl.ds(pl.multiple_of((2 * p + core_index) * head_width, head_width), head_width)

    length, head_cols = q_out.shape
    q, k, v, g, o = q_out, k_out, v_out, grad_heads, o_out
    dk_acc = o_out

    @pl.loop(0, blocks)
    def _(i):
        rows = rows_of(i, BQ)
        prod = jnp.transpose(g[rows, :].astype(F32) * o[rows, :])
        corr[0:1, rows] = jnp.sum(prod[:headd], axis=0, keepdims=True)
        corr[1:2, rows] = jnp.sum(prod[headd:], axis=0, keepdims=True)
        t = jnp.transpose(k[rows, :])
        for h in range(2):
            vt[h, 0:headd, rows] = t[h * headd : (h + 1) * headd]
        dk_acc[rows, :] = jnp.zeros((BQ, head_cols), F32)
        dv_acc[rows, :] = jnp.zeros((BQ, head_cols), F32)

    @pl.loop(0, blocks)
    def _(i):
        rows = rows_of(i, BQ)
        qb = q[rows, :] * jnp.bfloat16(scale)
        gb = g[rows, :]
        zero = jnp.zeros_like(qb)
        qs = (jnp.where(first, qb, zero), jnp.where(first, zero, qb))
        gs = (jnp.where(first, gb, zero), jnp.where(first, zero, gb))
        qz = jnp.concatenate(qs, axis=0)
        gz = jnp.concatenate(gs, axis=0)
        seg_q = seg[:, rows].astype(F32)
        dq = [jnp.zeros((headd, BQ), F32)] * 2
        for j in range(length // BK):
            cols = pl.ds(j * BK, BK)
            kb = k[cols, :]
            vb = v[cols, :]
            same = wide(seg_c[cols, :], BQ) == seg_q
            ps, ds = [], []
            for h in range(2):
                s = jnp.where(same, nt(kb, qs[h]), NEGATIVE)
                p = jnp.exp(s - lse[h : h + 1, rows])
                dp = nt(vb, gs[h])
                dscore = (p * (dp - corr[h : h + 1, rows])).astype(BF16)
                ps.append(p.astype(BF16))
                ds.append(dscore)
                dq[h] = dq[h] + nn(vt[h, 0:headd, cols], dscore)
            dv_acc[cols, :] += nn(jnp.concatenate(ps, axis=1), gz)
            dk_acc[cols, :] += nn(jnp.concatenate(ds, axis=1), qz)
        dqt[0:headd, :] = dq[0]
        dqt[headd:, :] = dq[1]
        act[i // 2, :, head_cols_of(0, lax.rem(i, 2))] = (jnp.transpose(dqt[...]) * scale).astype(BF16)
        for at, hook in hooks.items():

            @pl.when(i == at)
            def _(hook=hook):
                hook()

    @pl.loop(0, blocks)
    def _(i):
        rows = rows_of(i, BQ)
        act[i // 2, :, head_cols_of(1, lax.rem(i, 2))] = dk_acc[rows, :].astype(BF16)
        act[i // 2, :, head_cols_of(2, lax.rem(i, 2))] = dv_acc[rows, :].astype(BF16)

    gather2.drain()
    swaps = []
    for p in range(3):
        cols = pl.ds(pl.multiple_of(p * share + core * head_width, head_width), head_width)
        swaps.append(w.send(act.at[:, :, head_cols_of(p, 1 - core)], grads.at[:, :, cols], mate))
        grads[:, :, cols] = act[:, :, head_cols_of(p, core)]
    v_sum[...] = vec[...]
    for row, p in ((0, 0), (1, 2)):
        total = jnp.sum(act[:, :, 2 * p * head_width : 2 * (p + 1) * head_width].reshape(4 * toks, 2 * head_width).astype(F32), axis=0, keepdims=True)
        total = total[:, 0:head_width] + total[:, head_width:]
        v_sum[row : row + 1, rows_of(own, head_width)] = total
    rounds = [(None, mate), (None, lax.bitwise_xor(own, 2)), (None, lax.bitwise_xor(own, 4)), (lax.bitwise_xor(rep, 1), own), (lax.bitwise_xor(rep, 2), own)]
    flying = []

    def vec_start(i):
        copy = w.remote(v_sum.at[...] if i == 0 else v_recv.at[4 + i], v_recv.at[i], rounds[i][1], rounds[i][0])
        copy.start()
        w.sent.append(copy)
        flying.append(copy)

    def vec_step(i):
        flying[i].wait_recv()
        base = v_sum[...] if i == 0 else v_recv[4 + i]
        if i < 4:
            v_recv[5 + i] = base + v_recv[i]
            vec_start(i + 1)
        else:
            vec_sum[...] = base + v_recv[i]

    vec_start(0)

    def qkv_rows(which, kk, p):
        cols = pl.ds(pl.multiple_of((2 * kk + which) * piece, piece), piece)
        return tn(xs[:, :, cols].reshape(4 * toks, piece), grads[:, :, p * share : (p + 1) * share].reshape(4 * toks, share))

    def theirs(p):
        @pl.loop(0, 4)
        def _(kk):
            q_send[p, kk] = qkv_rows(1 - core, kk, p).astype(BF16)

        return w.send(q_send.at[p], q_recv.at[p], mate)

    moved = []

    def pieces(p, copy):
        copy.wait_recv()

        @pl.loop(0, 4)
        def _(kk):
            q_piece[p, kk] = (qkv_rows(core, kk, p) + q_recv[p, kk].astype(F32)).astype(BF16)

        cols = rows_of(chip, share)
        moved.append([w.send(q_piece.at[p, lax.bitwise_xor(chip, m // 2)], l_own.at[p, :, cols], lax.bitwise_xor(own, m)) for m in (6, 2, 4)])
        l_own[p, :, cols] = q_piece[p, chip]

    def line_start(p):
        for copy in moved[p]:
            copy.wait_recv()
        lines[p].start()

    swaps[0].wait_recv()
    copies = [theirs(0)]
    up_line.total((3,))
    side_line.collect((0,))
    swaps[1].wait_recv()
    copies.append(theirs(1))
    pieces(0, copies[0])
    out_start()
    swaps[2].wait_recv()
    copies.append(theirs(2))
    pieces(1, copies[1])
    side_line.collect((1,))
    side_line.total((0,))
    up_line.arrive(range(4))
    far_copy = w.send(upout_sum.at[pl.ds(piece, piece)], got.at[0, 0], lax.bitwise_xor(own, 6))
    pieces(2, copies[2])
    side_line.collect((2,))
    side_line.total((1,))
    vec_step(0)

    def partial(kk):
        @pl.loop(0, width // tile)
        def _(n):
            cols = rows_of(n, tile)
            part[kk, :, cols] = nt(grads[kk], w_full[cols, :]).astype(BF16)

    gather = Gather(w, part, side, last, half)
    partial(gather.cd)
    gather.send_diagonal()
    side_line.collect((3,))
    side_line.total((2,))
    partial(gather.cx)
    gather.send_x()
    line_start(0)
    partial(gather.cy)
    gather.send_y()
    line_start(1)
    out_line.collect((0,))
    side_line.total((3,))
    partial(chip)
    line_start(2)
    out_line.collect((1,))
    out_line.total((0,))
    vec_step(1)
    out_line.total((1,))
    gather.relay()
    vec_step(2)
    step = 32

    def final_rows(which, t):
        rows = pl.ds(pl.multiple_of(which * half + t * step, step), step)
        input_grad[rows, :] = (branch_grad[rows, :] + gather.total(which, t * step, step)).astype(BF16)

    order = [(p, i) for p in range(3) for i in range(4)]

    def hop(at):
        if at < len(order):
            lines[order[at][0]].collect((order[at][1],))
        if at >= 2:
            lines[order[at - 2][0]].total((order[at - 2][1],))

    for at in range(5):
        hop(at)
    vec_step(3)
    gather.wait_first()
    pl.loop(0, half // step)(functools.partial(final_rows, 0))
    for at in range(5, 8):
        hop(at)
    vec_step(4)
    gather.wait_second()
    pl.loop(0, half // step)(functools.partial(final_rows, 1))
    for at in range(8, len(order) + 2):
        hop(at)
    down_line.arrive(range(8))
    spill = [w.local(down_sum, h_down)]
    side_line.arrive(range(4))
    out_line.arrive(range(2))
    far_copy.wait_recv()
    for to, src_ref in ((0, upout_sum.at[pl.ds(0, piece)]), (1, got.at[0, 0])):
        spill.append(w.local(src_ref, h_upout.at[pl.ds(to * piece, piece)]))
    spill.append(w.local(upout_sum.at[pl.ds(2 * piece, 3 * piece)], h_upout.at[pl.ds(2 * piece, 3 * piece)]))
    for p in range(3):
        lines[p].arrive(range(4))
        spill.append(w.local(qkv_sum.at[p], h_qkv.at[p]))
    spill += [w.local(s, d) for s, d in ((output, h_output), (input_grad, h_input_grad), (vec_sum, h_vec))]
    for line in [down_line, up_line, side_line, out_line] + lines:
        line.finish()
    for copy in spill:
        copy.wait()
    qkv_hops.finish()
    hops.finish()
    w.finish()


def layer(scale, seg, x, cot, qkv_w, up_w, out_w, down_w, proj_bias, hidden_bias, gain, shift):
    toks, width = x.shape
    piece = up_w.shape[0]
    ff = 2 * down_w.shape[0]
    half = toks // 2
    share = width // 4
    head_width = width // 8
    length = 8 * toks
    shape = jax.ShapeDtypeStruct
    vm = pltpu.VMEM
    five = (5 * piece, width)
    small = vm((3, 4, piece, share), BF16)
    three = (3, piece, width)
    rows4 = vm((4, toks, width), BF16)
    block = vm((toks, width), BF16)
    block32 = vm((toks, width), F32)
    pieces = vm((4, piece, width), BF16)
    halfff = vm((ff // 2, width), BF16)
    heads = vm((length, head_width), BF16)
    heads32 = vm((length, head_width), F32)
    return pl.pallas_call(
        functools.partial(layer_body, scale),
        name="layer",
        out_shape=(
            shape((toks, width), BF16), shape((toks, width), BF16), shape(three, BF16), shape(five, BF16), shape((ff // 2, width), BF16), shape((16, width), F32),
        ),
        in_specs=[VM, VM, VM, VM, HBM, HBM, HBM] + [VM] * 4,
        out_specs=(HBM,) * 6,
        scratch_shapes=[
            heads, heads, heads, heads32, vm((8, length), F32), rows4, vm((8 * piece, 3 * share), BF16), block, block32, heads, vm((16, width), F32), halfff,
            vm((4, 2, piece, width), BF16),
            vm((4, toks, 3 * share), BF16), vm((2, head_width // 2 + 16, length), BF16), heads32, heads, block,
            vm((width, width), BF16), vm((width, ff), BF16), vm((ff, width), BF16), block32, block32, vm((toks, 128), F32),
            rows4, vm((4, toks, ff), BF16), vm((4, toks, ff), BF16), rows4, vm((4, half, width), BF16), vm((2, half, width), BF16), rows4, vm((4, toks, ff), BF16),
            block, block, vm((8, 8, width), F32), halfff, halfff, halfff, halfff, pieces, pieces, pieces, pieces,
            vm((8, length), F32), heads32, vm((head_width, BQ), F32), small, small, small, vm(three, BF16), vm(three, BF16), vm((3, 2, piece, width), BF16),
            vm(five, BF16), vm(five, BF16), vm(five, BF16), vm(three, BF16), block, vm((16, width), F32), vm((9, 16, width), F32), vm((16, width), F32),
            pltpu.SemaphoreType.DMA((320,)), pltpu.SemaphoreType.DMA((320,)), pltpu.SemaphoreType.DMA((40,)),
        ],
        compiler_params=pltpu.CompilerParams(collective_id=1, has_side_effects=True, vmem_limit_bytes=63 << 20),
    )(seg, x, cot, qkv_w, up_w, out_w, down_w, proj_bias, hidden_bias, gain, shift)


def emit_body(
    grad_scale, who, h_low, h_grad, h_qkv, h_upout, h_down, h_vec,
    output, input_grad, qkv_total, out_total, up_total, down_total, bias_total, hidden_total, gain_total, shift_total,
    qkv_sum, upout_sum, down_sum, vec_sum, sems,
):
    width = h_low.shape[1]
    piece = qkv_sum.shape[1]
    pairs = ((h_down, down_sum), (h_upout, upout_sum), (h_qkv, qkv_sum), (h_vec, vec_sum), (h_low, output), (h_grad, input_grad))
    copies = [pltpu.make_async_copy(src, dst, sems.at[i]) for i, (src, dst) in enumerate(pairs)]
    for copy in copies:
        copy.start()
    for copy in copies:
        copy.wait()
    for p in range(3):
        qkv_total[:, p * width : (p + 1) * width] = qkv_sum[p].astype(F32) * grad_scale
    chip = who[0]
    for at, m in enumerate((0, 3, 1, 2)):
        up_total[:, rows_of(lax.bitwise_xor(chip, m), width)] = upout_sum[at * piece : (at + 1) * piece, :].astype(F32) * grad_scale
    out_total[...] = upout_sum[4 * piece :, :].astype(F32) * grad_scale
    down_total[...] = down_sum[...].astype(F32) * grad_scale
    bias_total[...] = vec_sum[0:4] * grad_scale
    gain_total[...] = vec_sum[4:6] * grad_scale
    shift_total[...] = vec_sum[6:8] * grad_scale
    for kk in range(4):
        hidden_total[:, kk * width : (kk + 1) * width] = vec_sum[8 + kk : 9 + kk] * grad_scale


def emit(grad_scale, who, low, grad, qkv_sum, upout_sum, down_sum, vec_sum):
    toks, width = low.shape
    piece = qkv_sum.shape[1]
    shape = jax.ShapeDtypeStruct
    return pl.pallas_call(
        functools.partial(emit_body, grad_scale),
        name="emit",
        out_shape=(
            shape((toks, width), BF16), shape((toks, width), BF16), shape((piece, 3 * width), F32), shape((piece, width), F32), shape((piece, 4 * width), F32),
            shape(down_sum.shape, F32), shape((4, width), F32), shape((1, 4 * width), F32), shape((2, width), F32), shape((2, width), F32),
        ),
        in_specs=[SM] + [HBM] * 6,
        out_specs=(VM,) * 10,
        scratch_shapes=[
            pltpu.VMEM(qkv_sum.shape, BF16), pltpu.VMEM(upout_sum.shape, BF16), pltpu.VMEM(down_sum.shape, BF16), pltpu.VMEM(vec_sum.shape, F32),
            pltpu.SemaphoreType.DMA((6,)),
        ],
        compiler_params=pltpu.CompilerParams(vmem_limit_bytes=62 << 20),
    )(who, low, grad, qkv_sum, upout_sum, down_sum, vec_sum)


def local_tensor(tokens, segment_ids, qkv_weight, out_weight, up_weight, down_weight, proj_bias, hidden_bias, norm_gain, norm_shift, cotangent):
    inputs = tokens[0]
    toks, width = inputs.shape
    scale = (width // HEADS) ** (-0.5)
    grad_scale = (toks * lax.axis_size("fsdp") * lax.axis_size("rep")) ** (-0.5)
    low, grad, qkv_sum, upout_sum, down_sum, vec_sum = layer(
        scale, segment_ids, inputs, cotangent[0], qkv_weight, up_weight, out_weight, down_weight, proj_bias, hidden_bias[None], norm_gain, norm_shift
    )
    output, input_grad, qkv_total, out_total, up_total, down_total, bias_total, hidden_total, gain_total, shift_total = emit(
        grad_scale, (lax.axis_index("fsdp") // 2).reshape(1), low, grad, qkv_sum, upout_sum, down_sum, vec_sum
    )
    return (
        output[None],
        input_grad[None],
        qkv_total,
        out_total,
        up_total,
        down_total,
        bias_total,
        hidden_total.reshape(4 * width),
        gain_total,
        shift_total,
    )


def normalize(hidden, gain, shift):
    center = hidden - jnp.mean(hidden, axis=-1, keepdims=True)
    spread = jnp.mean(center * center, axis=-1, keepdims=True)
    return center * lax.rsqrt(spread + 1e-05) * gain + shift


def exact_gelu(value):
    return jax.nn.gelu(value, approximate=False)


def gather_attention(qkv_weight, out_weight):
    return (
        lax.all_gather(qkv_weight, "fsdp", axis=0, tiled=True),
        lax.all_gather(out_weight, "fsdp", axis=0, tiled=True),
    )


def gather_feedforward(up_weight, down_weight):
    return (
        lax.all_gather(up_weight, "fsdp", axis=0, tiled=True),
        lax.all_gather(down_weight, "fsdp", axis=0, tiled=True),
    )


def block_plan(row_count):
    block_rows = math.gcd(row_count, 1024)
    return (block_rows, row_count // block_rows)


def split_heads(matrix):
    return matrix.reshape(matrix.shape[0], HEADS, matrix.shape[1] // HEADS)


def join_heads(stacked):
    return jnp.transpose(stacked, (1, 0, 2)).reshape(
        stacked.shape[1], stacked.shape[0] * stacked.shape[2]
    )


def local_gather(
    tokens,
    segment_ids,
    qkv_weight,
    out_weight,
    up_weight,
    down_weight,
    proj_bias,
    hidden_bias,
    norm_gain,
    norm_shift,
    cotangent,
):
    inputs = tokens[0]
    tok_count, model_width = inputs.shape
    head_dim = model_width // HEADS
    score_scale = head_dim ** (-0.5)
    doc_ids = segment_ids[0]
    own_index = lax.axis_index("fsdp")
    own_docs = lax.dynamic_slice_in_dim(doc_ids, own_index * tok_count, tok_count)
    qkv_full, out_full = gather_attention(qkv_weight, out_weight)
    projected = jnp.dot(inputs, qkv_full, preferred_element_type=jnp.float32)
    queries = (projected[:, :model_width] + proj_bias[0]).astype(jnp.bfloat16)
    key_rows = projected[:, model_width : 2 * model_width].astype(jnp.bfloat16)
    value_rows = (projected[:, 2 * model_width :] + proj_bias[1]).astype(jnp.bfloat16)
    query_heads = split_heads(queries)
    key_own = split_heads(key_rows)
    value_own = split_heads(value_rows)
    initial = (
        jnp.zeros((HEADS, tok_count, head_dim), jnp.float32),
        jnp.full((HEADS, tok_count), NEGATIVE, jnp.float32),
        jnp.zeros((HEADS, tok_count), jnp.float32),
    )
    key_piece = lax.all_gather(key_rows, "fsdp", axis=0, tiled=True)
    value_piece = lax.all_gather(value_rows, "fsdp", axis=0, tiled=True)
    block_rows, blocks = block_plan(key_piece.shape[0])

    def forward_advance(block_index, running_state):
        weighted, running, denominator = running_state
        offset = block_index * block_rows
        key_block = split_heads(lax.dynamic_slice_in_dim(key_piece, offset, block_rows))
        value_block = split_heads(lax.dynamic_slice_in_dim(value_piece, offset, block_rows))
        block_docs = lax.dynamic_slice_in_dim(doc_ids, offset, block_rows)
        scores = (
            jnp.einsum("qhd,khd->hqk", query_heads, key_block, preferred_element_type=jnp.float32)
            * score_scale
        )
        same_doc = (own_docs[:, None] == block_docs[None, :])[None]
        highest = jnp.maximum(running, jnp.max(jnp.where(same_doc, scores, NEGATIVE), axis=2))
        factor = jnp.exp(running - highest)
        weights = jnp.where(same_doc, jnp.exp(scores - highest[:, :, None]), 0.0)
        denominator = denominator * factor + jnp.sum(weights, axis=2)
        weighted = weighted * factor[:, :, None] + jnp.einsum(
            "hqk,khd->hqd",
            weights.astype(jnp.bfloat16),
            value_block,
            preferred_element_type=jnp.float32,
        )
        return (weighted, highest, denominator)

    weighted, running, denominator = lax.fori_loop(0, blocks, forward_advance, initial)
    attended_heads = weighted / denominator[:, :, None]
    log_total = running + jnp.log(denominator)
    attended_low = join_heads(attended_heads).astype(jnp.bfloat16)
    branch = jnp.dot(attended_low, out_full, preferred_element_type=jnp.float32) + proj_bias[2]
    first_norm, norm_one_back = jax.vjp(
        normalize, inputs.astype(jnp.float32) + branch, norm_gain[0], norm_shift[0]
    )
    first_low = first_norm.astype(jnp.bfloat16)
    up_full, down_full = gather_feedforward(up_weight, down_weight)
    hidden_pre = jnp.dot(first_low, up_full, preferred_element_type=jnp.float32) + hidden_bias
    activated, gelu_back = jax.vjp(exact_gelu, hidden_pre)
    activated_low = activated.astype(jnp.bfloat16)
    second = jnp.dot(activated_low, down_full, preferred_element_type=jnp.float32) + proj_bias[3]
    output, norm_two_back = jax.vjp(normalize, first_norm + second, norm_gain[1], norm_shift[1])
    up_back, down_back = gather_feedforward(up_weight, down_weight)
    qkv_back, out_back = gather_attention(qkv_weight, out_weight)
    grad_second, gain_two, shift_two = norm_two_back(cotangent[0].astype(jnp.float32))
    second_low = grad_second.astype(jnp.bfloat16)
    down_term = jnp.einsum(
        "tf,td->fd", activated_low, second_low, preferred_element_type=jnp.float32
    )
    activated_grad = jnp.einsum(
        "td,fd->tf", second_low, down_back, preferred_element_type=jnp.float32
    )
    (pre_grad,) = gelu_back(activated_grad)
    pre_low = pre_grad.astype(jnp.bfloat16)
    up_term = jnp.einsum("td,tf->df", first_low, pre_low, preferred_element_type=jnp.float32)
    first_grad = grad_second + jnp.einsum(
        "tf,df->td", pre_low, up_back, preferred_element_type=jnp.float32
    )
    branch_grad, gain_one, shift_one = norm_one_back(first_grad)
    branch_low = branch_grad.astype(jnp.bfloat16)
    out_term = jnp.einsum("te,td->ed", attended_low, branch_low, preferred_element_type=jnp.float32)
    attended_grad = jnp.einsum(
        "td,ed->te", branch_low, out_back, preferred_element_type=jnp.float32
    ).astype(jnp.bfloat16)
    grad_heads = split_heads(attended_grad)
    correction = jnp.einsum("qhd,hqd->hq", grad_heads.astype(jnp.float32), attended_heads)
    lse_all, correction_all = (
        lax.all_gather(log_total, "fsdp", axis=1, tiled=True),
        lax.all_gather(correction, "fsdp", axis=1, tiled=True),
    )
    query_key_piece = lax.all_gather(key_rows, "fsdp", axis=0, tiled=True)
    query_value_piece = lax.all_gather(value_rows, "fsdp", axis=0, tiled=True)
    query_block_rows, blocks = block_plan(query_key_piece.shape[0])

    def query_advance(block_index, query_state):
        offset = block_index * query_block_rows
        key_block = split_heads(lax.dynamic_slice_in_dim(query_key_piece, offset, query_block_rows))
        value_block = split_heads(
            lax.dynamic_slice_in_dim(query_value_piece, offset, query_block_rows)
        )
        block_docs = lax.dynamic_slice_in_dim(doc_ids, offset, query_block_rows)
        scores = (
            jnp.einsum("qhd,khd->hqk", query_heads, key_block, preferred_element_type=jnp.float32)
            * score_scale
        )
        same_doc = (own_docs[:, None] == block_docs[None, :])[None]
        probabilities = jnp.where(same_doc, jnp.exp(scores - log_total[:, :, None]), 0.0)
        prob_grad = jnp.einsum(
            "qhd,khd->hqk", grad_heads, value_block, preferred_element_type=jnp.float32
        )
        score_grad = (probabilities * (prob_grad - correction[:, :, None])).astype(jnp.bfloat16)
        return query_state + jnp.einsum(
            "hqk,khd->hqd", score_grad, key_block, preferred_element_type=jnp.float32
        )

    query_acc = lax.fori_loop(
        0, blocks, query_advance, jnp.zeros((HEADS, tok_count, head_dim), jnp.float32)
    )
    query_grad = (join_heads(query_acc) * score_scale).astype(jnp.bfloat16)
    empty_heads = jnp.zeros((HEADS, tok_count, head_dim), jnp.float32)
    query_piece = lax.all_gather(queries, "fsdp", axis=0, tiled=True)
    grad_piece = lax.all_gather(attended_grad, "fsdp", axis=0, tiled=True)
    key_block_rows, blocks = block_plan(query_piece.shape[0])

    def key_advance(block_index, key_state):
        key_acc, value_acc = key_state
        offset = block_index * key_block_rows
        query_block = split_heads(lax.dynamic_slice_in_dim(query_piece, offset, key_block_rows))
        grad_block = split_heads(lax.dynamic_slice_in_dim(grad_piece, offset, key_block_rows))
        block_docs = lax.dynamic_slice_in_dim(doc_ids, offset, key_block_rows)
        lse_block = lax.dynamic_slice_in_dim(lse_all, offset, key_block_rows, axis=1)
        corr_block = lax.dynamic_slice_in_dim(correction_all, offset, key_block_rows, axis=1)
        scores = (
            jnp.einsum("qhd,khd->hqk", query_block, key_own, preferred_element_type=jnp.float32)
            * score_scale
        )
        same_doc = (block_docs[:, None] == own_docs[None, :])[None]
        probabilities = jnp.where(same_doc, jnp.exp(scores - lse_block[:, :, None]), 0.0)
        value_acc = value_acc + jnp.einsum(
            "hqk,qhd->hkd",
            probabilities.astype(jnp.bfloat16),
            grad_block,
            preferred_element_type=jnp.float32,
        )
        prob_grad = jnp.einsum(
            "qhd,khd->hqk", grad_block, value_own, preferred_element_type=jnp.float32
        )
        score_grad = (probabilities * (prob_grad - corr_block[:, :, None])).astype(jnp.bfloat16)
        key_acc = key_acc + jnp.einsum(
            "hqk,qhd->hkd", score_grad, query_block, preferred_element_type=jnp.float32
        )
        return (key_acc, value_acc)

    key_acc, value_acc = lax.fori_loop(0, blocks, key_advance, (empty_heads, empty_heads))
    key_grad = (join_heads(key_acc) * score_scale).astype(jnp.bfloat16)
    value_grad = join_heads(value_acc).astype(jnp.bfloat16)
    qkv_grad_low = jnp.concatenate([query_grad, key_grad, value_grad], axis=1)
    qkv_term = jnp.einsum("td,te->de", inputs, qkv_grad_low, preferred_element_type=jnp.float32)
    input_grad = branch_grad + jnp.einsum(
        "te,de->td", qkv_grad_low, qkv_back, preferred_element_type=jnp.float32
    )
    bias_term = jnp.stack(
        [
            jnp.sum(query_grad.astype(jnp.float32), axis=0),
            jnp.sum(value_grad.astype(jnp.float32), axis=0),
            jnp.sum(branch_low.astype(jnp.float32), axis=0),
            jnp.sum(second_low.astype(jnp.float32), axis=0),
        ]
    )
    hidden_term = jnp.sum(pre_low.astype(jnp.float32), axis=0)
    gain_term = jnp.stack([gain_one, gain_two])
    shift_term = jnp.stack([shift_one, shift_two])
    bias_total, hidden_total, gain_total, shift_total = lax.psum(
        (bias_term, hidden_term, gain_term, shift_term), ("rep", "fsdp")
    )
    up_sum, down_sum = (
        lax.psum_scatter(up_term, "fsdp", scatter_dimension=0, tiled=True),
        lax.psum_scatter(down_term, "fsdp", scatter_dimension=0, tiled=True),
    )
    qkv_sum, out_sum = (
        lax.psum_scatter(qkv_term, "fsdp", scatter_dimension=0, tiled=True),
        lax.psum_scatter(out_term, "fsdp", scatter_dimension=0, tiled=True),
    )
    qkv_total, out_total, up_total, down_total = lax.psum(
        (qkv_sum, out_sum, up_sum, down_sum), "rep"
    )
    grad_scale = (tok_count * lax.axis_size("fsdp") * lax.axis_size("rep")) ** (-0.5)
    return (
        output.astype(jnp.bfloat16)[None],
        input_grad.astype(jnp.bfloat16)[None],
        qkv_total * grad_scale,
        out_total * grad_scale,
        up_total * grad_scale,
        down_total * grad_scale,
        bias_total * grad_scale,
        hidden_total * grad_scale,
        gain_total * grad_scale,
        shift_total * grad_scale,
    )


def solution(mesh):
    small = mesh.shape["fsdp"] == 8 and mesh.shape["rep"] == 4
    local = local_tensor if small else local_gather
    return jax.shard_map(
        local,
        mesh=mesh,
        in_specs=(
            P("rep", "fsdp", None),
            P("rep", None),
            P("fsdp", None),
            P("fsdp", None),
            P("fsdp", None),
            P("fsdp", None),
            P(),
            P(),
            P(),
            P(),
            P("rep", "fsdp", None),
        ),
        out_specs=(
            P("rep", "fsdp", None),
            P("rep", "fsdp", None),
            P("fsdp", None),
            P("fsdp", None),
            P("fsdp", None),
            P("fsdp", None),
            P(),
            P(),
            P(),
            P(),
        ),
        check_vma=False,
    )
```

```python
import functools
import math

import jax
import jax.numpy as jnp
from jax import lax
from jax.experimental import pallas as pl
from jax.experimental.pallas import tpu as pltpu
from jax.sharding import PartitionSpec as P

HEADS = 16

NEGATIVE = -1e30
BQ = 256
BK = 512
VM = pl.BlockSpec(memory_space=pltpu.VMEM)
SM = pl.BlockSpec(memory_space=pltpu.SMEM)


def nt(a, b):
    return lax.dot_general(a, b, (((1,), (1,)), ((), ())), preferred_element_type=jnp.float32)


def nn(a, b):
    return jnp.dot(a, b, preferred_element_type=jnp.float32)


def head_lanes(shape, half):
    return lax.broadcasted_iota(jnp.int32, shape, 1) < half


def rows_of(index, size):
    return pl.ds(pl.multiple_of(index * size, size), size)


def seg_columns(seg_v, seg_c):
    length = seg_c.shape[0]

    @pl.loop(0, length // BQ)
    def _(i):
        rows = rows_of(i, BQ)
        seg_c[rows, :] = jnp.transpose(jnp.broadcast_to(seg_v[:, rows].astype(jnp.float32), (128, BQ)))


def wide(column, lanes):
    return jnp.concatenate([column] * (lanes // 128), axis=1)


MESH = pl.DeviceIdType.MESH
HBM = pl.BlockSpec(memory_space=pltpu.HBM)
F32 = jnp.float32
BF16 = jnp.bfloat16


def tn(a, b):
    return lax.dot_general(a, b, (((0,), (0,)), ((), ())), preferred_element_type=F32)


def fold_rows(v):
    return jnp.sum(v.reshape(v.shape[0] // 8, 8, v.shape[1]), axis=0)


class Wires:
    def __init__(self, send_sems, recv_sems, local_sems):
        self.send_sems, self.recv_sems, self.local_sems = send_sems, recv_sems, local_sems
        self.count = 0
        self.local_count = 0
        self.sent = []
        self.rep = lax.axis_index("rep")
        self.own = lax.axis_index("fsdp")

    def remote(self, src, dst, peer, rep=None):
        i = self.count
        self.count = i + 1
        return pltpu.make_async_remote_copy(
            src_ref=src, dst_ref=dst, send_sem=self.send_sems.at[i], recv_sem=self.recv_sems.at[i],
            device_id=(self.rep if rep is None else rep, peer), device_id_type=MESH,
        )

    def send(self, src, dst, peer):
        copy = self.remote(src, dst, peer)
        copy.start()
        self.sent.append(copy)
        return copy

    def local(self, src, dst):
        copy = pltpu.make_async_copy(src, dst, self.local_sems.at[self.local_count])
        self.local_count += 1
        copy.start()
        return copy

    def greet(self, peers):
        barrier = pltpu.get_barrier_semaphore()
        for rep, peer in peers:
            pl.semaphore_signal(barrier, inc=1, device_id=(rep, peer), device_id_type=MESH)
        pl.semaphore_wait(barrier, len(peers))

    def drain(self, copies):
        for copy in copies:
            copy.wait_send()
            self.sent = [other for other in self.sent if other is not copy]

    def finish(self):
        for copy in self.sent:
            copy.wait_send()


class Line:
    def __init__(self, wires, own, land, far, count, size=None):
        self.own, self.land, self.far = own, land, far
        rep, dev = wires.rep, wires.own
        size = own.shape[0] // count if size is None else size
        self.rows = [pl.ds(i * size, size) for i in range(count)]
        self.inner = jnp.logical_or(rep == 1, rep == 2)
        self.outer = jnp.logical_not(self.inner)
        near, across = lax.bitwise_xor(rep, 1), lax.bitwise_xor(rep, 3)
        self.first = [wires.remote(own.at[r], land.at[r], dev, near) for r in self.rows]
        self.middle = [wires.remote(own.at[r], far.at[r], dev, across) for r in self.rows]
        self.back = [wires.remote(land.at[r], land.at[r], dev, near) for r in self.rows]

    def start(self):
        @pl.when(self.outer)
        def _():
            for copy in self.first:
                copy.start()

    def collect(self, which):
        @pl.when(self.inner)
        def _():
            for i in which:
                r = self.rows[i]
                self.first[i].wait_recv()
                self.own[r, :] = (self.own[r, :].astype(F32) + self.land[r, :].astype(F32)).astype(BF16)
                self.middle[i].start()

    def total(self, which):
        @pl.when(self.inner)
        def _():
            for i in which:
                r = self.rows[i]
                self.middle[i].wait_recv()
                self.land[r, :] = (self.own[r, :].astype(F32) + self.far[r, :].astype(F32)).astype(BF16)
                self.back[i].start()

    def arrive(self, which):
        @pl.when(self.outer)
        def _():
            for i in which:
                self.back[i].wait_recv()

    def finish(self):
        @pl.when(self.outer)
        def _():
            for copy in self.first:
                copy.wait_send()

        @pl.when(self.inner)
        def _():
            for i in range(len(self.rows)):
                self.middle[i].wait_send()
                self.back[i].wait_send()


class Hops:
    def __init__(self, wires, view):
        rep, reps = wires.rep, 4
        self.all = []
        for hop in range(1, reps):
            for step in (1, -1):
                index, to, come = rep - step * (hop - 1), rep + step, rep - step * hop
                going = (index >= 0) & (index < reps) & (to >= 0) & (to < reps)
                coming = (come >= 0) & (come < reps)
                refs = view(jnp.clip(index, 0, reps - 1))
                copies = [wires.remote(ref, ref, wires.own, jnp.clip(to, 0, reps - 1)) for ref in refs]
                self.all.append((hop, going, coming, copies))

    def each(self, hop, kind):
        for at, going, coming, copies in self.all:
            if hop in (0, at):

                @pl.when(coming if kind == "wait_recv" else going)
                def _():
                    for copy in copies:
                        getattr(copy, kind)()

    def start(self, hop):
        self.each(hop, "start")

    def wait(self, hop):
        self.each(hop, "wait_recv")

    def finish(self):
        self.each(0, "wait_send")


class Spread:
    def __init__(self, wires, slots, half):
        self.wires, self.slots, self.half = wires, slots, half
        self.chip = wires.own // 2
        self.x, self.y = lax.bitwise_xor(wires.own, 2), lax.bitwise_xor(wires.own, 4)
        self.cx, self.cy, self.cd = (lax.bitwise_xor(self.chip, m) for m in (1, 2, 3))
        self.a, self.b = pl.ds(0, half), pl.ds(half, half)

    def piece(self, chip, part):
        return self.slots.at[chip, part]

    def put(self, chip, part, peer):
        return self.wires.send(self.piece(chip, part), self.piece(chip, part), peer)

    def first_half(self):
        self.xa = self.put(self.chip, self.a, self.x)
        self.ya = self.put(self.chip, self.a, self.y)

    def second_half(self):
        self.yb = self.put(self.chip, self.b, self.y)
        self.xb = self.put(self.chip, self.b, self.x)

    def relay(self):
        self.xa.wait_recv()
        self.da = self.put(self.cx, self.a, self.y)
        self.yb.wait_recv()
        self.db = self.put(self.cy, self.b, self.x)

    def wait_sides(self):
        self.xb.wait_recv()
        self.ya.wait_recv()

    def wait_diagonal(self):
        self.da.wait_recv()
        self.db.wait_recv()


class Gather:
    def __init__(self, wires, part, side, last, half):
        self.wires, self.part, self.side, self.last, self.half = wires, part, side, last, half
        self.chip = wires.own // 2
        self.x, self.y = lax.bitwise_xor(wires.own, 2), lax.bitwise_xor(wires.own, 4)
        self.cx, self.cy, self.cd = (lax.bitwise_xor(self.chip, m) for m in (1, 2, 3))
        self.a, self.b = pl.ds(0, half), pl.ds(half, half)

    def send_x(self):
        self.x_own = self.wires.send(self.part.at[self.cx, self.a], self.side.at[0], self.x)

    def send_y(self):
        self.y_own = self.wires.send(self.part.at[self.cy, self.b], self.side.at[1], self.y)

    def send_diagonal(self):
        self.x_far = self.wires.send(self.part.at[self.cd, self.a], self.side.at[2], self.x)
        self.y_far = self.wires.send(self.part.at[self.cd, self.b], self.side.at[3], self.y)

    def relay(self):
        step = 32

        def add(chip, start, slot):
            @pl.loop(0, self.half // step)
            def _(t):
                rows = pl.ds(pl.multiple_of(start + t * step, step), step)
                near = self.part[chip, rows, :].astype(F32) + self.side[slot, rows_of(t, step), :].astype(F32)
                self.part[chip, rows, :] = near.astype(BF16)

        self.x_far.wait_recv()
        add(self.cy, 0, 2)
        self.y_last = self.wires.send(self.part.at[self.cy, self.a], self.last.at[0], self.y)
        self.y_far.wait_recv()
        add(self.cx, self.half, 3)
        self.x_last = self.wires.send(self.part.at[self.cx, self.b], self.last.at[1], self.x)

    def drain(self):
        for copy in (self.x_own, self.y_own, self.x_far, self.y_far, self.x_last, self.y_last):
            copy.wait_send()
            self.wires.sent = [other for other in self.wires.sent if other is not copy]

    def wait_first(self):
        self.x_own.wait_recv()
        self.y_last.wait_recv()

    def wait_second(self):
        self.y_own.wait_recv()
        self.x_last.wait_recv()

    def total(self, which, offset, size):
        rows = pl.ds(pl.multiple_of(which * self.half + offset, size), size)
        here = pl.ds(pl.multiple_of(offset, size), size)
        return self.part[self.chip, rows, :].astype(F32) + self.side[which, here, :].astype(F32) + self.last[which, here, :].astype(F32)


def layer_body(
    scale, seg, x, cot, qkv_w, up_w, out_w, down_w, proj_bias, hidden_bias, gain, shift,
    h_output, h_input_grad, h_qkv, h_upout, h_down, h_vec,
    q_out, k_out, v_out, o_out, lse, xs, w_full, output, branch_grad, grad_heads, vec, down_grad, sends,
    stage, vt, seg_c, low, att, out_full, up_full, down_full, h1, z1, r1, fl, act, slope, part, side, last, sl, pre,
    branch_low, agl, acc, d_send, d_recv, d_far, down_sum, u_send, u_recv, o_send, o_recv,
    corr, dv_acc, dqt, q_send, q_recv, q_piece, l_own, l_far, got, y_own, y_far, upout_sum, qkv_sum, input_grad, v_sum, v_recv, vec_sum,
    send_sems, recv_sems, local_sems,
):
    w = Wires(send_sems, recv_sems, local_sems)
    own, rep = w.own, w.rep
    core, chip = lax.rem(own, 2), own // 2
    mate = lax.bitwise_xor(own, 1)
    cx, cy, cd = (lax.bitwise_xor(chip, m) for m in (1, 2, 3))
    others = (cd, cx, cy)
    toks, width = x.shape
    ff = up_full.shape[1]
    share = width // 4
    head_width = share // 2
    half = toks // 2
    piece = up_w.shape[0]
    quarter = piece // 4
    tile = 256
    w.greet(
        [(rep, lax.bitwise_xor(own, m)) for m in range(1, 8)]
        + [(lax.bitwise_xor(rep, m), own) for m in (1, 2, 3)]
    )

    mine, some = rows_of(own, piece), rows_of(rep, quarter)

    def quarter_of(full, k, r, cols=slice(None)):
        return full.at[pl.ds(pl.multiple_of((2 * k + core) * piece + r * quarter, quarter), quarter), cols]

    def qkv_cols(p, to_chip):
        return pl.ds(pl.multiple_of(p * width + to_chip * share, share), share)

    first_fetch = []
    for mask in (6, 2, 4):
        peer, to_chip = lax.bitwise_xor(own, mask), lax.bitwise_xor(chip, mask // 2)
        for p in range(3):
            first_fetch.append(w.send(qkv_w.at[some, qkv_cols(p, to_chip)], quarter_of(w_full, chip, rep, pl.ds(p * share, share)), peer))
    xs[chip] = x[...]
    spread0 = Spread(w, xs, half)
    spread0.first_half()
    spread0.second_half()
    fetch = []
    for mask in (6, 2, 4):
        peer, to_chip = lax.bitwise_xor(own, mask), lax.bitwise_xor(chip, mask // 2)
        fetch.append(w.send(up_w.at[some, rows_of(to_chip, ff)], quarter_of(up_full, chip, rep), peer))
        fetch.append(w.send(out_w.at[some], quarter_of(out_full, chip, rep), peer))
    here, there = [], []
    for p in range(3):
        src, dst = qkv_w.at[:, qkv_cols(p, chip)], w_full.at[mine, pl.ds(p * share, share)]
        here.append(w.local(src, dst))
        there.append(w.send(src, dst, mate))
    kept = []
    for src, dst in ((up_w.at[:, rows_of(chip, ff)], up_full.at[mine]), (out_w, out_full.at[mine]), (down_w, down_full.at[rows_of(core, ff // 2)])):
        kept.append((w.local(src, dst), w.send(src, dst, mate)))
    qkv_hops = Hops(w, lambda r: [quarter_of(w_full, k, r) for k in others])
    hops = Hops(w, lambda r: [quarter_of(full, k, r) for full in (up_full, out_full) for k in others])
    for copy in first_fetch:
        copy.wait_recv()
    qkv_hops.start(1)
    seg_columns(seg, seg_c)
    qkv_hops.wait(1)
    qkv_hops.start(2)
    spread0.relay()
    qkv_hops.wait(2)
    qkv_hops.start(3)
    for copy in fetch:
        copy.wait_recv()
    hops.start(1)
    qkv_hops.wait(3)
    for k in others:
        rows = rows_of(2 * k + core, piece)
        there.append(w.send(w_full.at[rows], w_full.at[rows], mate))
    for copy in here:
        copy.wait()
    for copy in there:
        copy.wait_recv()

    outs = (q_out, k_out, v_out)
    trades = []

    def block(k):
        rows = rows_of(2 * k + core, toks)
        for p in range(3):
            r = nn(xs[k], w_full[:, pl.ds(p * share, share)])
            if p != 1:
                r = r + proj_bias[p // 2 : p // 2 + 1, rows_of(chip, share)]
            stage[k, :, pl.ds(p * share, share)] = r.astype(BF16)
            theirs = pl.ds(pl.multiple_of(p * share + (1 - core) * head_width, head_width), head_width)
            trades.append(w.send(stage.at[k, :, theirs], outs[p].at[rows], mate))
            outs[p][rows, :] = stage[k, :, pl.ds(pl.multiple_of(p * share + core * head_width, head_width), head_width)]

    block(chip)
    spread0.wait_sides()
    block(cx)
    block(cy)
    hops.wait(1)
    hops.start(2)
    spread0.wait_diagonal()
    block(cd)
    for copy in trades:
        copy.wait_recv()
    w.drain(trades)

    headd = head_width // 2
    blocks = q_out.shape[0] // BQ
    first = head_lanes((BQ, head_width), headd)

    @pl.loop(0, blocks)
    def _(i):
        rows = rows_of(i, BQ)
        t = jnp.transpose(v_out[rows, :])
        for h in range(2):
            vt[h, 0:headd, rows] = t[h * headd : (h + 1) * headd]
            vt[h, headd : headd + 16, rows] = jnp.ones((16, BQ), BF16)

    swaps = {}
    for mask in range(1, 8):
        peer = lax.bitwise_xor(own, mask)
        swaps[mask] = w.remote(low.at[rows_of(peer, toks)], att.at[:, rows_of(own, head_width)], peer)

    @pl.loop(0, blocks)
    def _(t):
        i = lax.bitwise_xor(own, 7 - t)
        rows = rows_of(i, BQ)
        qb = q_out[rows, :] * jnp.bfloat16(scale)
        zero = jnp.zeros_like(qb)
        qs = (jnp.where(first, qb, zero), jnp.where(first, zero, qb))
        seg_q = seg[:, rows].astype(F32)
        both = []
        for h in range(2):
            scores = []
            for j in range(blocks):
                cols = pl.ds(j * BQ, BQ)
                same = wide(seg_c[cols, :], BQ) == seg_q
                scores.append(jnp.where(same, nt(k_out[cols, :], qs[h]), NEGATIVE))
            top = functools.reduce(jnp.maximum, [jnp.max(s, axis=0, keepdims=True) for s in scores])
            total = jnp.zeros((headd + 16, BQ), F32)
            for j in range(blocks):
                total = total + nn(vt[h, :, pl.ds(j * BQ, BQ)], jnp.exp(scores[j] - top).astype(BF16))
            norm = total[headd : headd + 1]
            both.append(total[0:headd] / norm)
            lse[h : h + 1, rows] = top + jnp.log(norm)
        out = jnp.transpose(jnp.concatenate(both, axis=0))
        o_out[rows, :] = out
        low[rows, :] = out.astype(BF16)
        for mask in range(1, 8):

            @pl.when(t == 7 - mask)
            def _(mask=mask):
                swaps[mask].start()

        @pl.when(t == 2)
        def _():
            hops.wait(2)
            hops.start(3)

    w.sent.extend(swaps.values())
    att[:, rows_of(own, head_width)] = low[rows_of(own, toks), :]
    hops.wait(3)
    for k in others:
        rows = rows_of(2 * k + core, piece)
        for full in (out_full, up_full):
            kept.append((None, w.send(full.at[rows], full.at[rows], mate)))
    for local, remote in kept:
        if local is not None:
            local.wait()
        remote.wait_recv()
    for copy in swaps.values():
        copy.wait_recv()

    @pl.loop(0, width // tile)
    def _(n):
        cols = rows_of(n, tile)
        h1[:, cols] = nn(att[...], out_full[:, cols]) + proj_bias[2:3, cols] + x[:, cols].astype(F32)

    step = 32
    acc[...] = jnp.zeros_like(acc)

    def first_rows(t):
        rows = rows_of(t, step)
        v = h1[rows, :]
        center = v - jnp.mean(v, axis=1, keepdims=True)
        inv = lax.rsqrt(jnp.mean(center * center, axis=1, keepdims=True) + 1e-05)
        z = center * inv
        z1[rows, :] = z
        r1[rows, :] = jnp.broadcast_to(inv, (step, 128))
        fl[chip, rows, :] = (z * gain[0:1, :] + shift[0:1, :]).astype(BF16)

    spread = Spread(w, fl, half)
    pl.loop(0, half // step)(first_rows)
    spread.first_half()
    pl.loop(half // step, toks // step)(first_rows)
    spread.second_half()

    def forward(k):
        @pl.loop(0, ff // tile)
        def _(n):
            cols = rows_of(n, tile)
            hidden = nn(fl[k], up_full[:, cols]) + hidden_bias[:, pl.ds(pl.multiple_of(chip * ff + n * tile, tile), tile)]
            cdf = 0.5 * (1.0 + lax.erf(hidden * (2.0**-0.5)))
            act[k, :, cols] = (hidden * cdf).astype(BF16)
            slope[k, :, cols] = (cdf + hidden * (jnp.exp(-0.5 * hidden * hidden) * ((2.0 * math.pi) ** -0.5))).astype(BF16)

        @pl.loop(0, width // tile)
        def _(n):
            cols = rows_of(n, tile)
            part[k, :, cols] = nn(act[k], down_full[:, cols]).astype(BF16)

    forward(chip)
    gather = Gather(w, part, side, last, half)
    spread.relay()
    spread.wait_sides()
    forward(cx)
    gather.send_x()
    forward(cy)
    gather.send_y()
    spread.wait_diagonal()
    forward(cd)
    gather.send_diagonal()

    gather.relay()

    def second_rows(which, t):
        rows = pl.ds(pl.multiple_of(which * half + t * step, step), step)
        v = z1[rows, :] * gain[0:1, :] + shift[0:1, :] + gather.total(which, t * step, step) + proj_bias[3:4, :]
        center = v - jnp.mean(v, axis=1, keepdims=True)
        inv = lax.rsqrt(jnp.mean(center * center, axis=1, keepdims=True) + 1e-05)
        z = center * inv
        output[rows, :] = (z * gain[1:2, :] + shift[1:2, :]).astype(BF16)
        c = cot[rows, :].astype(F32)
        e = c * gain[1:2, :]
        grad = inv * (e - jnp.mean(e, axis=1, keepdims=True) - z * jnp.mean(e * z, axis=1, keepdims=True))
        h1[rows, :] = grad
        low = grad.astype(BF16)
        sl[chip, rows, :] = low
        acc[0] += fold_rows(c * z)
        acc[1] += fold_rows(c)
        acc[2] += fold_rows(low.astype(F32))

    spread2 = Spread(w, sl, half)
    gather.wait_first()
    pl.loop(0, half // step)(functools.partial(second_rows, 0))
    spread2.first_half()
    gather.wait_second()
    pl.loop(0, half // step)(functools.partial(second_rows, 1))
    spread2.second_half()

    def backward(k):
        @pl.loop(0, ff // tile)
        def _(n):
            cols = rows_of(n, tile)
            grad = nt(sl[k], down_full[cols, :]) * slope[k, :, cols].astype(F32)
            low = grad.astype(BF16)
            pre[k, :, cols] = low
            acc[3, :, cols] += fold_rows(low.astype(F32))

        @pl.loop(0, width // tile)
        def _(n):
            cols = rows_of(n, tile)
            part[k, :, cols] = nt(pre[k], up_full[cols, :]).astype(BF16)

    gather.drain()
    backward(chip)
    gather2 = Gather(w, part, side, last, half)
    spread2.relay()
    spread2.wait_sides()
    backward(cx)
    gather2.send_x()
    backward(cy)
    gather2.send_y()
    spread2.wait_diagonal()
    backward(cd)
    gather2.send_diagonal()

    def down_rows(which, n):
        cols = pl.ds(pl.multiple_of(which * (ff // 2) + n * tile, tile), tile)
        lhs = act[:, :, cols].reshape(4 * toks, tile)
        return tn(lhs, sl[...].reshape(4 * toks, width))

    @pl.loop(0, ff // 2 // tile)
    def _(n):
        d_send[rows_of(n, tile), :] = down_rows(1 - core, n).astype(BF16)

    d_copy = w.send(d_send, d_recv, mate)
    d_copy.wait_recv()

    @pl.loop(0, ff // 2 // tile)
    def _(n):
        rows = rows_of(n, tile)
        down_grad[rows, :] = (down_rows(core, n) + d_recv[rows, :].astype(F32)).astype(BF16)

    down_line = Line(w, down_grad, down_sum, d_far, 8)
    down_line.start()
    gather2.relay()

    def up_rows(which, k):
        cols = pl.ds(pl.multiple_of((2 * k + which) * piece, piece), piece)
        lhs = fl[:, :, cols].reshape(4 * toks, piece)
        return tn(lhs, pre[...].reshape(4 * toks, ff))

    @pl.loop(0, 4)
    def _(k):
        u_send[k] = up_rows(1 - core, k).astype(BF16)

    u_copy = w.send(u_send, u_recv, mate)
    down_line.collect((0,))

    def branch_rows(which, t):
        rows = pl.ds(pl.multiple_of(which * half + t * step, step), step)
        grad = h1[rows, :] + gather2.total(which, t * step, step)
        z = z1[rows, :]
        e = grad * gain[0:1, :]
        out = r1[rows, 0:1] * (e - jnp.mean(e, axis=1, keepdims=True) - z * jnp.mean(e * z, axis=1, keepdims=True))
        branch_grad[rows, :] = out
        low = out.astype(BF16)
        branch_low[rows, :] = low
        acc[4] += fold_rows(grad * z)
        acc[5] += fold_rows(grad)
        acc[6] += fold_rows(low.astype(F32))

    gather2.wait_first()
    pl.loop(0, half // step)(functools.partial(branch_rows, 0))
    down_line.collect((1,))
    gather2.wait_second()
    pl.loop(0, half // step)(functools.partial(branch_rows, 1))

    @pl.loop(0, width // tile)
    def _(n):
        cols = rows_of(n, tile)
        agl[:, cols] = nt(branch_low[...], out_full[cols, :]).astype(BF16)

    backs = []
    for m in (6, 2, 4, 1, 3, 5, 7):
        peer = lax.bitwise_xor(own, m)
        backs.append(w.send(agl.at[:, rows_of(peer, head_width)], grad_heads.at[rows_of(own, toks)], peer))
    grad_heads[rows_of(own, toks), :] = agl[:, rows_of(own, head_width)]

    down_line.collect((2,))
    down_line.total((0,))
    u_copy.wait_recv()
    spread_up, spread_out = [], []

    def up_piece(m):
        k = lax.bitwise_xor(chip, m)
        return (up_rows(core, k) + u_recv[k].astype(F32)).astype(BF16)

    y_own[0:piece, :] = up_piece(0)
    y_own[piece : 2 * piece, :] = up_piece(3)
    up_line = Line(w, y_own.at[pl.ds(0, 2 * piece)], upout_sum.at[pl.ds(0, 2 * piece)], y_far.at[pl.ds(0, 2 * piece)], 4)
    up_line.start()
    for i, m in ((1, 1), (2, 2)):
        sends[i, 0] = up_piece(m)
        spread_up.append(w.send(sends.at[i, 0], got.at[i, 0], lax.bitwise_xor(own, 2 * m)))
    down_line.collect((3,))
    down_line.total((1,))

    def out_rows(which, k):
        cols = pl.ds(pl.multiple_of((2 * k + which) * piece, piece), piece)
        return tn(att[:, cols], branch_low[...])

    @pl.loop(0, 4)
    def _(k):
        o_send[k] = out_rows(1 - core, k).astype(BF16)

    o_copy = w.send(o_send, o_recv, mate)
    o_copy.wait_recv()
    for i, m in enumerate((3, 1, 2, 0)):
        k = lax.bitwise_xor(chip, m)
        sends[i, 1] = (out_rows(core, k) + o_recv[k].astype(F32)).astype(BF16)
        if m:
            spread_out.append(w.send(sends.at[i, 1], got.at[i, 1], lax.bitwise_xor(own, 2 * m)))
    down_line.collect((4, 5))
    down_line.total((2, 3))

    vec[...] = jnp.zeros_like(vec)
    for row, slot in ((2, 6), (3, 2), (4, 4), (5, 0), (6, 5), (7, 1)):
        vec[row : row + 1, :] = jnp.sum(acc[slot], axis=0, keepdims=True)
    hidden_sum = jnp.sum(acc[3], axis=0, keepdims=True)
    for k in range(4):
        vec[8 + k : 9 + k, :] = jnp.where(chip == k, hidden_sum, jnp.zeros_like(hidden_sum))
    for copy in backs:
        copy.wait_recv()

    got_up, got_out = spread_up, spread_out
    side_line = Line(w, y_own.at[pl.ds(2 * piece, 2 * piece)], upout_sum.at[pl.ds(2 * piece, 2 * piece)], y_far.at[pl.ds(2 * piece, 2 * piece)], 4)
    out_line = Line(w, y_own.at[pl.ds(4 * piece, piece)], upout_sum.at[pl.ds(4 * piece, piece)], y_far.at[pl.ds(4 * piece, piece)], 2)
    lines = [Line(w, l_own.at[p], qkv_sum.at[p], l_far.at[p], 2) for p in range(3)]

    def side_start():
        for copy in got_up:
            copy.wait_recv()
        for row, i in ((2, 1), (3, 2)):
            y_own[row * piece : (row + 1) * piece, :] = got[i, 0]
        side_line.start()

    def out_start():
        for copy in got_out:
            copy.wait_recv()
        y_own[4 * piece :, :] = (sends[3, 1].astype(F32) + got[0, 1].astype(F32) + got[1, 1].astype(F32) + got[2, 1].astype(F32)).astype(BF16)
        out_line.start()

    hooks = {
        0: lambda: (down_line.collect((6, 7)), down_line.total((4, 5))),
        1: lambda: down_line.total((6,)),
        2: lambda: up_line.collect((0,)),
        3: lambda: (side_start(), down_line.total((7,))),
        4: lambda: (up_line.collect((1,)), up_line.total((0,))),
        6: lambda: (up_line.collect((2,)), up_line.total((1,))),
        7: lambda: (up_line.collect((3,)), up_line.total((2,))),
    }

    grads = stage

    def head_cols_of(p, core_index):
        return pl.ds(pl.multiple_of((2 * p + core_index) * head_width, head_width), head_width)

    length, head_cols = q_out.shape
    q, k, v, g, o = q_out, k_out, v_out, grad_heads, o_out
    dk_acc = o_out

    @pl.loop(0, blocks)
    def _(i):
        rows = rows_of(i, BQ)
        prod = jnp.transpose(g[rows, :].astype(F32) * o[rows, :])
        corr[0:1, rows] = jnp.sum(prod[:headd], axis=0, keepdims=True)
        corr[1:2, rows] = jnp.sum(prod[headd:], axis=0, keepdims=True)
        t = jnp.transpose(k[rows, :])
        for h in range(2):
            vt[h, 0:headd, rows] = t[h * headd : (h + 1) * headd]
        dk_acc[rows, :] = jnp.zeros((BQ, head_cols), F32)
        dv_acc[rows, :] = jnp.zeros((BQ, head_cols), F32)

    @pl.loop(0, blocks)
    def _(i):
        rows = rows_of(i, BQ)
        qb = q[rows, :] * jnp.bfloat16(scale)
        gb = g[rows, :]
        zero = jnp.zeros_like(qb)
        qs = (jnp.where(first, qb, zero), jnp.where(first, zero, qb))
        gs = (jnp.where(first, gb, zero), jnp.where(first, zero, gb))
        qz = jnp.concatenate(qs, axis=0)
        gz = jnp.concatenate(gs, axis=0)
        seg_q = seg[:, rows].astype(F32)
        dq = [jnp.zeros((headd, BQ), F32)] * 2
        for j in range(length // BK):
            cols = pl.ds(j * BK, BK)
            kb = k[cols, :]
            vb = v[cols, :]
            same = wide(seg_c[cols, :], BQ) == seg_q
            ps, ds = [], []
            for h in range(2):
                s = jnp.where(same, nt(kb, qs[h]), NEGATIVE)
                p = jnp.exp(s - lse[h : h + 1, rows])
                dp = nt(vb, gs[h])
                dscore = (p * (dp - corr[h : h + 1, rows])).astype(BF16)
                ps.append(p.astype(BF16))
                ds.append(dscore)
                dq[h] = dq[h] + nn(vt[h, 0:headd, cols], dscore)
            dv_acc[cols, :] += nn(jnp.concatenate(ps, axis=1), gz)
            dk_acc[cols, :] += nn(jnp.concatenate(ds, axis=1), qz)
        dqt[0:headd, :] = dq[0]
        dqt[headd:, :] = dq[1]
        act[i // 2, :, head_cols_of(0, lax.rem(i, 2))] = (jnp.transpose(dqt[...]) * scale).astype(BF16)
        for at, hook in hooks.items():

            @pl.when(i == at)
            def _(hook=hook):
                hook()

    @pl.loop(0, blocks)
    def _(i):
        rows = rows_of(i, BQ)
        act[i // 2, :, head_cols_of(1, lax.rem(i, 2))] = dk_acc[rows, :].astype(BF16)
        act[i // 2, :, head_cols_of(2, lax.rem(i, 2))] = dv_acc[rows, :].astype(BF16)

    gather2.drain()
    swaps = []
    for p in range(3):
        cols = pl.ds(pl.multiple_of(p * share + core * head_width, head_width), head_width)
        swaps.append(w.send(act.at[:, :, head_cols_of(p, 1 - core)], grads.at[:, :, cols], mate))
        grads[:, :, cols] = act[:, :, head_cols_of(p, core)]
    v_sum[...] = vec[...]
    for row, p in ((0, 0), (1, 2)):
        total = jnp.sum(act[:, :, 2 * p * head_width : 2 * (p + 1) * head_width].reshape(4 * toks, 2 * head_width).astype(F32), axis=0, keepdims=True)
        total = total[:, 0:head_width] + total[:, head_width:]
        v_sum[row : row + 1, rows_of(own, head_width)] = total
    rounds = [(None, mate), (None, lax.bitwise_xor(own, 2)), (None, lax.bitwise_xor(own, 4)), (lax.bitwise_xor(rep, 1), own), (lax.bitwise_xor(rep, 2), own)]
    flying = []

    def vec_start(i):
        copy = w.remote(v_sum.at[...] if i == 0 else v_recv.at[4 + i], v_recv.at[i], rounds[i][1], rounds[i][0])
        copy.start()
        w.sent.append(copy)
        flying.append(copy)

    def vec_step(i):
        flying[i].wait_recv()
        base = v_sum[...] if i == 0 else v_recv[4 + i]
        if i < 4:
            v_recv[5 + i] = base + v_recv[i]
            vec_start(i + 1)
        else:
            vec_sum[...] = base + v_recv[i]

    vec_start(0)

    def qkv_rows(which, kk, p):
        cols = pl.ds(pl.multiple_of((2 * kk + which) * piece, piece), piece)
        return tn(xs[:, :, cols].reshape(4 * toks, piece), grads[:, :, p * share : (p + 1) * share].reshape(4 * toks, share))

    def theirs(p):
        @pl.loop(0, 4)
        def _(kk):
            q_send[p, kk] = qkv_rows(1 - core, kk, p).astype(BF16)

        return w.send(q_send.at[p], q_recv.at[p], mate)

    moved = []

    def pieces(p, copy):
        copy.wait_recv()

        @pl.loop(0, 4)
        def _(kk):
            q_piece[p, kk] = (qkv_rows(core, kk, p) + q_recv[p, kk].astype(F32)).astype(BF16)

        cols = rows_of(chip, share)
        moved.append([w.send(q_piece.at[p, lax.bitwise_xor(chip, m // 2)], l_own.at[p, :, cols], lax.bitwise_xor(own, m)) for m in (6, 2, 4)])
        l_own[p, :, cols] = q_piece[p, chip]

    def line_start(p):
        for copy in moved[p]:
            copy.wait_recv()
        lines[p].start()

    swaps[0].wait_recv()
    copies = [theirs(0)]
    up_line.total((3,))
    side_line.collect((0,))
    swaps[1].wait_recv()
    copies.append(theirs(1))
    pieces(0, copies[0])
    out_start()
    swaps[2].wait_recv()
    copies.append(theirs(2))
    pieces(1, copies[1])
    side_line.collect((1,))
    side_line.total((0,))
    up_line.arrive(range(4))
    far_copy = w.send(upout_sum.at[pl.ds(piece, piece)], got.at[0, 0], lax.bitwise_xor(own, 6))
    pieces(2, copies[2])
    side_line.collect((2,))
    side_line.total((1,))
    vec_step(0)

    def partial(kk):
        @pl.loop(0, width // tile)
        def _(n):
            cols = rows_of(n, tile)
            part[kk, :, cols] = nt(grads[kk], w_full[cols, :]).astype(BF16)

    gather = Gather(w, part, side, last, half)
    partial(gather.cd)
    side_line.collect((3,))
    side_line.total((2,))
    line_start(0)
    partial(gather.cx)
    line_start(1)
    partial(gather.cy)
    line_start(2)
    gather.send_diagonal()
    gather.send_x()
    gather.send_y()
    out_line.collect((0,))
    side_line.total((3,))
    partial(chip)
    out_line.collect((1,))
    out_line.total((0,))
    vec_step(1)
    step = 32

    def final_rows(which, t):
        rows = pl.ds(pl.multiple_of(which * half + t * step, step), step)
        input_grad[rows, :] = (branch_grad[rows, :] + gather.total(which, t * step, step)).astype(BF16)

    order = [(p, i) for p in range(3) for i in range(2)]

    def hop(at):
        if at < len(order):
            lines[order[at][0]].collect((order[at][1],))
        if at >= 1:
            lines[order[at - 1][0]].total((order[at - 1][1],))

    hop(0)
    out_line.total((1,))
    hop(1)
    gather.relay()
    vec_step(2)
    for at in range(2, 4):
        hop(at)
    vec_step(3)
    gather.wait_first()
    pl.loop(0, half // step)(functools.partial(final_rows, 0))
    hop(4)
    vec_step(4)
    gather.wait_second()
    pl.loop(0, half // step)(functools.partial(final_rows, 1))
    for at in range(5, len(order) + 1):
        hop(at)
    down_line.arrive(range(8))
    spill = [w.local(down_sum, h_down)]
    side_line.arrive(range(4))
    out_line.arrive(range(2))
    far_copy.wait_recv()
    for to, src_ref in ((0, upout_sum.at[pl.ds(0, piece)]), (1, got.at[0, 0])):
        spill.append(w.local(src_ref, h_upout.at[pl.ds(to * piece, piece)]))
    spill.append(w.local(upout_sum.at[pl.ds(2 * piece, 3 * piece)], h_upout.at[pl.ds(2 * piece, 3 * piece)]))
    for p in range(3):
        lines[p].arrive(range(2))
        spill.append(w.local(qkv_sum.at[p], h_qkv.at[p]))
    spill += [w.local(s, d) for s, d in ((output, h_output), (input_grad, h_input_grad), (vec_sum, h_vec))]
    for line in [down_line, up_line, side_line, out_line] + lines:
        line.finish()
    for copy in spill:
        copy.wait()
    qkv_hops.finish()
    hops.finish()
    w.finish()


def layer(scale, seg, x, cot, qkv_w, up_w, out_w, down_w, proj_bias, hidden_bias, gain, shift):
    toks, width = x.shape
    piece = up_w.shape[0]
    ff = 2 * down_w.shape[0]
    half = toks // 2
    share = width // 4
    head_width = width // 8
    length = 8 * toks
    shape = jax.ShapeDtypeStruct
    vm = pltpu.VMEM
    five = (5 * piece, width)
    small = vm((3, 4, piece, share), BF16)
    three = (3, piece, width)
    rows4 = vm((4, toks, width), BF16)
    block = vm((toks, width), BF16)
    block32 = vm((toks, width), F32)
    pieces = vm((4, piece, width), BF16)
    halfff = vm((ff // 2, width), BF16)
    heads = vm((length, head_width), BF16)
    heads32 = vm((length, head_width), F32)
    return pl.pallas_call(
        functools.partial(layer_body, scale),
        name="layer",
        out_shape=(
            shape((toks, width), BF16), shape((toks, width), BF16), shape(three, BF16), shape(five, BF16), shape((ff // 2, width), BF16), shape((16, width), F32),
        ),
        in_specs=[VM, VM, VM, VM, HBM, HBM, HBM] + [VM] * 4,
        out_specs=(HBM,) * 6,
        scratch_shapes=[
            heads, heads, heads, heads32, vm((8, length), F32), rows4, vm((8 * piece, 3 * share), BF16), block, block32, heads, vm((16, width), F32), halfff,
            vm((4, 2, piece, width), BF16),
            vm((4, toks, 3 * share), BF16), vm((2, head_width // 2 + 16, length), BF16), heads32, heads, block,
            vm((width, width), BF16), vm((width, ff), BF16), vm((ff, width), BF16), block32, block32, vm((toks, 128), F32),
            rows4, vm((4, toks, ff), BF16), vm((4, toks, ff), BF16), rows4, vm((4, half, width), BF16), vm((2, half, width), BF16), rows4, vm((4, toks, ff), BF16),
            block, block, vm((8, 8, width), F32), halfff, halfff, halfff, halfff, pieces, pieces, pieces, pieces,
            vm((8, length), F32), heads32, vm((head_width, BQ), F32), small, small, small, vm(three, BF16), vm(three, BF16), vm((3, 2, piece, width), BF16),
            vm(five, BF16), vm(five, BF16), vm(five, BF16), vm(three, BF16), block, vm((16, width), F32), vm((9, 16, width), F32), vm((16, width), F32),
            pltpu.SemaphoreType.DMA((320,)), pltpu.SemaphoreType.DMA((320,)), pltpu.SemaphoreType.DMA((40,)),
        ],
        compiler_params=pltpu.CompilerParams(collective_id=1, has_side_effects=True, vmem_limit_bytes=63 << 20),
    )(seg, x, cot, qkv_w, up_w, out_w, down_w, proj_bias, hidden_bias, gain, shift)


def emit_body(
    grad_scale, who, h_low, h_grad, h_qkv, h_upout, h_down, h_vec,
    output, input_grad, h_qkv_total, h_out_total, h_up_total, h_down_total, bias_total, hidden_total, gain_total, shift_total,
    qkv_sum, upout_sum, down_sum, vec_sum, qkv_total, out_total, up_total, down_total, sems,
):
    width = h_low.shape[1]
    piece = qkv_sum.shape[1]
    pairs = ((h_down, down_sum), (h_upout, upout_sum), (h_qkv, qkv_sum), (h_vec, vec_sum), (h_low, output), (h_grad, input_grad))
    copies = [pltpu.make_async_copy(src, dst, sems.at[i]) for i, (src, dst) in enumerate(pairs)]
    for copy in copies:
        copy.start()
    chip = who[0]
    sent = []

    def leave(src, dst):
        copy = pltpu.make_async_copy(src, dst, sems.at[6 + len(sent)])
        copy.start()
        sent.append(copy)

    copies[0].wait()
    down_total[...] = down_sum[...].astype(F32) * grad_scale
    leave(down_total, h_down_total)
    copies[1].wait()
    for at, m in enumerate((0, 3, 1, 2)):
        up_total[:, rows_of(lax.bitwise_xor(chip, m), width)] = upout_sum[at * piece : (at + 1) * piece, :].astype(F32) * grad_scale
    leave(up_total, h_up_total)
    out_total[...] = upout_sum[4 * piece :, :].astype(F32) * grad_scale
    leave(out_total, h_out_total)
    copies[2].wait()
    for p in range(3):
        qkv_total[:, p * width : (p + 1) * width] = qkv_sum[p].astype(F32) * grad_scale
    leave(qkv_total, h_qkv_total)
    copies[3].wait()
    bias_total[...] = vec_sum[0:4] * grad_scale
    gain_total[...] = vec_sum[4:6] * grad_scale
    shift_total[...] = vec_sum[6:8] * grad_scale
    for kk in range(4):
        hidden_total[:, kk * width : (kk + 1) * width] = vec_sum[8 + kk : 9 + kk] * grad_scale
    for copy in copies[4:] + sent:
        copy.wait()


def emit(grad_scale, who, low, grad, qkv_sum, upout_sum, down_sum, vec_sum):
    toks, width = low.shape
    piece = qkv_sum.shape[1]
    shape = jax.ShapeDtypeStruct
    return pl.pallas_call(
        functools.partial(emit_body, grad_scale),
        name="emit",
        out_shape=(
            shape((toks, width), BF16), shape((toks, width), BF16), shape((piece, 3 * width), F32), shape((piece, width), F32), shape((piece, 4 * width), F32),
            shape(down_sum.shape, F32), shape((4, width), F32), shape((1, 4 * width), F32), shape((2, width), F32), shape((2, width), F32),
        ),
        in_specs=[SM] + [HBM] * 6,
        out_specs=(VM, VM) + (HBM,) * 4 + (VM,) * 4,
        scratch_shapes=[
            pltpu.VMEM(qkv_sum.shape, BF16), pltpu.VMEM(upout_sum.shape, BF16), pltpu.VMEM(down_sum.shape, BF16), pltpu.VMEM(vec_sum.shape, F32),
            pltpu.VMEM((piece, 3 * width), F32), pltpu.VMEM((piece, width), F32), pltpu.VMEM((piece, 4 * width), F32), pltpu.VMEM(down_sum.shape, F32),
            pltpu.SemaphoreType.DMA((10,)),
        ],
        compiler_params=pltpu.CompilerParams(vmem_limit_bytes=62 << 20),
    )(who, low, grad, qkv_sum, upout_sum, down_sum, vec_sum)


def local_tensor(tokens, segment_ids, qkv_weight, out_weight, up_weight, down_weight, proj_bias, hidden_bias, norm_gain, norm_shift, cotangent):
    inputs = tokens[0]
    toks, width = inputs.shape
    scale = (width // HEADS) ** (-0.5)
    grad_scale = (toks * lax.axis_size("fsdp") * lax.axis_size("rep")) ** (-0.5)
    low, grad, qkv_sum, upout_sum, down_sum, vec_sum = layer(
        scale, segment_ids, inputs, cotangent[0], qkv_weight, up_weight, out_weight, down_weight, proj_bias, hidden_bias[None], norm_gain, norm_shift
    )
    output, input_grad, qkv_total, out_total, up_total, down_total, bias_total, hidden_total, gain_total, shift_total = emit(
        grad_scale, (lax.axis_index("fsdp") // 2).reshape(1), low, grad, qkv_sum, upout_sum, down_sum, vec_sum
    )
    return (
        output[None],
        input_grad[None],
        qkv_total,
        out_total,
        up_total,
        down_total,
        bias_total,
        hidden_total.reshape(4 * width),
        gain_total,
        shift_total,
    )


def normalize(hidden, gain, shift):
    center = hidden - jnp.mean(hidden, axis=-1, keepdims=True)
    spread = jnp.mean(center * center, axis=-1, keepdims=True)
    return center * lax.rsqrt(spread + 1e-05) * gain + shift


def exact_gelu(value):
    return jax.nn.gelu(value, approximate=False)


def gather_attention(qkv_weight, out_weight):
    return (
        lax.all_gather(qkv_weight, "fsdp", axis=0, tiled=True),
        lax.all_gather(out_weight, "fsdp", axis=0, tiled=True),
    )


def gather_feedforward(up_weight, down_weight):
    return (
        lax.all_gather(up_weight, "fsdp", axis=0, tiled=True),
        lax.all_gather(down_weight, "fsdp", axis=0, tiled=True),
    )


def block_plan(row_count):
    block_rows = math.gcd(row_count, 1024)
    return (block_rows, row_count // block_rows)


def split_heads(matrix):
    return matrix.reshape(matrix.shape[0], HEADS, matrix.shape[1] // HEADS)


def join_heads(stacked):
    return jnp.transpose(stacked, (1, 0, 2)).reshape(
        stacked.shape[1], stacked.shape[0] * stacked.shape[2]
    )


def local_gather(
    tokens,
    segment_ids,
    qkv_weight,
    out_weight,
    up_weight,
    down_weight,
    proj_bias,
    hidden_bias,
    norm_gain,
    norm_shift,
    cotangent,
):
    inputs = tokens[0]
    tok_count, model_width = inputs.shape
    head_dim = model_width // HEADS
    score_scale = head_dim ** (-0.5)
    doc_ids = segment_ids[0]
    own_index = lax.axis_index("fsdp")
    own_docs = lax.dynamic_slice_in_dim(doc_ids, own_index * tok_count, tok_count)
    qkv_full, out_full = gather_attention(qkv_weight, out_weight)
    projected = jnp.dot(inputs, qkv_full, preferred_element_type=jnp.float32)
    queries = (projected[:, :model_width] + proj_bias[0]).astype(jnp.bfloat16)
    key_rows = projected[:, model_width : 2 * model_width].astype(jnp.bfloat16)
    value_rows = (projected[:, 2 * model_width :] + proj_bias[1]).astype(jnp.bfloat16)
    query_heads = split_heads(queries)
    key_own = split_heads(key_rows)
    value_own = split_heads(value_rows)
    initial = (
        jnp.zeros((HEADS, tok_count, head_dim), jnp.float32),
        jnp.full((HEADS, tok_count), NEGATIVE, jnp.float32),
        jnp.zeros((HEADS, tok_count), jnp.float32),
    )
    key_piece = lax.all_gather(key_rows, "fsdp", axis=0, tiled=True)
    value_piece = lax.all_gather(value_rows, "fsdp", axis=0, tiled=True)
    block_rows, blocks = block_plan(key_piece.shape[0])

    def forward_advance(block_index, running_state):
        weighted, running, denominator = running_state
        offset = block_index * block_rows
        key_block = split_heads(lax.dynamic_slice_in_dim(key_piece, offset, block_rows))
        value_block = split_heads(lax.dynamic_slice_in_dim(value_piece, offset, block_rows))
        block_docs = lax.dynamic_slice_in_dim(doc_ids, offset, block_rows)
        scores = (
            jnp.einsum("qhd,khd->hqk", query_heads, key_block, preferred_element_type=jnp.float32)
            * score_scale
        )
        same_doc = (own_docs[:, None] == block_docs[None, :])[None]
        highest = jnp.maximum(running, jnp.max(jnp.where(same_doc, scores, NEGATIVE), axis=2))
        factor = jnp.exp(running - highest)
        weights = jnp.where(same_doc, jnp.exp(scores - highest[:, :, None]), 0.0)
        denominator = denominator * factor + jnp.sum(weights, axis=2)
        weighted = weighted * factor[:, :, None] + jnp.einsum(
            "hqk,khd->hqd",
            weights.astype(jnp.bfloat16),
            value_block,
            preferred_element_type=jnp.float32,
        )
        return (weighted, highest, denominator)

    weighted, running, denominator = lax.fori_loop(0, blocks, forward_advance, initial)
    attended_heads = weighted / denominator[:, :, None]
    log_total = running + jnp.log(denominator)
    attended_low = join_heads(attended_heads).astype(jnp.bfloat16)
    branch = jnp.dot(attended_low, out_full, preferred_element_type=jnp.float32) + proj_bias[2]
    first_norm, norm_one_back = jax.vjp(
        normalize, inputs.astype(jnp.float32) + branch, norm_gain[0], norm_shift[0]
    )
    first_low = first_norm.astype(jnp.bfloat16)
    up_full, down_full = gather_feedforward(up_weight, down_weight)
    hidden_pre = jnp.dot(first_low, up_full, preferred_element_type=jnp.float32) + hidden_bias
    activated, gelu_back = jax.vjp(exact_gelu, hidden_pre)
    activated_low = activated.astype(jnp.bfloat16)
    second = jnp.dot(activated_low, down_full, preferred_element_type=jnp.float32) + proj_bias[3]
    output, norm_two_back = jax.vjp(normalize, first_norm + second, norm_gain[1], norm_shift[1])
    up_back, down_back = gather_feedforward(up_weight, down_weight)
    qkv_back, out_back = gather_attention(qkv_weight, out_weight)
    grad_second, gain_two, shift_two = norm_two_back(cotangent[0].astype(jnp.float32))
    second_low = grad_second.astype(jnp.bfloat16)
    down_term = jnp.einsum(
        "tf,td->fd", activated_low, second_low, preferred_element_type=jnp.float32
    )
    activated_grad = jnp.einsum(
        "td,fd->tf", second_low, down_back, preferred_element_type=jnp.float32
    )
    (pre_grad,) = gelu_back(activated_grad)
    pre_low = pre_grad.astype(jnp.bfloat16)
    up_term = jnp.einsum("td,tf->df", first_low, pre_low, preferred_element_type=jnp.float32)
    first_grad = grad_second + jnp.einsum(
        "tf,df->td", pre_low, up_back, preferred_element_type=jnp.float32
    )
    branch_grad, gain_one, shift_one = norm_one_back(first_grad)
    branch_low = branch_grad.astype(jnp.bfloat16)
    out_term = jnp.einsum("te,td->ed", attended_low, branch_low, preferred_element_type=jnp.float32)
    attended_grad = jnp.einsum(
        "td,ed->te", branch_low, out_back, preferred_element_type=jnp.float32
    ).astype(jnp.bfloat16)
    grad_heads = split_heads(attended_grad)
    correction = jnp.einsum("qhd,hqd->hq", grad_heads.astype(jnp.float32), attended_heads)
    lse_all, correction_all = (
        lax.all_gather(log_total, "fsdp", axis=1, tiled=True),
        lax.all_gather(correction, "fsdp", axis=1, tiled=True),
    )
    query_key_piece = lax.all_gather(key_rows, "fsdp", axis=0, tiled=True)
    query_value_piece = lax.all_gather(value_rows, "fsdp", axis=0, tiled=True)
    query_block_rows, blocks = block_plan(query_key_piece.shape[0])

    def query_advance(block_index, query_state):
        offset = block_index * query_block_rows
        key_block = split_heads(lax.dynamic_slice_in_dim(query_key_piece, offset, query_block_rows))
        value_block = split_heads(
            lax.dynamic_slice_in_dim(query_value_piece, offset, query_block_rows)
        )
        block_docs = lax.dynamic_slice_in_dim(doc_ids, offset, query_block_rows)
        scores = (
            jnp.einsum("qhd,khd->hqk", query_heads, key_block, preferred_element_type=jnp.float32)
            * score_scale
        )
        same_doc = (own_docs[:, None] == block_docs[None, :])[None]
        probabilities = jnp.where(same_doc, jnp.exp(scores - log_total[:, :, None]), 0.0)
        prob_grad = jnp.einsum(
            "qhd,khd->hqk", grad_heads, value_block, preferred_element_type=jnp.float32
        )
        score_grad = (probabilities * (prob_grad - correction[:, :, None])).astype(jnp.bfloat16)
        return query_state + jnp.einsum(
            "hqk,khd->hqd", score_grad, key_block, preferred_element_type=jnp.float32
        )

    query_acc = lax.fori_loop(
        0, blocks, query_advance, jnp.zeros((HEADS, tok_count, head_dim), jnp.float32)
    )
    query_grad = (join_heads(query_acc) * score_scale).astype(jnp.bfloat16)
    empty_heads = jnp.zeros((HEADS, tok_count, head_dim), jnp.float32)
    query_piece = lax.all_gather(queries, "fsdp", axis=0, tiled=True)
    grad_piece = lax.all_gather(attended_grad, "fsdp", axis=0, tiled=True)
    key_block_rows, blocks = block_plan(query_piece.shape[0])

    def key_advance(block_index, key_state):
        key_acc, value_acc = key_state
        offset = block_index * key_block_rows
        query_block = split_heads(lax.dynamic_slice_in_dim(query_piece, offset, key_block_rows))
        grad_block = split_heads(lax.dynamic_slice_in_dim(grad_piece, offset, key_block_rows))
        block_docs = lax.dynamic_slice_in_dim(doc_ids, offset, key_block_rows)
        lse_block = lax.dynamic_slice_in_dim(lse_all, offset, key_block_rows, axis=1)
        corr_block = lax.dynamic_slice_in_dim(correction_all, offset, key_block_rows, axis=1)
        scores = (
            jnp.einsum("qhd,khd->hqk", query_block, key_own, preferred_element_type=jnp.float32)
            * score_scale
        )
        same_doc = (block_docs[:, None] == own_docs[None, :])[None]
        probabilities = jnp.where(same_doc, jnp.exp(scores - lse_block[:, :, None]), 0.0)
        value_acc = value_acc + jnp.einsum(
            "hqk,qhd->hkd",
            probabilities.astype(jnp.bfloat16),
            grad_block,
            preferred_element_type=jnp.float32,
        )
        prob_grad = jnp.einsum(
            "qhd,khd->hqk", grad_block, value_own, preferred_element_type=jnp.float32
        )
        score_grad = (probabilities * (prob_grad - corr_block[:, :, None])).astype(jnp.bfloat16)
        key_acc = key_acc + jnp.einsum(
            "hqk,qhd->hkd", score_grad, query_block, preferred_element_type=jnp.float32
        )
        return (key_acc, value_acc)

    key_acc, value_acc = lax.fori_loop(0, blocks, key_advance, (empty_heads, empty_heads))
    key_grad = (join_heads(key_acc) * score_scale).astype(jnp.bfloat16)
    value_grad = join_heads(value_acc).astype(jnp.bfloat16)
    qkv_grad_low = jnp.concatenate([query_grad, key_grad, value_grad], axis=1)
    qkv_term = jnp.einsum("td,te->de", inputs, qkv_grad_low, preferred_element_type=jnp.float32)
    input_grad = branch_grad + jnp.einsum(
        "te,de->td", qkv_grad_low, qkv_back, preferred_element_type=jnp.float32
    )
    bias_term = jnp.stack(
        [
            jnp.sum(query_grad.astype(jnp.float32), axis=0),
            jnp.sum(value_grad.astype(jnp.float32), axis=0),
            jnp.sum(branch_low.astype(jnp.float32), axis=0),
            jnp.sum(second_low.astype(jnp.float32), axis=0),
        ]
    )
    hidden_term = jnp.sum(pre_low.astype(jnp.float32), axis=0)
    gain_term = jnp.stack([gain_one, gain_two])
    shift_term = jnp.stack([shift_one, shift_two])
    bias_total, hidden_total, gain_total, shift_total = lax.psum(
        (bias_term, hidden_term, gain_term, shift_term), ("rep", "fsdp")
    )
    up_sum, down_sum = (
        lax.psum_scatter(up_term, "fsdp", scatter_dimension=0, tiled=True),
        lax.psum_scatter(down_term, "fsdp", scatter_dimension=0, tiled=True),
    )
    qkv_sum, out_sum = (
        lax.psum_scatter(qkv_term, "fsdp", scatter_dimension=0, tiled=True),
        lax.psum_scatter(out_term, "fsdp", scatter_dimension=0, tiled=True),
    )
    qkv_total, out_total, up_total, down_total = lax.psum(
        (qkv_sum, out_sum, up_sum, down_sum), "rep"
    )
    grad_scale = (tok_count * lax.axis_size("fsdp") * lax.axis_size("rep")) ** (-0.5)
    return (
        output.astype(jnp.bfloat16)[None],
        input_grad.astype(jnp.bfloat16)[None],
        qkv_total * grad_scale,
        out_total * grad_scale,
        up_total * grad_scale,
        down_total * grad_scale,
        bias_total * grad_scale,
        hidden_total * grad_scale,
        gain_total * grad_scale,
        shift_total * grad_scale,
    )


def solution(mesh):
    small = mesh.shape["fsdp"] == 8 and mesh.shape["rep"] == 4
    local = local_tensor if small else local_gather
    return jax.shard_map(
        local,
        mesh=mesh,
        in_specs=(
            P("rep", "fsdp", None),
            P("rep", None),
            P("fsdp", None),
            P("fsdp", None),
            P("fsdp", None),
            P("fsdp", None),
            P(),
            P(),
            P(),
            P(),
            P("rep", "fsdp", None),
        ),
        out_specs=(
            P("rep", "fsdp", None),
            P("rep", "fsdp", None),
            P("fsdp", None),
            P("fsdp", None),
            P("fsdp", None),
            P("fsdp", None),
            P(),
            P(),
            P(),
            P(),
        ),
        check_vma=False,
    )
```

```python
import functools
import math

import jax
import jax.numpy as jnp
from jax import lax
from jax.experimental import pallas as pl
from jax.experimental.pallas import tpu as pltpu
from jax.sharding import PartitionSpec as P

HEADS = 16

NEGATIVE = -1e30
BQ = 256
BK = 512
VM = pl.BlockSpec(memory_space=pltpu.VMEM)
SM = pl.BlockSpec(memory_space=pltpu.SMEM)


def nt(a, b):
    return lax.dot_general(a, b, (((1,), (1,)), ((), ())), preferred_element_type=jnp.float32)


def nn(a, b):
    return jnp.dot(a, b, preferred_element_type=jnp.float32)


def head_lanes(shape, half):
    return lax.broadcasted_iota(jnp.int32, shape, 1) < half


def rows_of(index, size):
    return pl.ds(pl.multiple_of(index * size, size), size)


def seg_columns(seg_v, seg_c):
    length = seg_c.shape[0]

    @pl.loop(0, length // BQ)
    def _(i):
        rows = rows_of(i, BQ)
        seg_c[rows, :] = jnp.transpose(jnp.broadcast_to(seg_v[:, rows].astype(jnp.float32), (128, BQ)))


def wide(column, lanes):
    return jnp.concatenate([column] * (lanes // 128), axis=1)


MESH = pl.DeviceIdType.MESH
HBM = pl.BlockSpec(memory_space=pltpu.HBM)
F32 = jnp.float32
BF16 = jnp.bfloat16


def tn(a, b):
    return lax.dot_general(a, b, (((0,), (0,)), ((), ())), preferred_element_type=F32)


def fold_rows(v):
    return jnp.sum(v.reshape(v.shape[0] // 8, 8, v.shape[1]), axis=0)


class Wires:
    def __init__(self, send_sems, recv_sems, local_sems):
        self.send_sems, self.recv_sems, self.local_sems = send_sems, recv_sems, local_sems
        self.count = 0
        self.local_count = 0
        self.sent = []
        self.rep = lax.axis_index("rep")
        self.own = lax.axis_index("fsdp")

    def remote(self, src, dst, peer, rep=None):
        i = self.count
        self.count = i + 1
        return pltpu.make_async_remote_copy(
            src_ref=src, dst_ref=dst, send_sem=self.send_sems.at[i], recv_sem=self.recv_sems.at[i],
            device_id=(self.rep if rep is None else rep, peer), device_id_type=MESH,
        )

    def send(self, src, dst, peer):
        copy = self.remote(src, dst, peer)
        copy.start()
        self.sent.append(copy)
        return copy

    def local(self, src, dst):
        copy = pltpu.make_async_copy(src, dst, self.local_sems.at[self.local_count])
        self.local_count += 1
        copy.start()
        return copy

    def greet(self, peers):
        barrier = pltpu.get_barrier_semaphore()
        for rep, peer in peers:
            pl.semaphore_signal(barrier, inc=1, device_id=(rep, peer), device_id_type=MESH)
        pl.semaphore_wait(barrier, len(peers))

    def drain(self, copies):
        for copy in copies:
            copy.wait_send()
            self.sent = [other for other in self.sent if other is not copy]

    def finish(self):
        for copy in self.sent:
            copy.wait_send()


class Line:
    def __init__(self, wires, own, land, far, count, size=None):
        self.own, self.land, self.far = own, land, far
        rep, dev = wires.rep, wires.own
        size = own.shape[0] // count if size is None else size
        self.rows = [pl.ds(i * size, size) for i in range(count)]
        self.inner = jnp.logical_or(rep == 1, rep == 2)
        self.outer = jnp.logical_not(self.inner)
        near, across = lax.bitwise_xor(rep, 1), lax.bitwise_xor(rep, 3)
        self.first = [wires.remote(own.at[r], land.at[r], dev, near) for r in self.rows]
        self.middle = [wires.remote(own.at[r], far.at[r], dev, across) for r in self.rows]
        self.back = [wires.remote(land.at[r], land.at[r], dev, near) for r in self.rows]

    def start(self):
        @pl.when(self.outer)
        def _():
            for copy in self.first:
                copy.start()

    def collect(self, which):
        @pl.when(self.inner)
        def _():
            for i in which:
                r = self.rows[i]
                self.first[i].wait_recv()
                self.own[r, :] = (self.own[r, :].astype(F32) + self.land[r, :].astype(F32)).astype(BF16)
                self.middle[i].start()

    def total(self, which):
        @pl.when(self.inner)
        def _():
            for i in which:
                r = self.rows[i]
                self.middle[i].wait_recv()
                self.land[r, :] = (self.own[r, :].astype(F32) + self.far[r, :].astype(F32)).astype(BF16)
                self.back[i].start()

    def arrive(self, which):
        @pl.when(self.outer)
        def _():
            for i in which:
                self.back[i].wait_recv()

    def finish(self):
        @pl.when(self.outer)
        def _():
            for copy in self.first:
                copy.wait_send()

        @pl.when(self.inner)
        def _():
            for i in range(len(self.rows)):
                self.middle[i].wait_send()
                self.back[i].wait_send()


class Hops:
    def __init__(self, wires, view):
        rep, reps = wires.rep, 4
        self.all = []
        for hop in range(1, reps):
            for step in (1, -1):
                index, to, come = rep - step * (hop - 1), rep + step, rep - step * hop
                going = (index >= 0) & (index < reps) & (to >= 0) & (to < reps)
                coming = (come >= 0) & (come < reps)
                refs = view(jnp.clip(index, 0, reps - 1))
                copies = [wires.remote(ref, ref, wires.own, jnp.clip(to, 0, reps - 1)) for ref in refs]
                self.all.append((hop, going, coming, copies))

    def each(self, hop, kind):
        for at, going, coming, copies in self.all:
            if hop in (0, at):

                @pl.when(coming if kind == "wait_recv" else going)
                def _():
                    for copy in copies:
                        getattr(copy, kind)()

    def start(self, hop):
        self.each(hop, "start")

    def wait(self, hop):
        self.each(hop, "wait_recv")

    def finish(self):
        self.each(0, "wait_send")


class Spread:
    def __init__(self, wires, slots, half):
        self.wires, self.slots, self.half = wires, slots, half
        self.chip = wires.own // 2
        self.x, self.y = lax.bitwise_xor(wires.own, 2), lax.bitwise_xor(wires.own, 4)
        self.cx, self.cy, self.cd = (lax.bitwise_xor(self.chip, m) for m in (1, 2, 3))
        self.a, self.b = pl.ds(0, half), pl.ds(half, half)

    def piece(self, chip, part):
        return self.slots.at[chip, part]

    def put(self, chip, part, peer):
        return self.wires.send(self.piece(chip, part), self.piece(chip, part), peer)

    def first_half(self):
        self.xa = self.put(self.chip, self.a, self.x)
        self.ya = self.put(self.chip, self.a, self.y)

    def second_half(self):
        self.yb = self.put(self.chip, self.b, self.y)
        self.xb = self.put(self.chip, self.b, self.x)

    def relay(self):
        self.xa.wait_recv()
        self.da = self.put(self.cx, self.a, self.y)
        self.yb.wait_recv()
        self.db = self.put(self.cy, self.b, self.x)

    def wait_sides(self):
        self.xb.wait_recv()
        self.ya.wait_recv()

    def wait_diagonal(self):
        self.da.wait_recv()
        self.db.wait_recv()


class Gather:
    def __init__(self, wires, part, side, last, half):
        self.wires, self.part, self.side, self.last, self.half = wires, part, side, last, half
        self.chip = wires.own // 2
        self.x, self.y = lax.bitwise_xor(wires.own, 2), lax.bitwise_xor(wires.own, 4)
        self.cx, self.cy, self.cd = (lax.bitwise_xor(self.chip, m) for m in (1, 2, 3))
        self.a, self.b = pl.ds(0, half), pl.ds(half, half)

    def send_x(self):
        self.x_own = self.wires.send(self.part.at[self.cx, self.a], self.side.at[0], self.x)

    def send_y(self):
        self.y_own = self.wires.send(self.part.at[self.cy, self.b], self.side.at[1], self.y)

    def send_diagonal(self):
        self.x_far = self.wires.send(self.part.at[self.cd, self.a], self.side.at[2], self.x)
        self.y_far = self.wires.send(self.part.at[self.cd, self.b], self.side.at[3], self.y)

    def relay(self):
        step = 32

        def add(chip, start, slot):
            @pl.loop(0, self.half // step)
            def _(t):
                rows = pl.ds(pl.multiple_of(start + t * step, step), step)
                near = self.part[chip, rows, :].astype(F32) + self.side[slot, rows_of(t, step), :].astype(F32)
                self.part[chip, rows, :] = near.astype(BF16)

        self.x_far.wait_recv()
        add(self.cy, 0, 2)
        self.y_last = self.wires.send(self.part.at[self.cy, self.a], self.last.at[0], self.y)
        self.y_far.wait_recv()
        add(self.cx, self.half, 3)
        self.x_last = self.wires.send(self.part.at[self.cx, self.b], self.last.at[1], self.x)

    def drain(self):
        for copy in (self.x_own, self.y_own, self.x_far, self.y_far, self.x_last, self.y_last):
            copy.wait_send()
            self.wires.sent = [other for other in self.wires.sent if other is not copy]

    def wait_first(self):
        self.x_own.wait_recv()
        self.y_last.wait_recv()

    def wait_second(self):
        self.y_own.wait_recv()
        self.x_last.wait_recv()

    def total(self, which, offset, size):
        rows = pl.ds(pl.multiple_of(which * self.half + offset, size), size)
        here = pl.ds(pl.multiple_of(offset, size), size)
        return self.part[self.chip, rows, :].astype(F32) + self.side[which, here, :].astype(F32) + self.last[which, here, :].astype(F32)


def layer_body(
    scale, seg, x, cot, qkv_w, up_w, out_w, down_w, proj_bias, hidden_bias, gain, shift,
    h_output, h_input_grad, h_qkv, h_upout, h_down, h_vec,
    q_out, k_out, v_out, o_out, lse, xs, w_full, output, branch_grad, grad_heads, vec, down_grad, sends,
    stage, vt, seg_c, low, att, out_full, up_full, down_full, h1, z1, r1, fl, act, slope, part, side, last, sl, pre,
    branch_low, agl, acc, d_send, d_recv, d_far, down_sum, u_send, u_recv, o_send, o_recv,
    corr, dv_acc, dqt, q_send, q_recv, q_piece, l_own, l_far, got, y_own, y_far, upout_sum, qkv_sum, input_grad, v_sum, v_recv, vec_sum,
    send_sems, recv_sems, local_sems,
):
    w = Wires(send_sems, recv_sems, local_sems)
    own, rep = w.own, w.rep
    core, chip = lax.rem(own, 2), own // 2
    mate = lax.bitwise_xor(own, 1)
    cx, cy, cd = (lax.bitwise_xor(chip, m) for m in (1, 2, 3))
    others = (cd, cx, cy)
    toks, width = x.shape
    ff = up_full.shape[1]
    share = width // 4
    head_width = share // 2
    half = toks // 2
    piece = up_w.shape[0]
    quarter = piece // 4
    tile = 256
    w.greet(
        [(rep, lax.bitwise_xor(own, m)) for m in range(1, 8)]
        + [(lax.bitwise_xor(rep, m), own) for m in (1, 2, 3)]
    )

    mine, some = rows_of(own, piece), rows_of(rep, quarter)

    def quarter_of(full, k, r, cols=slice(None)):
        return full.at[pl.ds(pl.multiple_of((2 * k + core) * piece + r * quarter, quarter), quarter), cols]

    def qkv_cols(p, to_chip):
        return pl.ds(pl.multiple_of(p * width + to_chip * share, share), share)

    first_fetch = []
    for mask in (6, 2, 4):
        peer, to_chip = lax.bitwise_xor(own, mask), lax.bitwise_xor(chip, mask // 2)
        for p in range(3):
            first_fetch.append(w.send(qkv_w.at[some, qkv_cols(p, to_chip)], quarter_of(w_full, chip, rep, pl.ds(p * share, share)), peer))
    xs[chip] = x[...]
    spread0 = Spread(w, xs, half)
    spread0.first_half()
    spread0.second_half()
    fetch = []
    for mask in (6, 2, 4):
        peer, to_chip = lax.bitwise_xor(own, mask), lax.bitwise_xor(chip, mask // 2)
        fetch.append(w.send(up_w.at[some, rows_of(to_chip, ff)], quarter_of(up_full, chip, rep), peer))
        fetch.append(w.send(out_w.at[some], quarter_of(out_full, chip, rep), peer))
    here, there = [], []
    for p in range(3):
        src, dst = qkv_w.at[:, qkv_cols(p, chip)], w_full.at[mine, pl.ds(p * share, share)]
        here.append(w.local(src, dst))
        there.append(w.send(src, dst, mate))
    kept = []
    for src, dst in ((up_w.at[:, rows_of(chip, ff)], up_full.at[mine]), (out_w, out_full.at[mine]), (down_w, down_full.at[rows_of(core, ff // 2)])):
        kept.append((w.local(src, dst), w.send(src, dst, mate)))
    qkv_hops = Hops(w, lambda r: [quarter_of(w_full, k, r) for k in others])
    hops = Hops(w, lambda r: [quarter_of(full, k, r) for full in (up_full, out_full) for k in others])
    for copy in first_fetch:
        copy.wait_recv()
    qkv_hops.start(1)
    seg_columns(seg, seg_c)
    qkv_hops.wait(1)
    qkv_hops.start(2)
    spread0.relay()
    qkv_hops.wait(2)
    qkv_hops.start(3)
    for copy in fetch:
        copy.wait_recv()
    hops.start(1)
    qkv_hops.wait(3)
    for k in others:
        rows = rows_of(2 * k + core, piece)
        there.append(w.send(w_full.at[rows], w_full.at[rows], mate))
    for copy in here:
        copy.wait()
    for copy in there:
        copy.wait_recv()

    outs = (q_out, k_out, v_out)
    trades = []

    def block(k):
        rows = rows_of(2 * k + core, toks)
        for p in range(3):
            r = nn(xs[k], w_full[:, pl.ds(p * share, share)])
            if p != 1:
                r = r + proj_bias[p // 2 : p // 2 + 1, rows_of(chip, share)]
            stage[k, :, pl.ds(p * share, share)] = r.astype(BF16)
            theirs = pl.ds(pl.multiple_of(p * share + (1 - core) * head_width, head_width), head_width)
            trades.append(w.send(stage.at[k, :, theirs], outs[p].at[rows], mate))
            outs[p][rows, :] = stage[k, :, pl.ds(pl.multiple_of(p * share + core * head_width, head_width), head_width)]

    block(chip)
    spread0.wait_sides()
    block(cx)
    block(cy)
    hops.wait(1)
    hops.start(2)
    spread0.wait_diagonal()
    block(cd)
    for copy in trades:
        copy.wait_recv()
    w.drain(trades)

    headd = head_width // 2
    blocks = q_out.shape[0] // BQ
    first = head_lanes((BQ, head_width), headd)

    @pl.loop(0, blocks)
    def _(i):
        rows = rows_of(i, BQ)
        t = jnp.transpose(v_out[rows, :])
        for h in range(2):
            vt[h, 0:headd, rows] = t[h * headd : (h + 1) * headd]
            vt[h, headd : headd + 16, rows] = jnp.ones((16, BQ), BF16)

    swaps = {}
    for mask in range(1, 8):
        peer = lax.bitwise_xor(own, mask)
        swaps[mask] = w.remote(low.at[rows_of(peer, toks)], att.at[:, rows_of(own, head_width)], peer)

    @pl.loop(0, blocks)
    def _(t):
        i = lax.bitwise_xor(own, 7 - t)
        rows = rows_of(i, BQ)
        qb = q_out[rows, :] * jnp.bfloat16(scale)
        zero = jnp.zeros_like(qb)
        qs = (jnp.where(first, qb, zero), jnp.where(first, zero, qb))
        seg_q = seg[:, rows].astype(F32)
        both = []
        for h in range(2):
            scores = []
            for j in range(blocks):
                cols = pl.ds(j * BQ, BQ)
                same = wide(seg_c[cols, :], BQ) == seg_q
                scores.append(jnp.where(same, nt(k_out[cols, :], qs[h]), NEGATIVE))
            top = functools.reduce(jnp.maximum, [jnp.max(s, axis=0, keepdims=True) for s in scores])
            total = jnp.zeros((headd + 16, BQ), F32)
            for j in range(blocks):
                total = total + nn(vt[h, :, pl.ds(j * BQ, BQ)], jnp.exp(scores[j] - top).astype(BF16))
            norm = total[headd : headd + 1]
            both.append(total[0:headd] / norm)
            lse[h : h + 1, rows] = top + jnp.log(norm)
        out = jnp.transpose(jnp.concatenate(both, axis=0))
        o_out[rows, :] = out
        low[rows, :] = out.astype(BF16)
        for mask in range(1, 8):

            @pl.when(t == 7 - mask)
            def _(mask=mask):
                swaps[mask].start()

        @pl.when(t == 1)
        def _():
            hops.wait(2)
            hops.start(3)

    w.sent.extend(swaps.values())
    att[:, rows_of(own, head_width)] = low[rows_of(own, toks), :]
    hops.wait(3)
    later = kept[:1] + kept[2:]
    soon = kept[1:2]
    for full, group in ((out_full, soon), (up_full, later)):
        for k in others:
            rows = rows_of(2 * k + core, piece)
            group.append((None, w.send(full.at[rows], full.at[rows], mate)))

    def settle(group):
        for local, remote in group:
            if local is not None:
                local.wait()
            remote.wait_recv()

    settle(soon)
    for copy in swaps.values():
        copy.wait_recv()

    @pl.loop(0, width // tile)
    def _(n):
        cols = rows_of(n, tile)
        h1[:, cols] = nn(att[...], out_full[:, cols]) + proj_bias[2:3, cols] + x[:, cols].astype(F32)

    step = 32
    acc[...] = jnp.zeros_like(acc)

    def first_rows(t):
        rows = rows_of(t, step)
        v = h1[rows, :]
        center = v - jnp.mean(v, axis=1, keepdims=True)
        inv = lax.rsqrt(jnp.mean(center * center, axis=1, keepdims=True) + 1e-05)
        z = center * inv
        z1[rows, :] = z
        r1[rows, :] = jnp.broadcast_to(inv, (step, 128))
        fl[chip, rows, :] = (z * gain[0:1, :] + shift[0:1, :]).astype(BF16)

    spread = Spread(w, fl, half)
    pl.loop(0, half // step)(first_rows)
    spread.first_half()
    pl.loop(half // step, toks // step)(first_rows)
    spread.second_half()

    def forward(k):
        @pl.loop(0, ff // tile)
        def _(n):
            cols = rows_of(n, tile)
            hidden = nn(fl[k], up_full[:, cols]) + hidden_bias[:, pl.ds(pl.multiple_of(chip * ff + n * tile, tile), tile)]
            cdf = 0.5 * (1.0 + lax.erf(hidden * (2.0**-0.5)))
            act[k, :, cols] = (hidden * cdf).astype(BF16)
            slope[k, :, cols] = (cdf + hidden * (jnp.exp(-0.5 * hidden * hidden) * ((2.0 * math.pi) ** -0.5))).astype(BF16)

        @pl.loop(0, width // tile)
        def _(n):
            cols = rows_of(n, tile)
            part[k, :, cols] = nn(act[k], down_full[:, cols]).astype(BF16)

    settle(later)
    forward(chip)
    gather = Gather(w, part, side, last, half)
    spread.relay()
    spread.wait_sides()
    forward(cx)
    gather.send_x()
    forward(cy)
    gather.send_y()
    spread.wait_diagonal()
    forward(cd)
    gather.send_diagonal()

    gather.relay()

    def second_rows(which, t):
        rows = pl.ds(pl.multiple_of(which * half + t * step, step), step)
        v = z1[rows, :] * gain[0:1, :] + shift[0:1, :] + gather.total(which, t * step, step) + proj_bias[3:4, :]
        center = v - jnp.mean(v, axis=1, keepdims=True)
        inv = lax.rsqrt(jnp.mean(center * center, axis=1, keepdims=True) + 1e-05)
        z = center * inv
        output[rows, :] = (z * gain[1:2, :] + shift[1:2, :]).astype(BF16)
        c = cot[rows, :].astype(F32)
        e = c * gain[1:2, :]
        grad = inv * (e - jnp.mean(e, axis=1, keepdims=True) - z * jnp.mean(e * z, axis=1, keepdims=True))
        h1[rows, :] = grad
        low = grad.astype(BF16)
        sl[chip, rows, :] = low
        acc[0] += fold_rows(c * z)
        acc[1] += fold_rows(c)
        acc[2] += fold_rows(low.astype(F32))

    spread2 = Spread(w, sl, half)
    gather.wait_first()
    pl.loop(0, half // step)(functools.partial(second_rows, 0))
    spread2.first_half()
    gather.wait_second()
    pl.loop(0, half // step)(functools.partial(second_rows, 1))
    spread2.second_half()

    def backward(k):
        @pl.loop(0, ff // tile)
        def _(n):
            cols = rows_of(n, tile)
            grad = nt(sl[k], down_full[cols, :]) * slope[k, :, cols].astype(F32)
            low = grad.astype(BF16)
            pre[k, :, cols] = low
            acc[3, :, cols] += fold_rows(low.astype(F32))

        @pl.loop(0, width // tile)
        def _(n):
            cols = rows_of(n, tile)
            part[k, :, cols] = nt(pre[k], up_full[cols, :]).astype(BF16)

    gather.drain()
    backward(chip)
    gather2 = Gather(w, part, side, last, half)
    spread2.relay()
    spread2.wait_sides()
    backward(cx)
    gather2.send_x()
    backward(cy)
    gather2.send_y()
    spread2.wait_diagonal()
    backward(cd)
    gather2.send_diagonal()

    def down_rows(which, n):
        cols = pl.ds(pl.multiple_of(which * (ff // 2) + n * tile, tile), tile)
        lhs = act[:, :, cols].reshape(4 * toks, tile)
        return tn(lhs, sl[...].reshape(4 * toks, width))

    @pl.loop(0, ff // 2 // tile)
    def _(n):
        d_send[rows_of(n, tile), :] = down_rows(1 - core, n).astype(BF16)

    d_copy = w.send(d_send, d_recv, mate)
    d_copy.wait_recv()

    @pl.loop(0, ff // 2 // tile)
    def _(n):
        rows = rows_of(n, tile)
        down_grad[rows, :] = (down_rows(core, n) + d_recv[rows, :].astype(F32)).astype(BF16)

    down_line = Line(w, down_grad, down_sum, d_far, 8)
    down_line.start()
    gather2.relay()

    def up_rows(which, k):
        cols = pl.ds(pl.multiple_of((2 * k + which) * piece, piece), piece)
        lhs = fl[:, :, cols].reshape(4 * toks, piece)
        return tn(lhs, pre[...].reshape(4 * toks, ff))

    @pl.loop(0, 4)
    def _(k):
        u_send[k] = up_rows(1 - core, k).astype(BF16)

    u_copy = w.send(u_send, u_recv, mate)
    down_line.collect((0,))

    def branch_rows(which, t):
        rows = pl.ds(pl.multiple_of(which * half + t * step, step), step)
        grad = h1[rows, :] + gather2.total(which, t * step, step)
        z = z1[rows, :]
        e = grad * gain[0:1, :]
        out = r1[rows, 0:1] * (e - jnp.mean(e, axis=1, keepdims=True) - z * jnp.mean(e * z, axis=1, keepdims=True))
        branch_grad[rows, :] = out
        low = out.astype(BF16)
        branch_low[rows, :] = low
        acc[4] += fold_rows(grad * z)
        acc[5] += fold_rows(grad)
        acc[6] += fold_rows(low.astype(F32))

    gather2.wait_first()
    pl.loop(0, half // step)(functools.partial(branch_rows, 0))
    down_line.collect((1,))
    gather2.wait_second()
    pl.loop(0, half // step)(functools.partial(branch_rows, 1))

    @pl.loop(0, width // tile)
    def _(n):
        cols = rows_of(n, tile)
        agl[:, cols] = nt(branch_low[...], out_full[cols, :]).astype(BF16)

    backs = []
    for m in (6, 2, 4, 1, 3, 5, 7):
        peer = lax.bitwise_xor(own, m)
        backs.append(w.send(agl.at[:, rows_of(peer, head_width)], grad_heads.at[rows_of(own, toks)], peer))
    grad_heads[rows_of(own, toks), :] = agl[:, rows_of(own, head_width)]

    down_line.collect((2,))
    down_line.total((0,))
    u_copy.wait_recv()
    spread_up, spread_out = [], []

    def up_piece(m):
        k = lax.bitwise_xor(chip, m)
        return (up_rows(core, k) + u_recv[k].astype(F32)).astype(BF16)

    y_own[0:piece, :] = up_piece(0)
    y_own[piece : 2 * piece, :] = up_piece(3)
    up_line = Line(w, y_own.at[pl.ds(0, 2 * piece)], upout_sum.at[pl.ds(0, 2 * piece)], y_far.at[pl.ds(0, 2 * piece)], 4)
    up_line.start()
    for i, m in ((1, 1), (2, 2)):
        sends[i, 0] = up_piece(m)
        spread_up.append(w.send(sends.at[i, 0], got.at[i, 0], lax.bitwise_xor(own, 2 * m)))
    down_line.collect((3,))
    down_line.total((1,))

    def out_rows(which, k):
        cols = pl.ds(pl.multiple_of((2 * k + which) * piece, piece), piece)
        return tn(att[:, cols], branch_low[...])

    @pl.loop(0, 4)
    def _(k):
        o_send[k] = out_rows(1 - core, k).astype(BF16)

    o_copy = w.send(o_send, o_recv, mate)
    o_copy.wait_recv()
    for i, m in enumerate((3, 1, 2, 0)):
        k = lax.bitwise_xor(chip, m)
        sends[i, 1] = (out_rows(core, k) + o_recv[k].astype(F32)).astype(BF16)
        if m:
            spread_out.append(w.send(sends.at[i, 1], got.at[i, 1], lax.bitwise_xor(own, 2 * m)))
    down_line.collect((4, 5))
    down_line.total((2, 3))

    vec[...] = jnp.zeros_like(vec)
    for row, slot in ((2, 6), (3, 2), (4, 4), (5, 0), (6, 5), (7, 1)):
        vec[row : row + 1, :] = jnp.sum(acc[slot], axis=0, keepdims=True)
    hidden_sum = jnp.sum(acc[3], axis=0, keepdims=True)
    for k in range(4):
        vec[8 + k : 9 + k, :] = jnp.where(chip == k, hidden_sum, jnp.zeros_like(hidden_sum))
    for copy in backs:
        copy.wait_recv()

    got_up, got_out = spread_up, spread_out
    side_line = Line(w, y_own.at[pl.ds(2 * piece, 2 * piece)], upout_sum.at[pl.ds(2 * piece, 2 * piece)], y_far.at[pl.ds(2 * piece, 2 * piece)], 4)
    out_line = Line(w, y_own.at[pl.ds(4 * piece, piece)], upout_sum.at[pl.ds(4 * piece, piece)], y_far.at[pl.ds(4 * piece, piece)], 2)
    lines = [Line(w, l_own.at[p], qkv_sum.at[p], l_far.at[p], 2) for p in range(3)]

    def side_start():
        for copy in got_up:
            copy.wait_recv()
        for row, i in ((2, 1), (3, 2)):
            y_own[row * piece : (row + 1) * piece, :] = got[i, 0]
        side_line.start()

    def out_start():
        for copy in got_out:
            copy.wait_recv()
        y_own[4 * piece :, :] = (sends[3, 1].astype(F32) + got[0, 1].astype(F32) + got[1, 1].astype(F32) + got[2, 1].astype(F32)).astype(BF16)
        out_line.start()

    hooks = {
        0: lambda: (down_line.collect((6, 7)), down_line.total((4, 5))),
        1: lambda: down_line.total((6,)),
        2: lambda: up_line.collect((0,)),
        3: lambda: (side_start(), down_line.total((7,))),
        4: lambda: (up_line.collect((1,)), up_line.total((0,))),
        6: lambda: (up_line.collect((2,)), up_line.total((1,))),
        7: lambda: (up_line.collect((3,)), up_line.total((2,))),
    }

    grads = stage

    def head_cols_of(p, core_index):
        return pl.ds(pl.multiple_of((2 * p + core_index) * head_width, head_width), head_width)

    length, head_cols = q_out.shape
    q, k, v, g, o = q_out, k_out, v_out, grad_heads, o_out
    dk_acc = o_out

    @pl.loop(0, blocks)
    def _(i):
        rows = rows_of(i, BQ)
        prod = jnp.transpose(g[rows, :].astype(F32) * o[rows, :])
        corr[0:1, rows] = jnp.sum(prod[:headd], axis=0, keepdims=True)
        corr[1:2, rows] = jnp.sum(prod[headd:], axis=0, keepdims=True)
        t = jnp.transpose(k[rows, :])
        for h in range(2):
            vt[h, 0:headd, rows] = t[h * headd : (h + 1) * headd]
        dk_acc[rows, :] = jnp.zeros((BQ, head_cols), F32)
        dv_acc[rows, :] = jnp.zeros((BQ, head_cols), F32)

    @pl.loop(0, blocks)
    def _(i):
        rows = rows_of(i, BQ)
        qb = q[rows, :] * jnp.bfloat16(scale)
        gb = g[rows, :]
        zero = jnp.zeros_like(qb)
        qs = (jnp.where(first, qb, zero), jnp.where(first, zero, qb))
        gs = (jnp.where(first, gb, zero), jnp.where(first, zero, gb))
        qz = jnp.concatenate(qs, axis=0)
        gz = jnp.concatenate(gs, axis=0)
        seg_q = seg[:, rows].astype(F32)
        dq = [jnp.zeros((headd, BQ), F32)] * 2
        for j in range(length // BK):
            cols = pl.ds(j * BK, BK)
            kb = k[cols, :]
            vb = v[cols, :]
            same = wide(seg_c[cols, :], BQ) == seg_q
            ps, ds = [], []
            for h in range(2):
                s = jnp.where(same, nt(kb, qs[h]), NEGATIVE)
                p = jnp.exp(s - lse[h : h + 1, rows])
                dp = nt(vb, gs[h])
                dscore = (p * (dp - corr[h : h + 1, rows])).astype(BF16)
                ps.append(p.astype(BF16))
                ds.append(dscore)
                dq[h] = dq[h] + nn(vt[h, 0:headd, cols], dscore)
            dv_acc[cols, :] += nn(jnp.concatenate(ps, axis=1), gz)
            dk_acc[cols, :] += nn(jnp.concatenate(ds, axis=1), qz)
        dqt[0:headd, :] = dq[0]
        dqt[headd:, :] = dq[1]
        act[i // 2, :, head_cols_of(0, lax.rem(i, 2))] = (jnp.transpose(dqt[...]) * scale).astype(BF16)
        for at, hook in hooks.items():

            @pl.when(i == at)
            def _(hook=hook):
                hook()

    @pl.loop(0, blocks)
    def _(i):
        rows = rows_of(i, BQ)
        act[i // 2, :, head_cols_of(1, lax.rem(i, 2))] = dk_acc[rows, :].astype(BF16)
        act[i // 2, :, head_cols_of(2, lax.rem(i, 2))] = dv_acc[rows, :].astype(BF16)

    gather2.drain()
    swaps = []
    for p in range(3):
        cols = pl.ds(pl.multiple_of(p * share + core * head_width, head_width), head_width)
        swaps.append(w.send(act.at[:, :, head_cols_of(p, 1 - core)], grads.at[:, :, cols], mate))
        grads[:, :, cols] = act[:, :, head_cols_of(p, core)]
    v_sum[...] = vec[...]
    for row, p in ((0, 0), (1, 2)):
        total = jnp.sum(act[:, :, 2 * p * head_width : 2 * (p + 1) * head_width].reshape(4 * toks, 2 * head_width).astype(F32), axis=0, keepdims=True)
        total = total[:, 0:head_width] + total[:, head_width:]
        v_sum[row : row + 1, rows_of(own, head_width)] = total
    rounds = [(None, mate), (None, lax.bitwise_xor(own, 2)), (None, lax.bitwise_xor(own, 4)), (lax.bitwise_xor(rep, 1), own), (lax.bitwise_xor(rep, 2), own)]
    flying = []

    def vec_start(i):
        copy = w.remote(v_sum.at[...] if i == 0 else v_recv.at[4 + i], v_recv.at[i], rounds[i][1], rounds[i][0])
        copy.start()
        w.sent.append(copy)
        flying.append(copy)

    def vec_step(i):
        flying[i].wait_recv()
        base = v_sum[...] if i == 0 else v_recv[4 + i]
        if i < 4:
            v_recv[5 + i] = base + v_recv[i]
            vec_start(i + 1)
        else:
            vec_sum[...] = base + v_recv[i]

    vec_start(0)

    def qkv_rows(which, kk, p):
        cols = pl.ds(pl.multiple_of((2 * kk + which) * piece, piece), piece)
        return tn(xs[:, :, cols].reshape(4 * toks, piece), grads[:, :, p * share : (p + 1) * share].reshape(4 * toks, share))

    def theirs(p):
        @pl.loop(0, 4)
        def _(kk):
            q_send[p, kk] = qkv_rows(1 - core, kk, p).astype(BF16)

        return w.send(q_send.at[p], q_recv.at[p], mate)

    moved = []

    def pieces(p, copy):
        copy.wait_recv()

        @pl.loop(0, 4)
        def _(kk):
            q_piece[p, kk] = (qkv_rows(core, kk, p) + q_recv[p, kk].astype(F32)).astype(BF16)

        cols = rows_of(chip, share)
        moved.append([w.send(q_piece.at[p, lax.bitwise_xor(chip, m // 2)], l_own.at[p, :, cols], lax.bitwise_xor(own, m)) for m in (6, 2, 4)])
        l_own[p, :, cols] = q_piece[p, chip]

    def line_start(p):
        for copy in moved[p]:
            copy.wait_recv()
        lines[p].start()

    swaps[0].wait_recv()
    copies = [theirs(0)]
    up_line.total((3,))
    side_line.collect((0,))
    swaps[1].wait_recv()
    copies.append(theirs(1))
    pieces(0, copies[0])
    out_start()
    swaps[2].wait_recv()
    copies.append(theirs(2))
    pieces(1, copies[1])
    side_line.collect((1,))
    side_line.total((0,))
    up_line.arrive(range(4))
    far_copy = w.send(upout_sum.at[pl.ds(piece, piece)], got.at[0, 0], lax.bitwise_xor(own, 6))
    pieces(2, copies[2])
    side_line.collect((2,))
    side_line.total((1,))
    vec_step(0)

    def partial(kk):
        @pl.loop(0, width // tile)
        def _(n):
            cols = rows_of(n, tile)
            part[kk, :, cols] = nt(grads[kk], w_full[cols, :]).astype(BF16)

    gather = Gather(w, part, side, last, half)
    partial(gather.cd)
    side_line.collect((3,))
    side_line.total((2,))
    line_start(0)
    partial(gather.cx)
    line_start(1)
    partial(gather.cy)
    line_start(2)
    gather.send_diagonal()
    gather.send_x()
    gather.send_y()
    out_line.collect((0,))
    side_line.total((3,))
    partial(chip)
    out_line.collect((1,))
    out_line.total((0,))
    vec_step(1)
    step = 32

    def final_rows(which, t):
        rows = pl.ds(pl.multiple_of(which * half + t * step, step), step)
        input_grad[rows, :] = (branch_grad[rows, :] + gather.total(which, t * step, step)).astype(BF16)

    order = [(p, i) for p in range(3) for i in range(2)]

    def hop(at):
        if at < len(order):
            lines[order[at][0]].collect((order[at][1],))
        if at >= 1:
            lines[order[at - 1][0]].total((order[at - 1][1],))

    hop(0)
    out_line.total((1,))
    hop(1)
    gather.relay()
    vec_step(2)
    for at in range(2, 4):
        hop(at)
    vec_step(3)
    gather.wait_first()
    pl.loop(0, half // step)(functools.partial(final_rows, 0))
    hop(4)
    vec_step(4)
    gather.wait_second()
    pl.loop(0, half // step)(functools.partial(final_rows, 1))
    for at in range(5, len(order) + 1):
        hop(at)
    down_line.arrive(range(8))
    spill = [w.local(down_sum, h_down)]
    side_line.arrive(range(4))
    out_line.arrive(range(2))
    far_copy.wait_recv()
    for to, src_ref in ((0, upout_sum.at[pl.ds(0, piece)]), (1, got.at[0, 0])):
        spill.append(w.local(src_ref, h_upout.at[pl.ds(to * piece, piece)]))
    spill.append(w.local(upout_sum.at[pl.ds(2 * piece, 3 * piece)], h_upout.at[pl.ds(2 * piece, 3 * piece)]))
    for p in range(3):
        lines[p].arrive(range(2))
        spill.append(w.local(qkv_sum.at[p], h_qkv.at[p]))
    spill += [w.local(s, d) for s, d in ((output, h_output), (input_grad, h_input_grad), (vec_sum, h_vec))]
    for line in [down_line, up_line, side_line, out_line] + lines:
        line.finish()
    for copy in spill:
        copy.wait()
    qkv_hops.finish()
    hops.finish()
    w.finish()


def layer(scale, seg, x, cot, qkv_w, up_w, out_w, down_w, proj_bias, hidden_bias, gain, shift):
    toks, width = x.shape
    piece = up_w.shape[0]
    ff = 2 * down_w.shape[0]
    half = toks // 2
    share = width // 4
    head_width = width // 8
    length = 8 * toks
    shape = jax.ShapeDtypeStruct
    vm = pltpu.VMEM
    five = (5 * piece, width)
    small = vm((3, 4, piece, share), BF16)
    three = (3, piece, width)
    rows4 = vm((4, toks, width), BF16)
    block = vm((toks, width), BF16)
    block32 = vm((toks, width), F32)
    pieces = vm((4, piece, width), BF16)
    halfff = vm((ff // 2, width), BF16)
    heads = vm((length, head_width), BF16)
    heads32 = vm((length, head_width), F32)
    return pl.pallas_call(
        functools.partial(layer_body, scale),
        name="layer",
        out_shape=(
            shape((toks, width), BF16), shape((toks, width), BF16), shape(three, BF16), shape(five, BF16), shape((ff // 2, width), BF16), shape((16, width), F32),
        ),
        in_specs=[VM, VM, VM, VM, HBM, HBM, HBM] + [VM] * 4,
        out_specs=(HBM,) * 6,
        scratch_shapes=[
            heads, heads, heads, heads32, vm((8, length), F32), rows4, vm((8 * piece, 3 * share), BF16), block, block32, heads, vm((16, width), F32), halfff,
            vm((4, 2, piece, width), BF16),
            vm((4, toks, 3 * share), BF16), vm((2, head_width // 2 + 16, length), BF16), heads32, heads, block,
            vm((width, width), BF16), vm((width, ff), BF16), vm((ff, width), BF16), block32, block32, vm((toks, 128), F32),
            rows4, vm((4, toks, ff), BF16), vm((4, toks, ff), BF16), rows4, vm((4, half, width), BF16), vm((2, half, width), BF16), rows4, vm((4, toks, ff), BF16),
            block, block, vm((8, 8, width), F32), halfff, halfff, halfff, halfff, pieces, pieces, pieces, pieces,
            vm((8, length), F32), heads32, vm((head_width, BQ), F32), small, small, small, vm(three, BF16), vm(three, BF16), vm((3, 2, piece, width), BF16),
            vm(five, BF16), vm(five, BF16), vm(five, BF16), vm(three, BF16), block, vm((16, width), F32), vm((9, 16, width), F32), vm((16, width), F32),
            pltpu.SemaphoreType.DMA((320,)), pltpu.SemaphoreType.DMA((320,)), pltpu.SemaphoreType.DMA((40,)),
        ],
        compiler_params=pltpu.CompilerParams(collective_id=1, has_side_effects=True, vmem_limit_bytes=63 << 20),
    )(seg, x, cot, qkv_w, up_w, out_w, down_w, proj_bias, hidden_bias, gain, shift)


def emit_body(
    grad_scale, who, h_low, h_grad, h_qkv, h_upout, h_down, h_vec,
    output, input_grad, h_qkv_total, h_out_total, h_up_total, h_down_total, bias_total, hidden_total, gain_total, shift_total,
    qkv_sum, upout_sum, down_sum, vec_sum, qkv_total, out_total, up_total, down_total, sems,
):
    width = h_low.shape[1]
    piece = qkv_sum.shape[1]
    pairs = ((h_down, down_sum), (h_upout, upout_sum), (h_qkv, qkv_sum), (h_vec, vec_sum), (h_low, output), (h_grad, input_grad))
    copies = [pltpu.make_async_copy(src, dst, sems.at[i]) for i, (src, dst) in enumerate(pairs)]
    for copy in copies:
        copy.start()
    chip = who[0]
    sent = []

    def leave(src, dst):
        copy = pltpu.make_async_copy(src, dst, sems.at[6 + len(sent)])
        copy.start()
        sent.append(copy)

    copies[0].wait()
    down_total[...] = down_sum[...].astype(F32) * grad_scale
    leave(down_total, h_down_total)
    copies[1].wait()
    for at, m in enumerate((0, 3, 1, 2)):
        up_total[:, rows_of(lax.bitwise_xor(chip, m), width)] = upout_sum[at * piece : (at + 1) * piece, :].astype(F32) * grad_scale
    leave(up_total, h_up_total)
    out_total[...] = upout_sum[4 * piece :, :].astype(F32) * grad_scale
    leave(out_total, h_out_total)
    copies[2].wait()
    for p in range(3):
        qkv_total[:, p * width : (p + 1) * width] = qkv_sum[p].astype(F32) * grad_scale
    leave(qkv_total, h_qkv_total)
    copies[3].wait()
    bias_total[...] = vec_sum[0:4] * grad_scale
    gain_total[...] = vec_sum[4:6] * grad_scale
    shift_total[...] = vec_sum[6:8] * grad_scale
    for kk in range(4):
        hidden_total[:, kk * width : (kk + 1) * width] = vec_sum[8 + kk : 9 + kk] * grad_scale
    for copy in copies[4:] + sent:
        copy.wait()


def emit(grad_scale, who, low, grad, qkv_sum, upout_sum, down_sum, vec_sum):
    toks, width = low.shape
    piece = qkv_sum.shape[1]
    shape = jax.ShapeDtypeStruct
    return pl.pallas_call(
        functools.partial(emit_body, grad_scale),
        name="emit",
        out_shape=(
            shape((toks, width), BF16), shape((toks, width), BF16), shape((piece, 3 * width), F32), shape((piece, width), F32), shape((piece, 4 * width), F32),
            shape(down_sum.shape, F32), shape((4, width), F32), shape((1, 4 * width), F32), shape((2, width), F32), shape((2, width), F32),
        ),
        in_specs=[SM] + [HBM] * 6,
        out_specs=(VM, VM) + (HBM,) * 4 + (VM,) * 4,
        scratch_shapes=[
            pltpu.VMEM(qkv_sum.shape, BF16), pltpu.VMEM(upout_sum.shape, BF16), pltpu.VMEM(down_sum.shape, BF16), pltpu.VMEM(vec_sum.shape, F32),
            pltpu.VMEM((piece, 3 * width), F32), pltpu.VMEM((piece, width), F32), pltpu.VMEM((piece, 4 * width), F32), pltpu.VMEM(down_sum.shape, F32),
            pltpu.SemaphoreType.DMA((10,)),
        ],
        compiler_params=pltpu.CompilerParams(vmem_limit_bytes=62 << 20),
    )(who, low, grad, qkv_sum, upout_sum, down_sum, vec_sum)


def local_tensor(tokens, segment_ids, qkv_weight, out_weight, up_weight, down_weight, proj_bias, hidden_bias, norm_gain, norm_shift, cotangent):
    inputs = tokens[0]
    toks, width = inputs.shape
    scale = (width // HEADS) ** (-0.5)
    grad_scale = (toks * lax.axis_size("fsdp") * lax.axis_size("rep")) ** (-0.5)
    low, grad, qkv_sum, upout_sum, down_sum, vec_sum = layer(
        scale, segment_ids, inputs, cotangent[0], qkv_weight, up_weight, out_weight, down_weight, proj_bias, hidden_bias[None], norm_gain, norm_shift
    )
    output, input_grad, qkv_total, out_total, up_total, down_total, bias_total, hidden_total, gain_total, shift_total = emit(
        grad_scale, (lax.axis_index("fsdp") // 2).reshape(1), low, grad, qkv_sum, upout_sum, down_sum, vec_sum
    )
    return (
        output[None],
        input_grad[None],
        qkv_total,
        out_total,
        up_total,
        down_total,
        bias_total,
        hidden_total.reshape(4 * width),
        gain_total,
        shift_total,
    )


def normalize(hidden, gain, shift):
    center = hidden - jnp.mean(hidden, axis=-1, keepdims=True)
    spread = jnp.mean(center * center, axis=-1, keepdims=True)
    return center * lax.rsqrt(spread + 1e-05) * gain + shift


def exact_gelu(value):
    return jax.nn.gelu(value, approximate=False)


def gather_attention(qkv_weight, out_weight):
    return (
        lax.all_gather(qkv_weight, "fsdp", axis=0, tiled=True),
        lax.all_gather(out_weight, "fsdp", axis=0, tiled=True),
    )


def gather_feedforward(up_weight, down_weight):
    return (
        lax.all_gather(up_weight, "fsdp", axis=0, tiled=True),
        lax.all_gather(down_weight, "fsdp", axis=0, tiled=True),
    )


def block_plan(row_count):
    block_rows = math.gcd(row_count, 1024)
    return (block_rows, row_count // block_rows)


def split_heads(matrix):
    return matrix.reshape(matrix.shape[0], HEADS, matrix.shape[1] // HEADS)


def join_heads(stacked):
    return jnp.transpose(stacked, (1, 0, 2)).reshape(
        stacked.shape[1], stacked.shape[0] * stacked.shape[2]
    )


def local_gather(
    tokens,
    segment_ids,
    qkv_weight,
    out_weight,
    up_weight,
    down_weight,
    proj_bias,
    hidden_bias,
    norm_gain,
    norm_shift,
    cotangent,
):
    inputs = tokens[0]
    tok_count, model_width = inputs.shape
    head_dim = model_width // HEADS
    score_scale = head_dim ** (-0.5)
    doc_ids = segment_ids[0]
    own_index = lax.axis_index("fsdp")
    own_docs = lax.dynamic_slice_in_dim(doc_ids, own_index * tok_count, tok_count)
    qkv_full, out_full = gather_attention(qkv_weight, out_weight)
    projected = jnp.dot(inputs, qkv_full, preferred_element_type=jnp.float32)
    queries = (projected[:, :model_width] + proj_bias[0]).astype(jnp.bfloat16)
    key_rows = projected[:, model_width : 2 * model_width].astype(jnp.bfloat16)
    value_rows = (projected[:, 2 * model_width :] + proj_bias[1]).astype(jnp.bfloat16)
    query_heads = split_heads(queries)
    key_own = split_heads(key_rows)
    value_own = split_heads(value_rows)
    initial = (
        jnp.zeros((HEADS, tok_count, head_dim), jnp.float32),
        jnp.full((HEADS, tok_count), NEGATIVE, jnp.float32),
        jnp.zeros((HEADS, tok_count), jnp.float32),
    )
    key_piece = lax.all_gather(key_rows, "fsdp", axis=0, tiled=True)
    value_piece = lax.all_gather(value_rows, "fsdp", axis=0, tiled=True)
    block_rows, blocks = block_plan(key_piece.shape[0])

    def forward_advance(block_index, running_state):
        weighted, running, denominator = running_state
        offset = block_index * block_rows
        key_block = split_heads(lax.dynamic_slice_in_dim(key_piece, offset, block_rows))
        value_block = split_heads(lax.dynamic_slice_in_dim(value_piece, offset, block_rows))
        block_docs = lax.dynamic_slice_in_dim(doc_ids, offset, block_rows)
        scores = (
            jnp.einsum("qhd,khd->hqk", query_heads, key_block, preferred_element_type=jnp.float32)
            * score_scale
        )
        same_doc = (own_docs[:, None] == block_docs[None, :])[None]
        highest = jnp.maximum(running, jnp.max(jnp.where(same_doc, scores, NEGATIVE), axis=2))
        factor = jnp.exp(running - highest)
        weights = jnp.where(same_doc, jnp.exp(scores - highest[:, :, None]), 0.0)
        denominator = denominator * factor + jnp.sum(weights, axis=2)
        weighted = weighted * factor[:, :, None] + jnp.einsum(
            "hqk,khd->hqd",
            weights.astype(jnp.bfloat16),
            value_block,
            preferred_element_type=jnp.float32,
        )
        return (weighted, highest, denominator)

    weighted, running, denominator = lax.fori_loop(0, blocks, forward_advance, initial)
    attended_heads = weighted / denominator[:, :, None]
    log_total = running + jnp.log(denominator)
    attended_low = join_heads(attended_heads).astype(jnp.bfloat16)
    branch = jnp.dot(attended_low, out_full, preferred_element_type=jnp.float32) + proj_bias[2]
    first_norm, norm_one_back = jax.vjp(
        normalize, inputs.astype(jnp.float32) + branch, norm_gain[0], norm_shift[0]
    )
    first_low = first_norm.astype(jnp.bfloat16)
    up_full, down_full = gather_feedforward(up_weight, down_weight)
    hidden_pre = jnp.dot(first_low, up_full, preferred_element_type=jnp.float32) + hidden_bias
    activated, gelu_back = jax.vjp(exact_gelu, hidden_pre)
    activated_low = activated.astype(jnp.bfloat16)
    second = jnp.dot(activated_low, down_full, preferred_element_type=jnp.float32) + proj_bias[3]
    output, norm_two_back = jax.vjp(normalize, first_norm + second, norm_gain[1], norm_shift[1])
    up_back, down_back = gather_feedforward(up_weight, down_weight)
    qkv_back, out_back = gather_attention(qkv_weight, out_weight)
    grad_second, gain_two, shift_two = norm_two_back(cotangent[0].astype(jnp.float32))
    second_low = grad_second.astype(jnp.bfloat16)
    down_term = jnp.einsum(
        "tf,td->fd", activated_low, second_low, preferred_element_type=jnp.float32
    )
    activated_grad = jnp.einsum(
        "td,fd->tf", second_low, down_back, preferred_element_type=jnp.float32
    )
    (pre_grad,) = gelu_back(activated_grad)
    pre_low = pre_grad.astype(jnp.bfloat16)
    up_term = jnp.einsum("td,tf->df", first_low, pre_low, preferred_element_type=jnp.float32)
    first_grad = grad_second + jnp.einsum(
        "tf,df->td", pre_low, up_back, preferred_element_type=jnp.float32
    )
    branch_grad, gain_one, shift_one = norm_one_back(first_grad)
    branch_low = branch_grad.astype(jnp.bfloat16)
    out_term = jnp.einsum("te,td->ed", attended_low, branch_low, preferred_element_type=jnp.float32)
    attended_grad = jnp.einsum(
        "td,ed->te", branch_low, out_back, preferred_element_type=jnp.float32
    ).astype(jnp.bfloat16)
    grad_heads = split_heads(attended_grad)
    correction = jnp.einsum("qhd,hqd->hq", grad_heads.astype(jnp.float32), attended_heads)
    lse_all, correction_all = (
        lax.all_gather(log_total, "fsdp", axis=1, tiled=True),
        lax.all_gather(correction, "fsdp", axis=1, tiled=True),
    )
    query_key_piece = lax.all_gather(key_rows, "fsdp", axis=0, tiled=True)
    query_value_piece = lax.all_gather(value_rows, "fsdp", axis=0, tiled=True)
    query_block_rows, blocks = block_plan(query_key_piece.shape[0])

    def query_advance(block_index, query_state):
        offset = block_index * query_block_rows
        key_block = split_heads(lax.dynamic_slice_in_dim(query_key_piece, offset, query_block_rows))
        value_block = split_heads(
            lax.dynamic_slice_in_dim(query_value_piece, offset, query_block_rows)
        )
        block_docs = lax.dynamic_slice_in_dim(doc_ids, offset, query_block_rows)
        scores = (
            jnp.einsum("qhd,khd->hqk", query_heads, key_block, preferred_element_type=jnp.float32)
            * score_scale
        )
        same_doc = (own_docs[:, None] == block_docs[None, :])[None]
        probabilities = jnp.where(same_doc, jnp.exp(scores - log_total[:, :, None]), 0.0)
        prob_grad = jnp.einsum(
            "qhd,khd->hqk", grad_heads, value_block, preferred_element_type=jnp.float32
        )
        score_grad = (probabilities * (prob_grad - correction[:, :, None])).astype(jnp.bfloat16)
        return query_state + jnp.einsum(
            "hqk,khd->hqd", score_grad, key_block, preferred_element_type=jnp.float32
        )

    query_acc = lax.fori_loop(
        0, blocks, query_advance, jnp.zeros((HEADS, tok_count, head_dim), jnp.float32)
    )
    query_grad = (join_heads(query_acc) * score_scale).astype(jnp.bfloat16)
    empty_heads = jnp.zeros((HEADS, tok_count, head_dim), jnp.float32)
    query_piece = lax.all_gather(queries, "fsdp", axis=0, tiled=True)
    grad_piece = lax.all_gather(attended_grad, "fsdp", axis=0, tiled=True)
    key_block_rows, blocks = block_plan(query_piece.shape[0])

    def key_advance(block_index, key_state):
        key_acc, value_acc = key_state
        offset = block_index * key_block_rows
        query_block = split_heads(lax.dynamic_slice_in_dim(query_piece, offset, key_block_rows))
        grad_block = split_heads(lax.dynamic_slice_in_dim(grad_piece, offset, key_block_rows))
        block_docs = lax.dynamic_slice_in_dim(doc_ids, offset, key_block_rows)
        lse_block = lax.dynamic_slice_in_dim(lse_all, offset, key_block_rows, axis=1)
        corr_block = lax.dynamic_slice_in_dim(correction_all, offset, key_block_rows, axis=1)
        scores = (
            jnp.einsum("qhd,khd->hqk", query_block, key_own, preferred_element_type=jnp.float32)
            * score_scale
        )
        same_doc = (block_docs[:, None] == own_docs[None, :])[None]
        probabilities = jnp.where(same_doc, jnp.exp(scores - lse_block[:, :, None]), 0.0)
        value_acc = value_acc + jnp.einsum(
            "hqk,qhd->hkd",
            probabilities.astype(jnp.bfloat16),
            grad_block,
            preferred_element_type=jnp.float32,
        )
        prob_grad = jnp.einsum(
            "qhd,khd->hqk", grad_block, value_own, preferred_element_type=jnp.float32
        )
        score_grad = (probabilities * (prob_grad - corr_block[:, :, None])).astype(jnp.bfloat16)
        key_acc = key_acc + jnp.einsum(
            "hqk,qhd->hkd", score_grad, query_block, preferred_element_type=jnp.float32
        )
        return (key_acc, value_acc)

    key_acc, value_acc = lax.fori_loop(0, blocks, key_advance, (empty_heads, empty_heads))
    key_grad = (join_heads(key_acc) * score_scale).astype(jnp.bfloat16)
    value_grad = join_heads(value_acc).astype(jnp.bfloat16)
    qkv_grad_low = jnp.concatenate([query_grad, key_grad, value_grad], axis=1)
    qkv_term = jnp.einsum("td,te->de", inputs, qkv_grad_low, preferred_element_type=jnp.float32)
    input_grad = branch_grad + jnp.einsum(
        "te,de->td", qkv_grad_low, qkv_back, preferred_element_type=jnp.float32
    )
    bias_term = jnp.stack(
        [
            jnp.sum(query_grad.astype(jnp.float32), axis=0),
            jnp.sum(value_grad.astype(jnp.float32), axis=0),
            jnp.sum(branch_low.astype(jnp.float32), axis=0),
            jnp.sum(second_low.astype(jnp.float32), axis=0),
        ]
    )
    hidden_term = jnp.sum(pre_low.astype(jnp.float32), axis=0)
    gain_term = jnp.stack([gain_one, gain_two])
    shift_term = jnp.stack([shift_one, shift_two])
    bias_total, hidden_total, gain_total, shift_total = lax.psum(
        (bias_term, hidden_term, gain_term, shift_term), ("rep", "fsdp")
    )
    up_sum, down_sum = (
        lax.psum_scatter(up_term, "fsdp", scatter_dimension=0, tiled=True),
        lax.psum_scatter(down_term, "fsdp", scatter_dimension=0, tiled=True),
    )
    qkv_sum, out_sum = (
        lax.psum_scatter(qkv_term, "fsdp", scatter_dimension=0, tiled=True),
        lax.psum_scatter(out_term, "fsdp", scatter_dimension=0, tiled=True),
    )
    qkv_total, out_total, up_total, down_total = lax.psum(
        (qkv_sum, out_sum, up_sum, down_sum), "rep"
    )
    grad_scale = (tok_count * lax.axis_size("fsdp") * lax.axis_size("rep")) ** (-0.5)
    return (
        output.astype(jnp.bfloat16)[None],
        input_grad.astype(jnp.bfloat16)[None],
        qkv_total * grad_scale,
        out_total * grad_scale,
        up_total * grad_scale,
        down_total * grad_scale,
        bias_total * grad_scale,
        hidden_total * grad_scale,
        gain_total * grad_scale,
        shift_total * grad_scale,
    )


def solution(mesh):
    small = mesh.shape["fsdp"] == 8 and mesh.shape["rep"] == 4
    local = local_tensor if small else local_gather
    return jax.shard_map(
        local,
        mesh=mesh,
        in_specs=(
            P("rep", "fsdp", None),
            P("rep", None),
            P("fsdp", None),
            P("fsdp", None),
            P("fsdp", None),
            P("fsdp", None),
            P(),
            P(),
            P(),
            P(),
            P("rep", "fsdp", None),
        ),
        out_specs=(
            P("rep", "fsdp", None),
            P("rep", "fsdp", None),
            P("fsdp", None),
            P("fsdp", None),
            P("fsdp", None),
            P("fsdp", None),
            P(),
            P(),
            P(),
            P(),
        ),
        check_vma=False,
    )
```
